256 devices in a mesh: dp: 8 (over y, z_lo), tensor: 32 (over x, z_hi, core).
Axes of the slice: x: 4, y: 4, z: 8 (z_hi: 4, z_lo: 2; z = z_hi * 2 + z_lo), core: 2. Of those that a mesh axis runs over, the one named last changes fastest.
Arguments:
- hidden_in: bfloat16 [6144, 2304], P(('dp', 'tensor')), parts along dimension 0, may hold values from -6 to 6
- attn_gain: bfloat16 [2304], replicated, may hold values from 0.099609375 to 1.8984375
- w_query: bfloat16 [2304, 2048], P(None, 'tensor'), may hold values from -0.125 to 0.125
- w_key: bfloat16 [2304, 2048], P(None, 'tensor'), may hold values from -0.25 to 0.25
- w_value: bfloat16 [2304, 2048], P(None, 'tensor'), may hold values from -0.375 to 0.375
- w_out: bfloat16 [2048, 2304], P('tensor'), may hold values from -0.125 to 0.125
- cache_k: bfloat16 [64, 32, 2048, 64], P('dp', 'tensor'), parts along dimension 0, may hold values from -250 to 250
- cache_v: bfloat16 [64, 32, 2048, 64], P('dp', 'tensor'), parts along dimension 0, may hold values from -16 to 16
- cache_len: int32 [64], P('dp'), parts along dimension 0, may hold values from 1 to 2048, as said below
- ffn_gain: bfloat16 [2304], replicated, may hold values from 0.099609375 to 1.8984375
- router: bfloat16 [2304, 4], replicated, may hold values from -0.375 to 0.375
- routes: int32 [6144, 2], P('dp'), parts along dimension 0, may hold values from 0 to 3, all different within a row; in each aligned block of 768 rows (0 to 767, 768 to 1535, ...) at most 576 rows name the same one
- w_gate_up: bfloat16 [4, 2, 2304, 4096], P(None, None, None, 'tensor'), may hold values from -0.125 to 0.125
- w_down: bfloat16 [4, 4096, 2304], P(None, 'tensor'), may hold values from -0.09375 to 0.09375
Outputs:
- block_out: bfloat16 [6144, 2304], P(('dp', 'tensor')), parts along dimension 0
The draws below stay inside these ranges and needn't reach their ends.
There are 8 independent parts, one for each index of `dp`. The reference program is written for one: setup_inputs(seed, part) draws one part's arguments, and reference() takes and returns one part's arrays. A program takes and returns all parts, laid end to end along the dimension named above; an argument that names none is the same for every part. Nothing has to cross between parts.
Inputs may be any that keep to these rules, and one draw needn't show every extreme that they name: `cache_len`: some request's cache is full in every draw. `routes`: each token names two different experts; no expert is named by more than 576 tokens of the group, and one is named by exactly 576.
All inputs are finite; a program needn't handle non-finite values.
Results may differ from the reference program's by a relative error of at most 0.019.
The reference program's roundings to bfloat16 on the way count: a program that leaves them out, or rounds other values in their place, can miss the bound.
Values may be sent and summed in bfloat16 or wider, within the bound.
A program may use at most 128 MiB of HBM per device.

```python
import math
import jax
import jax.numpy as jnp
import numpy as np
from jax import lax

D = 2304
HEADS = 32
HDIM = 64
EXPERTS = 4
FF = 4096
REQS = 8
NEW = 96
LMAX = 2048
TOKENS = 768
CAP = 576


def draw_cache_k(key, part):
    base_key = jax.random.fold_in(key, 0)
    shape = (REQS, HEADS, LMAX, HDIM)
    return (2.0 * jax.random.normal(base_key, shape, jnp.float32)).astype(jnp.bfloat16)


def draw_cache_len(key, part):
    length_key, index_key = jax.random.split(key, 2)
    lengths = jax.random.randint(length_key, (REQS,), 1, LMAX + 1)
    fullest = jax.random.randint(index_key, (), 0, REQS)
    return jnp.where(jnp.arange(REQS, dtype=jnp.int32) == fullest, LMAX, lengths).astype(jnp.int32)


def level_of(own_key, extent, cuts, low, largest):
    level, own = 1.0, jax.random.fold_in(own_key, 6)
    for axis_at, shards_of in cuts:
        draws = jnp.exp(jax.random.uniform(jax.random.fold_in(own, axis_at), (shards_of,), jnp.float32, low / len(cuts), largest / len(cuts)))
        level = level * jnp.repeat(draws, extent[axis_at] // shards_of).reshape([-1 if axis == axis_at else 1 for axis in range(len(extent))])
    return level


def shared_out(key, own, number, rows, amount, top, bound, skew):
    ranking = jax.random.permutation(key, amount)
    heavy_load, common = shares(amount, rows * top, bound, skew, True), shares(amount, rows * top, bound, skew, False)
    places = jnp.arange(amount)

    def named(sizes, turn):
        used = int((sizes > 0).sum())
        fixed = max(1, used // 4)
        moved = fixed + (places - fixed + turn * (used - fixed)) % max(1, amount - fixed)
        return jnp.zeros((amount,), jnp.int32).at[ranking[jnp.where(places < fixed, places, moved)]].set(jnp.asarray(sizes, jnp.int32))

    sizes = jnp.where(number % 4 == 0, named(heavy_load, number // 4), named(common, number - number // 4 - 1))
    mixed = jax.random.permutation(jax.random.fold_in(own, 3), amount)
    donor, taker = mixed[0:amount // 2 * 2:2], mixed[1:amount // 2 * 2:2]
    room = jnp.minimum(sizes[donor] - 1, bound - sizes[taker]) // 2
    room = jnp.where((donor == ranking[0]) | (taker == ranking[0]) | (sizes[taker] == 0), 0, jnp.maximum(room, 0))
    moved = jax.random.randint(jax.random.fold_in(own, 4), (amount // 2,), 0, 1 << 20) % (room + 1)
    sizes = sizes.at[donor].add(-moved).at[taker].add(moved)
    items = jnp.searchsorted(jnp.cumsum(sizes), jnp.arange(rows * top), side="right").astype(jnp.int32)
    grid = items.reshape(top, rows).T
    grid = grid[jax.random.permutation(jax.random.fold_in(own, 1), rows)]
    turn = jax.random.randint(jax.random.fold_in(own, 2), (rows, 1), 0, top)
    return jnp.take_along_axis(grid, (jnp.arange(top)[None, :] + turn) % top, axis=1)


def shares(amount, total, most, lean, full):
    loads = [(1 << 20) // math.isqrt(rank ** lean) + 1 for rank in range(1, amount + 1)]
    largest = most if full else min(most, max(-(-total // amount), total * loads[0] // sum(loads)))
    least = 1 if total - largest >= amount - 1 else 0
    holding, rest = [largest] + [least] * (amount - 1), total - largest - least * (amount - 1)
    while rest > 0:
        movable = [i for i in range(1, amount) if holding[i] < largest] or [i for i in range(1, amount) if holding[i] < most]
        mass, left = sum([loads[i] for i in movable]), rest
        for i in movable:
            addition = min(most - holding[i], max(1, left * loads[i] // mass), rest)
            holding[i] = holding[i] + addition
            rest = rest - addition
    return np.array(holding)


def scatter_about(stream_key, extent, scale, most, shards=(), kind=jnp.bfloat16):
    entries = jax.random.normal(stream_key, extent, jnp.float32) * scale
    if len(shards) > 0:
        entries = level_of(stream_key, extent, shards, -0.22, 0.18) * entries
    return jnp.clip(entries, min=-most, max=most).astype(kind)


def setup_inputs(seed: int = 0, part: int = 0) -> dict:
    splits = jax.random.split(jax.random.key(seed), 15)
    part_keys = jax.random.split(jax.random.fold_in(splits[14], part), 15)
    hidden_in = scatter_about(part_keys[0], (TOKENS, D), 1.0, 6.0, ((0, 32),))
    attn_gain = jnp.clip(1.0 + 0.18 * jax.random.normal(splits[1], (D,), jnp.float32), 0.099609375, 1.8984375).astype(jnp.bfloat16)
    w_query = scatter_about(splits[2], (D, HEADS * HDIM), D ** -0.5, 0.125, ((1, 32),))
    w_key = scatter_about(splits[3], (D, HEADS * HDIM), (D // 4) ** -0.5, 0.25, ((1, 32),))
    w_value = scatter_about(splits[4], (D, HEADS * HDIM), (D // 9) ** -0.5, 0.375, ((1, 32),))
    w_out = scatter_about(splits[5], (HEADS * HDIM, D), (HEADS * HDIM) ** -0.5, 0.125, ((0, 32),))
    cache_k = draw_cache_k(jax.random.fold_in(jax.random.fold_in(splits[14], part), 71), part)
    cache_v = scatter_about(part_keys[7], (REQS, HEADS, LMAX, HDIM), 3.0, 16.0, ((1, 32),))
    cache_len = draw_cache_len(jax.random.fold_in(jax.random.fold_in(splits[14], part), 71), part)
    ffn_gain = jnp.clip(1.0 + 0.18 * jax.random.normal(splits[9], (D,), jnp.float32), 0.099609375, 1.8984375).astype(jnp.bfloat16)
    router = scatter_about(splits[10], (D, EXPERTS), (D // 9) ** -0.5, 0.375)
    routes_keys = jax.random.split(jax.random.fold_in(part_keys[11], 1), TOKENS // TOKENS)
    routes_turns = jax.random.permutation(jax.random.fold_in(part_keys[11], 3), TOKENS // TOKENS)
    routes = jax.vmap(lambda own, number: shared_out(jax.random.fold_in(part_keys[11], 2), own, number, TOKENS, EXPERTS, 2, CAP, 2))(routes_keys, routes_turns).reshape((TOKENS, 2))
    w_gate_up = scatter_about(splits[12], (EXPERTS, 2, D, FF), D ** -0.5, 0.125, ((3, 32),))
    w_down = scatter_about(splits[13], (EXPERTS, FF, D), FF ** -0.5, 0.09375, ((1, 32),))
    return {"hidden_in": hidden_in, "attn_gain": attn_gain, "w_query": w_query, "w_key": w_key, "w_value": w_value, "w_out": w_out, "cache_k": cache_k, "cache_v": cache_v, "cache_len": cache_len, "ffn_gain": ffn_gain, "router": router, "routes": routes, "w_gate_up": w_gate_up, "w_down": w_down}


eps = 1e-05

def rms_scale(rows_in, gain):
    values = rows_in.astype(jnp.float32)
    mean_square = lax.optimization_barrier(jnp.mean(values * values, axis=-1, keepdims=True))
    return (values * lax.rsqrt(mean_square + eps) * gain.astype(jnp.float32)).astype(jnp.bfloat16)

def rotate(values, positions):
    half_dim = values.shape[-1] // 2
    inverse = 10000.0 ** (-2.0 * jnp.arange(half_dim, dtype=jnp.float32) / values.shape[-1])
    angles = positions.astype(jnp.float32)[:, None] * inverse[None, :]
    cosine = jnp.cos(angles)[:, None, :]
    sine_part = jnp.sin(angles)[:, None, :]
    front = values[..., :half_dim]
    back = values[..., half_dim:]
    return jnp.concatenate([front * cosine - back * sine_part, back * cosine + front * sine_part], axis=-1)

def route_weights(logits, routes):
    expert_iota = jnp.arange(logits.shape[1], dtype=jnp.int32)[None, :]
    first_logit = lax.optimization_barrier(jnp.sum(jnp.where(routes[:, 0:1] == expert_iota, logits, 0.0), axis=1))
    second_logit = lax.optimization_barrier(jnp.sum(jnp.where(routes[:, 1:2] == expert_iota, logits, 0.0), axis=1))
    first_weight = 1.0 / (1.0 + jnp.exp(second_logit - first_logit))
    second_weight = 1.0 / (1.0 + jnp.exp(first_logit - second_logit))
    return jnp.stack([first_weight, second_weight], axis=1)

def expert_slots(routes, pair_weights):
    flat_ids = routes.reshape(-1)
    onehot = (flat_ids[:, None] == jnp.arange(EXPERTS, dtype=jnp.int32)[None, :]).astype(jnp.int32)
    before = jnp.cumsum(onehot, axis=0) - onehot
    slot_ids = lax.optimization_barrier(jnp.sum(before * onehot, axis=1))
    target = flat_ids * CAP + slot_ids
    token_ids = jnp.arange(flat_ids.shape[0], dtype=jnp.int32) // 2
    table = jnp.zeros((EXPERTS * CAP,), jnp.int32).at[target].set(token_ids)
    row_weight = jnp.zeros((EXPERTS * CAP,), jnp.float32).at[target].set(pair_weights.reshape(-1))
    return (table, row_weight)

def attend(query, key_new, value_new, cache_k, cache_v, cache_len):
    query_f = query.astype(jnp.float32)
    cached_scores = jnp.einsum('rhqd,rhkd->rhqk', query_f, cache_k.astype(jnp.float32)) * 0.125
    fresh_scores = jnp.einsum('rhqd,rhkd->rhqk', query_f, key_new.astype(jnp.float32)) * 0.125
    key_pos = jnp.arange(cache_k.shape[2], dtype=jnp.int32)
    cached_mask = key_pos[None, None, None, :] < cache_len[:, None, None, None]
    new_pos = jnp.arange(query.shape[2], dtype=jnp.int32)
    fresh_mask = (new_pos[:, None] >= new_pos[None, :])[None, None]
    cached_scores = jnp.where(cached_mask, cached_scores, -1e+30)
    fresh_scores = jnp.where(fresh_mask, fresh_scores, -1e+30)
    peak = jnp.maximum(lax.optimization_barrier(jnp.max(cached_scores, axis=-1, keepdims=True)), lax.optimization_barrier(jnp.max(fresh_scores, axis=-1, keepdims=True)))
    cached_expo = jnp.exp(cached_scores - peak)
    fresh_expo = jnp.exp(fresh_scores - peak)
    denominator = lax.optimization_barrier(jnp.sum(cached_expo, axis=-1, keepdims=True)) + lax.optimization_barrier(jnp.sum(fresh_expo, axis=-1, keepdims=True))
    cached_probs = cached_expo.astype(jnp.bfloat16).astype(jnp.float32)
    fresh_probs = fresh_expo.astype(jnp.bfloat16).astype(jnp.float32)
    mixed = jnp.einsum('rhqk,rhkd->rhqd', cached_probs, cache_v.astype(jnp.float32))
    mixed = mixed + jnp.einsum('rhqk,rhkd->rhqd', fresh_probs, value_new.astype(jnp.float32))
    return (mixed / denominator).astype(jnp.bfloat16)

def reference(hidden_in, attn_gain, w_query, w_key, w_value, w_out, cache_k, cache_v, cache_len, ffn_gain, router, routes, w_gate_up, w_down):
    normed = rms_scale(hidden_in, attn_gain)
    positions = (cache_len[:, None] + jnp.arange(NEW, dtype=jnp.int32)[None, :]).reshape(-1)

    def project(weight):
        return jnp.dot(normed, weight, preferred_element_type=jnp.float32).reshape(TOKENS, HEADS, HDIM)

    def by_request(values):
        return values.reshape(REQS, NEW, HEADS, HDIM).transpose(0, 2, 1, 3)
    query = rotate(project(w_query), positions).astype(jnp.bfloat16)
    key_new = rotate(project(w_key), positions).astype(jnp.bfloat16)
    value_new = project(w_value).astype(jnp.bfloat16)
    heads_out = attend(by_request(query), by_request(key_new), by_request(value_new), cache_k, cache_v, cache_len)
    heads_flat = heads_out.transpose(0, 2, 1, 3).reshape(TOKENS, HEADS * HDIM)
    attn = jnp.dot(heads_flat, w_out, preferred_element_type=jnp.float32)
    middle = (hidden_in.astype(jnp.float32) + attn).astype(jnp.bfloat16)
    normed2 = rms_scale(middle, ffn_gain)
    logits = jnp.dot(normed2, router, preferred_element_type=jnp.float32)
    pair_weights = route_weights(logits, routes)
    table, row_weight = expert_slots(routes, pair_weights)
    running = jnp.zeros((TOKENS, D), jnp.float32)
    for expert in range(EXPERTS):
        row_ids = table[expert * CAP:(expert + 1) * CAP]
        picked = normed2[row_ids]
        gate_part = jnp.dot(picked, w_gate_up[expert, 0], preferred_element_type=jnp.float32)
        up_part = jnp.dot(picked, w_gate_up[expert, 1], preferred_element_type=jnp.float32)
        inner = (jax.nn.silu(gate_part) * up_part).astype(jnp.bfloat16)
        out_rows = jnp.dot(inner, w_down[expert], preferred_element_type=jnp.float32)
        running = running.at[row_ids].add(out_rows * row_weight[expert * CAP:(expert + 1) * CAP, None])
    return (middle.astype(jnp.float32) + running).astype(jnp.bfloat16)
```

```python
import jax
import jax.numpy as jnp
from jax import lax
from jax.sharding import Mesh
from jax.sharding import PartitionSpec as P

HDIM = 64
REQS = 8
NEW = 96
TOKENS = 768

SUB = (("x", 4), ("zh", 4), ("core", 2))
TENSOR = tuple(name for name, _ in SUB)
SIZE = dict(SUB)

eps = 1e-05


def rms_scale(rows_in, gain):
    values = rows_in.astype(jnp.float32)
    mean_square = jnp.mean(values * values, axis=-1, keepdims=True)
    return (values * lax.rsqrt(mean_square + eps) * gain.astype(jnp.float32)).astype(jnp.bfloat16)


def rotate(values, positions):
    half_dim = values.shape[-1] // 2
    inverse = 10000.0 ** (-2.0 * jnp.arange(half_dim, dtype=jnp.float32) / values.shape[-1])
    angles = positions.astype(jnp.float32)[:, None] * inverse[None, :]
    cosine = jnp.cos(angles)[:, None, :]
    sine_part = jnp.sin(angles)[:, None, :]
    front = values[..., :half_dim]
    back = values[..., half_dim:]
    return jnp.concatenate(
        [front * cosine - back * sine_part, back * cosine + front * sine_part], axis=-1
    )


def route_weights(logits, routes):
    expert_iota = jnp.arange(logits.shape[1], dtype=jnp.int32)[None, :]
    first_logit = jnp.sum(jnp.where(routes[:, 0:1] == expert_iota, logits, 0.0), axis=1)
    second_logit = jnp.sum(jnp.where(routes[:, 1:2] == expert_iota, logits, 0.0), axis=1)
    first_weight = 1.0 / (1.0 + jnp.exp(second_logit - first_logit))
    second_weight = 1.0 / (1.0 + jnp.exp(first_logit - second_logit))
    return jnp.stack([first_weight, second_weight], axis=1)


def expert_apply(rows_in, gate_up, down_part):
    both = jnp.einsum("td,kdf->ktf", rows_in, gate_up, preferred_element_type=jnp.float32)
    inner = (jax.nn.silu(both[0]) * both[1]).astype(jnp.bfloat16)
    return jnp.dot(inner, down_part, preferred_element_type=jnp.float32)


def attend(query, key_new, value_new, cache_k, cache_v, cache_len):
    cached_scores = (
        jnp.einsum("rhqd,rhkd->rhqk", query, cache_k, preferred_element_type=jnp.float32) * 0.125
    )
    fresh_scores = (
        jnp.einsum("rhqd,rhkd->rhqk", query, key_new, preferred_element_type=jnp.float32) * 0.125
    )
    key_pos = jnp.arange(cache_k.shape[2], dtype=jnp.int32)
    cached_mask = key_pos[None, None, None, :] < cache_len[:, None, None, None]
    new_pos = jnp.arange(query.shape[2], dtype=jnp.int32)
    fresh_mask = (new_pos[:, None] >= new_pos[None, :])[None, None]
    cached_scores = jnp.where(cached_mask, cached_scores, -1e30)
    fresh_scores = jnp.where(fresh_mask, fresh_scores, -1e30)
    peak = jnp.maximum(
        jnp.max(cached_scores, axis=-1, keepdims=True),
        jnp.max(fresh_scores, axis=-1, keepdims=True),
    )
    cached_expo = jnp.exp(cached_scores - peak)
    fresh_expo = jnp.exp(fresh_scores - peak)
    denominator = jnp.sum(cached_expo, axis=-1, keepdims=True) + jnp.sum(
        fresh_expo, axis=-1, keepdims=True
    )
    mixed = jnp.einsum(
        "rhqk,rhkd->rhqd",
        cached_expo.astype(jnp.bfloat16),
        cache_v,
        preferred_element_type=jnp.float32,
    )
    mixed = mixed + jnp.einsum(
        "rhqk,rhkd->rhqd",
        fresh_expo.astype(jnp.bfloat16),
        value_new,
        preferred_element_type=jnp.float32,
    )
    return (mixed / denominator).astype(jnp.bfloat16)


def shifts(axis, step):
    n = SIZE[axis]
    return [(i, (i + step) % n) for i in range(n)]


def gather_stage(rows, axis):
    n = SIZE[axis]
    me = lax.axis_index(axis)
    blk = rows.shape[0]
    out = jnp.zeros((n * blk,) + rows.shape[1:], rows.dtype)
    out = lax.dynamic_update_slice_in_dim(out, rows, me * blk, axis=0)
    for step in range(1, n):
        got = lax.ppermute(rows, axis, shifts(axis, step))
        out = lax.dynamic_update_slice_in_dim(out, got, ((me - step) % n) * blk, axis=0)
    return out


def scatter_stage(rows, axis):
    n = SIZE[axis]
    me = lax.axis_index(axis)
    chunks = rows.reshape((n, rows.shape[0] // n) + rows.shape[1:])
    total = lax.dynamic_index_in_dim(chunks, me, axis=0, keepdims=False).astype(jnp.float32)
    for step in range(1, n):
        send = lax.dynamic_index_in_dim(chunks, (me + step) % n, axis=0, keepdims=False)
        got = lax.ppermute(send.astype(jnp.bfloat16), axis, shifts(axis, step))
        total = total + got.astype(jnp.float32)
    return total


def gather_rows(rows):
    rows = gather_stage(rows, "zh")
    rows = gather_stage(rows, "x")
    return gather_stage(rows, "core")


def scatter_rows(rows):
    rows = scatter_stage(rows, "core")
    rows = scatter_stage(rows.astype(jnp.bfloat16), "x")
    return scatter_stage(rows.astype(jnp.bfloat16), "zh")


def to_request_order(values):
    nx, nz, nc = SIZE["x"], SIZE["zh"], SIZE["core"]
    blk = TOKENS // (nx * nz * nc)
    tail = values.shape[1:]
    values = values.reshape((nc, nx, nz, blk) + tail)
    values = jnp.moveaxis(values, 0, 2)
    return values.reshape((TOKENS,) + tail)


def from_request_order(values):
    nx, nz, nc = SIZE["x"], SIZE["zh"], SIZE["core"]
    blk = TOKENS // (nx * nz * nc)
    tail = values.shape[1:]
    values = values.reshape((nx, nz, nc, blk) + tail)
    values = jnp.moveaxis(values, 2, 0)
    return values.reshape((TOKENS,) + tail)


def local(
    hidden_in,
    attn_gain,
    w_query,
    w_key,
    w_value,
    w_out,
    cache_k,
    cache_v,
    cache_len,
    ffn_gain,
    router,
    routes,
    w_gate_up,
    w_down,
):
    width = hidden_in.shape[1]
    head_dev = cache_k.shape[1]
    n_experts = w_gate_up.shape[0]
    whole_in = gather_rows(hidden_in)
    normed = rms_scale(whole_in, attn_gain)
    positions = (cache_len[:, None] + jnp.arange(NEW, dtype=jnp.int32)[None, :]).reshape(-1)
    positions = from_request_order(positions)

    def project(weight):
        return jnp.dot(normed, weight, preferred_element_type=jnp.float32).reshape(
            TOKENS, head_dev, HDIM
        )

    def by_request(values):
        values = to_request_order(values)
        return values.reshape(REQS, NEW, head_dev, HDIM).transpose(0, 2, 1, 3)

    query = rotate(project(w_query), positions).astype(jnp.bfloat16)
    key_new = rotate(project(w_key), positions).astype(jnp.bfloat16)
    value_new = project(w_value).astype(jnp.bfloat16)
    heads_out = attend(
        by_request(query), by_request(key_new), by_request(value_new), cache_k, cache_v, cache_len
    )
    heads_flat = from_request_order(heads_out.transpose(0, 2, 1, 3).reshape(TOKENS, head_dev * HDIM))
    attn = scatter_rows(
        jnp.dot(heads_flat, w_out, preferred_element_type=jnp.float32).astype(jnp.bfloat16)
    )
    middle = (hidden_in.astype(jnp.float32) + attn).astype(jnp.bfloat16)
    normed2 = gather_rows(rms_scale(middle, ffn_gain))
    logits = jnp.dot(normed2, router, preferred_element_type=jnp.float32)
    routes = from_request_order(routes)
    pair_weights = route_weights(logits, routes)
    running = jnp.zeros((TOKENS, width), jnp.float32)
    for expert in range(n_experts):
        dense_weight = jnp.sum(jnp.where(routes == expert, pair_weights, 0.0), axis=1)
        running = (
            running
            + expert_apply(normed2, w_gate_up[expert], w_down[expert]) * dense_weight[:, None]
        )
    expert_out = scatter_rows(running.astype(jnp.bfloat16))
    return (middle.astype(jnp.float32) + expert_out).astype(jnp.bfloat16)


def solution(mesh):
    dp = mesh.shape["dp"]
    fine = Mesh(mesh.devices.reshape((dp,) + tuple(n for _, n in SUB)), ("dp",) + TENSOR)
    rows = ("dp",) + TENSOR
    in_specs = (
        P(rows, None),
        P(),
        P(None, TENSOR),
        P(None, TENSOR),
        P(None, TENSOR),
        P(TENSOR, None),
        P("dp", TENSOR, None, None),
        P("dp", TENSOR, None, None),
        P("dp"),
        P(),
        P(),
        P("dp", None),
        P(None, None, None, TENSOR),
        P(None, TENSOR, None),
    )
    out_specs = P(rows, None)
    return jax.shard_map(local, mesh=fine, in_specs=in_specs, out_specs=out_specs, check_vma=False)
```

```python
import jax
import jax.numpy as jnp
from jax import lax
from jax.sharding import Mesh
from jax.sharding import PartitionSpec as P

HDIM = 64
REQS = 8
NEW = 96
TOKENS = 768

SUB = (("x", 4), ("zh", 4), ("core", 2))
TENSOR = tuple(name for name, _ in SUB)
SIZE = dict(SUB)
PIECES = 2

eps = 1e-05


def rms_scale(rows_in, gain):
    values = rows_in.astype(jnp.float32)
    mean_square = jnp.mean(values * values, axis=-1, keepdims=True)
    return (values * lax.rsqrt(mean_square + eps) * gain.astype(jnp.float32)).astype(jnp.bfloat16)


def rotate(values, positions):
    half_dim = values.shape[-1] // 2
    inverse = 10000.0 ** (-2.0 * jnp.arange(half_dim, dtype=jnp.float32) / values.shape[-1])
    angles = positions.astype(jnp.float32)[:, None] * inverse[None, :]
    cosine = jnp.cos(angles)[:, None, :]
    sine_part = jnp.sin(angles)[:, None, :]
    front = values[..., :half_dim]
    back = values[..., half_dim:]
    return jnp.concatenate(
        [front * cosine - back * sine_part, back * cosine + front * sine_part], axis=-1
    )


def route_weights(logits, routes):
    expert_iota = jnp.arange(logits.shape[1], dtype=jnp.int32)[None, :]
    first_logit = jnp.sum(jnp.where(routes[:, 0:1] == expert_iota, logits, 0.0), axis=1)
    second_logit = jnp.sum(jnp.where(routes[:, 1:2] == expert_iota, logits, 0.0), axis=1)
    first_weight = 1.0 / (1.0 + jnp.exp(second_logit - first_logit))
    second_weight = 1.0 / (1.0 + jnp.exp(first_logit - second_logit))
    return jnp.stack([first_weight, second_weight], axis=1)


def attend(query, key_new, value_new, cache_k, cache_v, cache_len):
    cached_scores = (
        jnp.einsum("rhqd,rhkd->rhqk", query, cache_k, preferred_element_type=jnp.float32) * 0.125
    )
    fresh_scores = (
        jnp.einsum("rhqd,rhkd->rhqk", query, key_new, preferred_element_type=jnp.float32) * 0.125
    )
    key_pos = jnp.arange(cache_k.shape[2], dtype=jnp.int32)
    cached_mask = key_pos[None, None, None, :] < cache_len[:, None, None, None]
    new_pos = jnp.arange(query.shape[2], dtype=jnp.int32)
    fresh_mask = (new_pos[:, None] >= new_pos[None, :])[None, None]
    cached_scores = jnp.where(cached_mask, cached_scores, -1e30)
    fresh_scores = jnp.where(fresh_mask, fresh_scores, -1e30)
    peak = jnp.maximum(
        jnp.max(cached_scores, axis=-1, keepdims=True),
        jnp.max(fresh_scores, axis=-1, keepdims=True),
    )
    cached_expo = jnp.exp(cached_scores - peak)
    fresh_expo = jnp.exp(fresh_scores - peak)
    denominator = jnp.sum(cached_expo, axis=-1, keepdims=True) + jnp.sum(
        fresh_expo, axis=-1, keepdims=True
    )
    mixed = jnp.einsum(
        "rhqk,rhkd->rhqd",
        cached_expo.astype(jnp.bfloat16),
        cache_v,
        preferred_element_type=jnp.float32,
    )
    mixed = mixed + jnp.einsum(
        "rhqk,rhkd->rhqd",
        fresh_expo.astype(jnp.bfloat16),
        value_new,
        preferred_element_type=jnp.float32,
    )
    return (mixed / denominator).astype(jnp.bfloat16)


def shifts(axis, step):
    n = SIZE[axis]
    return [(i, (i + step) % n) for i in range(n)]


def gather_stage(rows, axis):
    n = SIZE[axis]
    me = lax.axis_index(axis)
    blk = rows.shape[0]
    out = jnp.zeros((n * blk,) + rows.shape[1:], rows.dtype)
    out = lax.dynamic_update_slice_in_dim(out, rows, me * blk, axis=0)
    for step in range(1, n):
        got = lax.ppermute(rows, axis, shifts(axis, step))
        out = lax.dynamic_update_slice_in_dim(out, got, ((me - step) % n) * blk, axis=0)
    return out


def scatter_stage(rows, axis):
    n = SIZE[axis]
    me = lax.axis_index(axis)
    chunks = rows.reshape((n, rows.shape[0] // n) + rows.shape[1:])
    total = lax.dynamic_index_in_dim(chunks, me, axis=0, keepdims=False).astype(jnp.float32)
    for step in range(1, n):
        send = lax.dynamic_index_in_dim(chunks, (me + step) % n, axis=0, keepdims=False)
        got = lax.ppermute(send.astype(jnp.bfloat16), axis, shifts(axis, step))
        total = total + got.astype(jnp.float32)
    return total


def gather_rows(rows):
    rows = gather_stage(rows, "zh")
    rows = gather_stage(rows, "x")
    return gather_stage(rows, "core")


def scatter_rows(rows):
    rows = scatter_stage(rows, "core")
    rows = scatter_stage(rows.astype(jnp.bfloat16), "x")
    return scatter_stage(rows.astype(jnp.bfloat16), "zh")


def to_request_order(values):
    nx, nz, nc = SIZE["x"], SIZE["zh"], SIZE["core"]
    blk = TOKENS // (nx * nz * nc)
    tail = values.shape[1:]
    values = values.reshape((nc, nx, nz, blk) + tail)
    values = jnp.moveaxis(values, 0, 2)
    return values.reshape((TOKENS,) + tail)


def from_request_order(values):
    nx, nz, nc = SIZE["x"], SIZE["zh"], SIZE["core"]
    blk = TOKENS // (nx * nz * nc)
    tail = values.shape[1:]
    values = values.reshape((nx, nz, nc, blk) + tail)
    values = jnp.moveaxis(values, 2, 0)
    return values.reshape((TOKENS,) + tail)


def local(
    hidden_in,
    attn_gain,
    w_query,
    w_key,
    w_value,
    w_out,
    cache_k,
    cache_v,
    cache_len,
    ffn_gain,
    router,
    routes,
    w_gate_up,
    w_down,
):
    width = hidden_in.shape[1]
    head_dev = cache_k.shape[1]
    n_experts = w_gate_up.shape[0]
    span = width // PIECES
    cols = [slice(k * span, (k + 1) * span) for k in range(PIECES)]
    normed_own = rms_scale(hidden_in, attn_gain)
    normed = [gather_rows(normed_own[:, c]) for c in cols]
    positions = (cache_len[:, None] + jnp.arange(NEW, dtype=jnp.int32)[None, :]).reshape(-1)
    positions = from_request_order(positions)
    w_qkv = jnp.concatenate([w_query, w_key, w_value], axis=1)
    qkv = sum(
        jnp.dot(part, w_qkv[c], preferred_element_type=jnp.float32) for part, c in zip(normed, cols)
    )
    qkv = qkv.reshape(TOKENS, 3, head_dev, HDIM)

    def by_request(values):
        values = to_request_order(values)
        return values.reshape(REQS, NEW, head_dev, HDIM).transpose(0, 2, 1, 3)

    query = rotate(qkv[:, 0], positions).astype(jnp.bfloat16)
    key_new = rotate(qkv[:, 1], positions).astype(jnp.bfloat16)
    value_new = qkv[:, 2].astype(jnp.bfloat16)
    heads_out = attend(
        by_request(query), by_request(key_new), by_request(value_new), cache_k, cache_v, cache_len
    )
    heads_flat = from_request_order(heads_out.transpose(0, 2, 1, 3).reshape(TOKENS, head_dev * HDIM))
    attn = jnp.concatenate(
        [
            scatter_rows(
                jnp.dot(heads_flat, w_out[:, c], preferred_element_type=jnp.float32).astype(
                    jnp.bfloat16
                )
            )
            for c in cols
        ],
        axis=1,
    )
    middle = (hidden_in.astype(jnp.float32) + attn).astype(jnp.bfloat16)
    normed2_own = rms_scale(middle, ffn_gain)
    normed2 = [gather_rows(normed2_own[:, c]) for c in cols]
    logits = sum(
        jnp.dot(part, router[c], preferred_element_type=jnp.float32) for part, c in zip(normed2, cols)
    )
    routes = from_request_order(routes)
    pair_weights = route_weights(logits, routes)
    both = sum(
        jnp.einsum("td,ekdf->ektf", part, w_gate_up[:, :, c], preferred_element_type=jnp.float32)
        for part, c in zip(normed2, cols)
    )
    inner = (jax.nn.silu(both[:, 0]) * both[:, 1]).astype(jnp.bfloat16)
    dense_weight = [
        jnp.sum(jnp.where(routes == expert, pair_weights, 0.0), axis=1) for expert in range(n_experts)
    ]
    pieces = []
    for c in cols:
        running = jnp.zeros((TOKENS, span), jnp.float32)
        for expert in range(n_experts):
            running = running + (
                jnp.dot(inner[expert], w_down[expert][:, c], preferred_element_type=jnp.float32)
                * dense_weight[expert][:, None]
            )
        pieces.append(scatter_rows(running.astype(jnp.bfloat16)))
    expert_out = jnp.concatenate(pieces, axis=1)
    return (middle.astype(jnp.float32) + expert_out).astype(jnp.bfloat16)


def solution(mesh):
    dp = mesh.shape["dp"]
    fine = Mesh(mesh.devices.reshape((dp,) + tuple(n for _, n in SUB)), ("dp",) + TENSOR)
    rows = ("dp",) + TENSOR
    in_specs = (
        P(rows, None),
        P(),
        P(None, TENSOR),
        P(None, TENSOR),
        P(None, TENSOR),
        P(TENSOR, None),
        P("dp", TENSOR, None, None),
        P("dp", TENSOR, None, None),
        P("dp"),
        P(),
        P(),
        P("dp", None),
        P(None, None, None, TENSOR),
        P(None, TENSOR, None),
    )
    out_specs = P(rows, None)
    return jax.shard_map(local, mesh=fine, in_specs=in_specs, out_specs=out_specs, check_vma=False)
```

```python
import jax
import jax.numpy as jnp
from jax import lax
from jax.experimental import pallas as pl
from jax.experimental.pallas import tpu as pltpu
from jax.sharding import Mesh
from jax.sharding import PartitionSpec as P

HDIM = 64
REQS = 8
NEW = 96
TOKENS = 768

SUB = (("x", 4), ("zh", 4), ("core", 2))
TENSOR = tuple(name for name, _ in SUB)
SIZE = dict(SUB)

eps = 1e-05


def rms_scale(rows_in, gain):
    values = rows_in.astype(jnp.float32)
    mean_square = jnp.mean(values * values, axis=-1, keepdims=True)
    return (values * lax.rsqrt(mean_square + eps) * gain.astype(jnp.float32)).astype(jnp.bfloat16)


def rotate(values, positions):
    half_dim = values.shape[-1] // 2
    inverse = 10000.0 ** (-2.0 * jnp.arange(half_dim, dtype=jnp.float32) / values.shape[-1])
    angles = positions.astype(jnp.float32)[:, None] * inverse[None, :]
    cosine = jnp.cos(angles)[:, None, :]
    sine_part = jnp.sin(angles)[:, None, :]
    front = values[..., :half_dim]
    back = values[..., half_dim:]
    return jnp.concatenate(
        [front * cosine - back * sine_part, back * cosine + front * sine_part], axis=-1
    )


def route_weights(logits, routes):
    expert_iota = jnp.arange(logits.shape[1], dtype=jnp.int32)[None, :]
    first_logit = jnp.sum(jnp.where(routes[:, 0:1] == expert_iota, logits, 0.0), axis=1)
    second_logit = jnp.sum(jnp.where(routes[:, 1:2] == expert_iota, logits, 0.0), axis=1)
    first_weight = 1.0 / (1.0 + jnp.exp(second_logit - first_logit))
    second_weight = 1.0 / (1.0 + jnp.exp(first_logit - second_logit))
    return jnp.stack([first_weight, second_weight], axis=1)


def expert_apply(rows_in, gate_up, down_part):
    both = jnp.einsum("td,kdf->ktf", rows_in, gate_up, preferred_element_type=jnp.float32)
    inner = (jax.nn.silu(both[0]) * both[1]).astype(jnp.bfloat16)
    return jnp.dot(inner, down_part, preferred_element_type=jnp.float32)


def attend(query, key_new, value_new, cache_k, cache_v, cache_len):
    cached_scores = (
        jnp.einsum("rhqd,rhkd->rhqk", query, cache_k, preferred_element_type=jnp.float32) * 0.125
    )
    fresh_scores = (
        jnp.einsum("rhqd,rhkd->rhqk", query, key_new, preferred_element_type=jnp.float32) * 0.125
    )
    key_pos = jnp.arange(cache_k.shape[2], dtype=jnp.int32)
    cached_mask = key_pos[None, None, None, :] < cache_len[:, None, None, None]
    new_pos = jnp.arange(query.shape[2], dtype=jnp.int32)
    fresh_mask = (new_pos[:, None] >= new_pos[None, :])[None, None]
    cached_scores = jnp.where(cached_mask, cached_scores, -1e30)
    fresh_scores = jnp.where(fresh_mask, fresh_scores, -1e30)
    peak = jnp.maximum(
        jnp.max(cached_scores, axis=-1, keepdims=True),
        jnp.max(fresh_scores, axis=-1, keepdims=True),
    )
    cached_expo = jnp.exp(cached_scores - peak)
    fresh_expo = jnp.exp(fresh_scores - peak)
    denominator = jnp.sum(cached_expo, axis=-1, keepdims=True) + jnp.sum(
        fresh_expo, axis=-1, keepdims=True
    )
    mixed = jnp.einsum(
        "rhqk,rhkd->rhqd",
        cached_expo.astype(jnp.bfloat16),
        cache_v,
        preferred_element_type=jnp.float32,
    )
    mixed = mixed + jnp.einsum(
        "rhqk,rhkd->rhqd",
        fresh_expo.astype(jnp.bfloat16),
        value_new,
        preferred_element_type=jnp.float32,
    )
    return (mixed / denominator).astype(jnp.bfloat16)


def shifts(axis, step):
    n = SIZE[axis]
    return [(i, (i + step) % n) for i in range(n)]


def gather_stage(rows, axis):
    n = SIZE[axis]
    me = lax.axis_index(axis)
    blk = rows.shape[0]
    out = jnp.zeros((n * blk,) + rows.shape[1:], rows.dtype)
    out = lax.dynamic_update_slice_in_dim(out, rows, me * blk, axis=0)
    for step in range(1, n):
        got = lax.ppermute(rows, axis, shifts(axis, step))
        out = lax.dynamic_update_slice_in_dim(out, got, ((me - step) % n) * blk, axis=0)
    return out


def scatter_stage(rows, axis):
    n = SIZE[axis]
    me = lax.axis_index(axis)
    chunks = rows.reshape((n, rows.shape[0] // n) + rows.shape[1:])
    total = lax.dynamic_index_in_dim(chunks, me, axis=0, keepdims=False).astype(jnp.float32)
    for step in range(1, n):
        send = lax.dynamic_index_in_dim(chunks, (me + step) % n, axis=0, keepdims=False)
        got = lax.ppermute(send.astype(jnp.bfloat16), axis, shifts(axis, step))
        total = total + got.astype(jnp.float32)
    return total


def gather_kernel(own_ref, out_ref, send_sem, recv_sem, local_sem):
    nx, nz = SIZE["x"], SIZE["zh"]
    dp = lax.axis_index("dp")
    x = lax.axis_index("x")
    z = lax.axis_index("zh")
    c = lax.axis_index("core")
    mesh_id = pl.DeviceIdType.MESH
    z_peers = [(dp, x, (z + s) % nz, c) for s in range(1, nz)]
    z_from = [(z + nz - s) % nz for s in range(1, nz)]
    x_peers = [(dp, (x + s) % nx, z, c) for s in range(1, nx)]
    x_from = [(x + nx - s) % nx for s in range(1, nx)]
    sibling = (dp, x, z, 1 - c)
    barrier = pltpu.get_barrier_semaphore()
    for peer in z_peers + x_peers + [sibling]:
        pl.semaphore_signal(barrier, 1, device_id=peer, device_id_type=mesh_id)
    pl.semaphore_wait(barrier, len(z_peers) + len(x_peers) + 1)
    local = pltpu.make_async_copy(own_ref, out_ref.at[c, x, z], local_sem.at[0])
    local.start()
    sent = []
    for k, peer in enumerate(z_peers):
        copy = pltpu.make_async_remote_copy(
            src_ref=own_ref,
            dst_ref=out_ref.at[c, x, z],
            send_sem=send_sem.at[k],
            recv_sem=recv_sem.at[k],
            device_id=peer,
            device_id_type=mesh_id,
        )
        copy.start()
        sent.append(copy)
    local.wait()
    for k, src in enumerate(z_from):
        pltpu.make_async_remote_copy(
            src_ref=own_ref,
            dst_ref=out_ref.at[c, x, src],
            send_sem=send_sem.at[k],
            recv_sem=recv_sem.at[k],
            device_id=z_peers[k],
            device_id_type=mesh_id,
        ).wait_recv()
    base = len(z_peers)
    for k, peer in enumerate(x_peers):
        copy = pltpu.make_async_remote_copy(
            src_ref=out_ref.at[c, x],
            dst_ref=out_ref.at[c, x],
            send_sem=send_sem.at[base + k],
            recv_sem=recv_sem.at[base + k],
            device_id=peer,
            device_id_type=mesh_id,
        )
        copy.start()
        sent.append(copy)
    for k, src in enumerate(x_from):
        pltpu.make_async_remote_copy(
            src_ref=out_ref.at[c, x],
            dst_ref=out_ref.at[c, src],
            send_sem=send_sem.at[base + k],
            recv_sem=recv_sem.at[base + k],
            device_id=x_peers[k],
            device_id_type=mesh_id,
        ).wait_recv()
    last = base + len(x_peers)
    copy = pltpu.make_async_remote_copy(
        src_ref=out_ref.at[c],
        dst_ref=out_ref.at[c],
        send_sem=send_sem.at[last],
        recv_sem=recv_sem.at[last],
        device_id=sibling,
        device_id_type=mesh_id,
    )
    copy.start()
    sent.append(copy)
    pltpu.make_async_remote_copy(
        src_ref=out_ref.at[c],
        dst_ref=out_ref.at[1 - c],
        send_sem=send_sem.at[last],
        recv_sem=recv_sem.at[last],
        device_id=sibling,
        device_id_type=mesh_id,
    ).wait_recv()
    for copy in sent:
        copy.wait_send()


def gather_rows(rows):
    nx, nz, nc = SIZE["x"], SIZE["zh"], SIZE["core"]
    links = (nz - 1) + (nx - 1) + 1
    out = pl.pallas_call(
        gather_kernel,
        out_shape=jax.ShapeDtypeStruct((nc, nx, nz) + rows.shape, rows.dtype),
        in_specs=[pl.BlockSpec(memory_space=pltpu.VMEM)],
        out_specs=pl.BlockSpec(memory_space=pltpu.VMEM),
        scratch_shapes=[
            pltpu.SemaphoreType.DMA((links,)),
            pltpu.SemaphoreType.DMA((links,)),
            pltpu.SemaphoreType.DMA((1,)),
        ],
        compiler_params=pltpu.CompilerParams(collective_id=0, has_side_effects=True),
    )(rows)
    return out.reshape((nc * nx * nz * rows.shape[0],) + rows.shape[1:])


def scatter_rows(rows):
    rows = scatter_stage(rows, "core")
    rows = scatter_stage(rows.astype(jnp.bfloat16), "x")
    return scatter_stage(rows.astype(jnp.bfloat16), "zh")


def to_request_order(values):
    nx, nz, nc = SIZE["x"], SIZE["zh"], SIZE["core"]
    blk = TOKENS // (nx * nz * nc)
    tail = values.shape[1:]
    values = values.reshape((nc, nx, nz, blk) + tail)
    values = jnp.moveaxis(values, 0, 2)
    return values.reshape((TOKENS,) + tail)


def from_request_order(values):
    nx, nz, nc = SIZE["x"], SIZE["zh"], SIZE["core"]
    blk = TOKENS // (nx * nz * nc)
    tail = values.shape[1:]
    values = values.reshape((nx, nz, nc, blk) + tail)
    values = jnp.moveaxis(values, 2, 0)
    return values.reshape((TOKENS,) + tail)


def local(
    hidden_in,
    attn_gain,
    w_query,
    w_key,
    w_value,
    w_out,
    cache_k,
    cache_v,
    cache_len,
    ffn_gain,
    router,
    routes,
    w_gate_up,
    w_down,
):
    width = hidden_in.shape[1]
    head_dev = cache_k.shape[1]
    n_experts = w_gate_up.shape[0]
    whole_in = gather_rows(hidden_in)
    normed = rms_scale(whole_in, attn_gain)
    positions = (cache_len[:, None] + jnp.arange(NEW, dtype=jnp.int32)[None, :]).reshape(-1)
    positions = from_request_order(positions)

    def project(weight):
        return jnp.dot(normed, weight, preferred_element_type=jnp.float32).reshape(
            TOKENS, head_dev, HDIM
        )

    def by_request(values):
        values = to_request_order(values)
        return values.reshape(REQS, NEW, head_dev, HDIM).transpose(0, 2, 1, 3)

    query = rotate(project(w_query), positions).astype(jnp.bfloat16)
    key_new = rotate(project(w_key), positions).astype(jnp.bfloat16)
    value_new = project(w_value).astype(jnp.bfloat16)
    heads_out = attend(
        by_request(query), by_request(key_new), by_request(value_new), cache_k, cache_v, cache_len
    )
    heads_flat = from_request_order(heads_out.transpose(0, 2, 1, 3).reshape(TOKENS, head_dev * HDIM))
    attn = scatter_rows(
        jnp.dot(heads_flat, w_out, preferred_element_type=jnp.float32).astype(jnp.bfloat16)
    )
    middle = (hidden_in.astype(jnp.float32) + attn).astype(jnp.bfloat16)
    normed2 = gather_rows(rms_scale(middle, ffn_gain))
    logits = jnp.dot(normed2, router, preferred_element_type=jnp.float32)
    routes = from_request_order(routes)
    pair_weights = route_weights(logits, routes)
    running = jnp.zeros((TOKENS, width), jnp.float32)
    for expert in range(n_experts):
        dense_weight = jnp.sum(jnp.where(routes == expert, pair_weights, 0.0), axis=1)
        running = (
            running
            + expert_apply(normed2, w_gate_up[expert], w_down[expert]) * dense_weight[:, None]
        )
    expert_out = scatter_rows(running.astype(jnp.bfloat16))
    return (middle.astype(jnp.float32) + expert_out).astype(jnp.bfloat16)


def solution(mesh):
    dp = mesh.shape["dp"]
    fine = Mesh(mesh.devices.reshape((dp,) + tuple(n for _, n in SUB)), ("dp",) + TENSOR)
    rows = ("dp",) + TENSOR
    in_specs = (
        P(rows, None),
        P(),
        P(None, TENSOR),
        P(None, TENSOR),
        P(None, TENSOR),
        P(TENSOR, None),
        P("dp", TENSOR, None, None),
        P("dp", TENSOR, None, None),
        P("dp"),
        P(),
        P(),
        P("dp", None),
        P(None, None, None, TENSOR),
        P(None, TENSOR, None),
    )
    out_specs = P(rows, None)
    return jax.shard_map(local, mesh=fine, in_specs=in_specs, out_specs=out_specs, check_vma=False)
```

```python
import jax
import jax.numpy as jnp
from jax import lax
from jax.experimental import pallas as pl
from jax.experimental.pallas import tpu as pltpu
from jax.sharding import Mesh
from jax.sharding import PartitionSpec as P

HDIM = 64
REQS = 8
NEW = 96
TOKENS = 768

SUB = (("x", 4), ("zh", 4), ("core", 2))
TENSOR = tuple(name for name, _ in SUB)
SIZE = dict(SUB)

eps = 1e-05


def rms_scale(rows_in, gain):
    values = rows_in.astype(jnp.float32)
    mean_square = jnp.mean(values * values, axis=-1, keepdims=True)
    return (values * lax.rsqrt(mean_square + eps) * gain.astype(jnp.float32)).astype(jnp.bfloat16)


def rotate(values, positions):
    half_dim = values.shape[-1] // 2
    inverse = 10000.0 ** (-2.0 * jnp.arange(half_dim, dtype=jnp.float32) / values.shape[-1])
    angles = positions.astype(jnp.float32)[:, None] * inverse[None, :]
    cosine = jnp.cos(angles)[:, None, :]
    sine_part = jnp.sin(angles)[:, None, :]
    front = values[..., :half_dim]
    back = values[..., half_dim:]
    return jnp.concatenate(
        [front * cosine - back * sine_part, back * cosine + front * sine_part], axis=-1
    )


def route_weights(logits, routes):
    expert_iota = jnp.arange(logits.shape[1], dtype=jnp.int32)[None, :]
    first_logit = jnp.sum(jnp.where(routes[:, 0:1] == expert_iota, logits, 0.0), axis=1)
    second_logit = jnp.sum(jnp.where(routes[:, 1:2] == expert_iota, logits, 0.0), axis=1)
    first_weight = 1.0 / (1.0 + jnp.exp(second_logit - first_logit))
    second_weight = 1.0 / (1.0 + jnp.exp(first_logit - second_logit))
    return jnp.stack([first_weight, second_weight], axis=1)


def expert_apply(rows_in, gate_up, down_part):
    both = jnp.einsum("td,kdf->ktf", rows_in, gate_up, preferred_element_type=jnp.float32)
    inner = (jax.nn.silu(both[0]) * both[1]).astype(jnp.bfloat16)
    return jnp.dot(inner, down_part, preferred_element_type=jnp.float32)


def attend(query, key_new, value_new, cache_k, cache_v, cache_len):
    cached_scores = (
        jnp.einsum("rhqd,rhkd->rhqk", query, cache_k, preferred_element_type=jnp.float32) * 0.125
    )
    fresh_scores = (
        jnp.einsum("rhqd,rhkd->rhqk", query, key_new, preferred_element_type=jnp.float32) * 0.125
    )
    key_pos = jnp.arange(cache_k.shape[2], dtype=jnp.int32)
    cached_mask = key_pos[None, None, None, :] < cache_len[:, None, None, None]
    new_pos = jnp.arange(query.shape[2], dtype=jnp.int32)
    fresh_mask = (new_pos[:, None] >= new_pos[None, :])[None, None]
    cached_scores = jnp.where(cached_mask, cached_scores, -1e30)
    fresh_scores = jnp.where(fresh_mask, fresh_scores, -1e30)
    peak = jnp.maximum(
        jnp.max(cached_scores, axis=-1, keepdims=True),
        jnp.max(fresh_scores, axis=-1, keepdims=True),
    )
    cached_expo = jnp.exp(cached_scores - peak)
    fresh_expo = jnp.exp(fresh_scores - peak)
    denominator = jnp.sum(cached_expo, axis=-1, keepdims=True) + jnp.sum(
        fresh_expo, axis=-1, keepdims=True
    )
    mixed = jnp.einsum(
        "rhqk,rhkd->rhqd",
        cached_expo.astype(jnp.bfloat16),
        cache_v,
        preferred_element_type=jnp.float32,
    )
    mixed = mixed + jnp.einsum(
        "rhqk,rhkd->rhqd",
        fresh_expo.astype(jnp.bfloat16),
        value_new,
        preferred_element_type=jnp.float32,
    )
    return (mixed / denominator).astype(jnp.bfloat16)


def shifts(axis, step):
    n = SIZE[axis]
    return [(i, (i + step) % n) for i in range(n)]


def gather_stage(rows, axis):
    n = SIZE[axis]
    me = lax.axis_index(axis)
    blk = rows.shape[0]
    out = jnp.zeros((n * blk,) + rows.shape[1:], rows.dtype)
    out = lax.dynamic_update_slice_in_dim(out, rows, me * blk, axis=0)
    for step in range(1, n):
        got = lax.ppermute(rows, axis, shifts(axis, step))
        out = lax.dynamic_update_slice_in_dim(out, got, ((me - step) % n) * blk, axis=0)
    return out


def scatter_stage(rows, axis):
    n = SIZE[axis]
    me = lax.axis_index(axis)
    chunks = rows.reshape((n, rows.shape[0] // n) + rows.shape[1:])
    total = lax.dynamic_index_in_dim(chunks, me, axis=0, keepdims=False).astype(jnp.float32)
    for step in range(1, n):
        send = lax.dynamic_index_in_dim(chunks, (me + step) % n, axis=0, keepdims=False)
        got = lax.ppermute(send.astype(jnp.bfloat16), axis, shifts(axis, step))
        total = total + got.astype(jnp.float32)
    return total


def gather_kernel(own_ref, out_ref, send_sem, recv_sem, local_sem):
    nx, nz = SIZE["x"], SIZE["zh"]
    dp = lax.axis_index("dp")
    x = lax.axis_index("x")
    z = lax.axis_index("zh")
    c = lax.axis_index("core")
    mesh_id = pl.DeviceIdType.MESH
    z_peers = [(dp, x, (z + s) % nz, c) for s in range(1, nz)]
    z_from = [(z + nz - s) % nz for s in range(1, nz)]
    x_peers = [(dp, (x + s) % nx, z, c) for s in range(1, nx)]
    x_from = [(x + nx - s) % nx for s in range(1, nx)]
    sibling = (dp, x, z, 1 - c)
    barrier = pltpu.get_barrier_semaphore()
    for peer in z_peers + x_peers + [sibling]:
        pl.semaphore_signal(barrier, 1, device_id=peer, device_id_type=mesh_id)
    pl.semaphore_wait(barrier, len(z_peers) + len(x_peers) + 1)
    local = pltpu.make_async_copy(own_ref, out_ref.at[c, x, z], local_sem.at[0])
    local.start()
    sent = []
    for k, peer in enumerate(z_peers):
        copy = pltpu.make_async_remote_copy(
            src_ref=own_ref,
            dst_ref=out_ref.at[c, x, z],
            send_sem=send_sem.at[k],
            recv_sem=recv_sem.at[k],
            device_id=peer,
            device_id_type=mesh_id,
        )
        copy.start()
        sent.append(copy)
    local.wait()
    for k, src in enumerate(z_from):
        pltpu.make_async_remote_copy(
            src_ref=own_ref,
            dst_ref=out_ref.at[c, x, src],
            send_sem=send_sem.at[k],
            recv_sem=recv_sem.at[k],
            device_id=z_peers[k],
            device_id_type=mesh_id,
        ).wait_recv()
    base = len(z_peers)
    for k, peer in enumerate(x_peers):
        copy = pltpu.make_async_remote_copy(
            src_ref=out_ref.at[c, x],
            dst_ref=out_ref.at[c, x],
            send_sem=send_sem.at[base + k],
            recv_sem=recv_sem.at[base + k],
            device_id=peer,
            device_id_type=mesh_id,
        )
        copy.start()
        sent.append(copy)
    for k, src in enumerate(x_from):
        pltpu.make_async_remote_copy(
            src_ref=out_ref.at[c, x],
            dst_ref=out_ref.at[c, src],
            send_sem=send_sem.at[base + k],
            recv_sem=recv_sem.at[base + k],
            device_id=x_peers[k],
            device_id_type=mesh_id,
        ).wait_recv()
    last = base + len(x_peers)
    copy = pltpu.make_async_remote_copy(
        src_ref=out_ref.at[c],
        dst_ref=out_ref.at[c],
        send_sem=send_sem.at[last],
        recv_sem=recv_sem.at[last],
        device_id=sibling,
        device_id_type=mesh_id,
    )
    copy.start()
    sent.append(copy)
    pltpu.make_async_remote_copy(
        src_ref=out_ref.at[c],
        dst_ref=out_ref.at[1 - c],
        send_sem=send_sem.at[last],
        recv_sem=recv_sem.at[last],
        device_id=sibling,
        device_id_type=mesh_id,
    ).wait_recv()
    for copy in sent:
        copy.wait_send()


def gather_rows(rows):
    nx, nz, nc = SIZE["x"], SIZE["zh"], SIZE["core"]
    links = (nz - 1) + (nx - 1) + 1
    out = pl.pallas_call(
        gather_kernel,
        out_shape=jax.ShapeDtypeStruct((nc, nx, nz) + rows.shape, rows.dtype),
        in_specs=[pl.BlockSpec(memory_space=pltpu.VMEM)],
        out_specs=pl.BlockSpec(memory_space=pltpu.VMEM),
        scratch_shapes=[
            pltpu.SemaphoreType.DMA((links,)),
            pltpu.SemaphoreType.DMA((links,)),
            pltpu.SemaphoreType.DMA((1,)),
        ],
        compiler_params=pltpu.CompilerParams(collective_id=0, has_side_effects=True),
    )(rows)
    return out.reshape((nc * nx * nz * rows.shape[0],) + rows.shape[1:])


def scatter_kernel(part_ref, out_ref, got_c, sum_c, got_x, sum_x, got_z, send_sem, recv_sem):
    nx, nz = SIZE["x"], SIZE["zh"]
    dp = lax.axis_index("dp")
    x = lax.axis_index("x")
    z = lax.axis_index("zh")
    c = lax.axis_index("core")
    mesh_id = pl.DeviceIdType.MESH
    sibling = (dp, x, z, 1 - c)
    x_peers = [(dp, (x + s) % nx, z, c) for s in range(1, nx)]
    z_peers = [(dp, x, (z + s) % nz, c) for s in range(1, nz)]
    barrier = pltpu.get_barrier_semaphore()
    for peer in [sibling] + x_peers + z_peers:
        pl.semaphore_signal(barrier, 1, device_id=peer, device_id_type=mesh_id)
    pl.semaphore_wait(barrier, 1 + len(x_peers) + len(z_peers))
    sent = []

    def exchange(src, dst, k, peer):
        copy = pltpu.make_async_remote_copy(
            src_ref=src,
            dst_ref=dst,
            send_sem=send_sem.at[k],
            recv_sem=recv_sem.at[k],
            device_id=peer,
            device_id_type=mesh_id,
        )
        copy.start()
        sent.append(copy)
        return copy

    exchange(part_ref.at[1 - c], got_c, 0, sibling).wait_recv()
    sum_c[...] = (
        part_ref[c].astype(jnp.float32) + got_c[...].astype(jnp.float32)
    ).astype(sum_c.dtype)
    copies = [
        exchange(sum_c.at[(x + s) % nx], got_x.at[s - 1], s, x_peers[s - 1]) for s in range(1, nx)
    ]
    for copy in copies:
        copy.wait_recv()
    total = sum_c[x].astype(jnp.float32)
    for k in range(nx - 1):
        total = total + got_x[k].astype(jnp.float32)
    sum_x[...] = total.astype(sum_x.dtype)
    base = nx - 1
    copies = [
        exchange(sum_x.at[(z + s) % nz], got_z.at[s - 1], base + s, z_peers[s - 1])
        for s in range(1, nz)
    ]
    for copy in copies:
        copy.wait_recv()
    total = sum_x[z].astype(jnp.float32)
    for k in range(nz - 1):
        total = total + got_z[k].astype(jnp.float32)
    out_ref[...] = total
    for copy in sent:
        copy.wait_send()


def scatter_rows(rows):
    nx, nz, nc = SIZE["x"], SIZE["zh"], SIZE["core"]
    blk = rows.shape[0] // (nx * nz * nc)
    tail = rows.shape[1:]
    part = rows.reshape((nc, nx, nz, blk) + tail)
    links = 1 + (nx - 1) + (nz - 1)
    return pl.pallas_call(
        scatter_kernel,
        out_shape=jax.ShapeDtypeStruct((blk,) + tail, jnp.float32),
        in_specs=[pl.BlockSpec(memory_space=pltpu.VMEM)],
        out_specs=pl.BlockSpec(memory_space=pltpu.VMEM),
        scratch_shapes=[
            pltpu.VMEM((nx, nz, blk) + tail, rows.dtype),
            pltpu.VMEM((nx, nz, blk) + tail, rows.dtype),
            pltpu.VMEM((nx - 1, nz, blk) + tail, rows.dtype),
            pltpu.VMEM((nz, blk) + tail, rows.dtype),
            pltpu.VMEM((nz - 1, blk) + tail, rows.dtype),
            pltpu.SemaphoreType.DMA((links,)),
            pltpu.SemaphoreType.DMA((links,)),
        ],
        compiler_params=pltpu.CompilerParams(collective_id=1, has_side_effects=True),
    )(part)


def to_request_order(values):
    nx, nz, nc = SIZE["x"], SIZE["zh"], SIZE["core"]
    blk = TOKENS // (nx * nz * nc)
    tail = values.shape[1:]
    values = values.reshape((nc, nx, nz, blk) + tail)
    values = jnp.moveaxis(values, 0, 2)
    return values.reshape((TOKENS,) + tail)


def from_request_order(values):
    nx, nz, nc = SIZE["x"], SIZE["zh"], SIZE["core"]
    blk = TOKENS // (nx * nz * nc)
    tail = values.shape[1:]
    values = values.reshape((nx, nz, nc, blk) + tail)
    values = jnp.moveaxis(values, 2, 0)
    return values.reshape((TOKENS,) + tail)


def local(
    hidden_in,
    attn_gain,
    w_query,
    w_key,
    w_value,
    w_out,
    cache_k,
    cache_v,
    cache_len,
    ffn_gain,
    router,
    routes,
    w_gate_up,
    w_down,
):
    width = hidden_in.shape[1]
    head_dev = cache_k.shape[1]
    n_experts = w_gate_up.shape[0]
    whole_in = gather_rows(hidden_in)
    normed = rms_scale(whole_in, attn_gain)
    positions = (cache_len[:, None] + jnp.arange(NEW, dtype=jnp.int32)[None, :]).reshape(-1)
    positions = from_request_order(positions)

    def project(weight):
        return jnp.dot(normed, weight, preferred_element_type=jnp.float32).reshape(
            TOKENS, head_dev, HDIM
        )

    def by_request(values):
        values = to_request_order(values)
        return values.reshape(REQS, NEW, head_dev, HDIM).transpose(0, 2, 1, 3)

    query = rotate(project(w_query), positions).astype(jnp.bfloat16)
    key_new = rotate(project(w_key), positions).astype(jnp.bfloat16)
    value_new = project(w_value).astype(jnp.bfloat16)
    heads_out = attend(
        by_request(query), by_request(key_new), by_request(value_new), cache_k, cache_v, cache_len
    )
    heads_flat = from_request_order(heads_out.transpose(0, 2, 1, 3).reshape(TOKENS, head_dev * HDIM))
    attn = scatter_rows(
        jnp.dot(heads_flat, w_out, preferred_element_type=jnp.float32).astype(jnp.bfloat16)
    )
    middle = (hidden_in.astype(jnp.float32) + attn).astype(jnp.bfloat16)
    normed2 = gather_rows(rms_scale(middle, ffn_gain))
    logits = jnp.dot(normed2, router, preferred_element_type=jnp.float32)
    routes = from_request_order(routes)
    pair_weights = route_weights(logits, routes)
    running = jnp.zeros((TOKENS, width), jnp.float32)
    for expert in range(n_experts):
        dense_weight = jnp.sum(jnp.where(routes == expert, pair_weights, 0.0), axis=1)
        running = (
            running
            + expert_apply(normed2, w_gate_up[expert], w_down[expert]) * dense_weight[:, None]
        )
    expert_out = scatter_rows(running.astype(jnp.bfloat16))
    return (middle.astype(jnp.float32) + expert_out).astype(jnp.bfloat16)


def solution(mesh):
    dp = mesh.shape["dp"]
    fine = Mesh(mesh.devices.reshape((dp,) + tuple(n for _, n in SUB)), ("dp",) + TENSOR)
    rows = ("dp",) + TENSOR
    in_specs = (
        P(rows, None),
        P(),
        P(None, TENSOR),
        P(None, TENSOR),
        P(None, TENSOR),
        P(TENSOR, None),
        P("dp", TENSOR, None, None),
        P("dp", TENSOR, None, None),
        P("dp"),
        P(),
        P(),
        P("dp", None),
        P(None, None, None, TENSOR),
        P(None, TENSOR, None),
    )
    out_specs = P(rows, None)
    return jax.shard_map(local, mesh=fine, in_specs=in_specs, out_specs=out_specs, check_vma=False)
```

```python
import jax
import jax.numpy as jnp
from jax import lax
from jax.experimental import pallas as pl
from jax.experimental.pallas import tpu as pltpu
from jax.sharding import Mesh
from jax.sharding import PartitionSpec as P

HDIM = 64
REQS = 8
NEW = 96
TOKENS = 768

SUB = (("x", 4), ("zh", 4), ("core", 2))
TENSOR = tuple(name for name, _ in SUB)
SIZE = dict(SUB)

eps = 1e-05


def rms_scale(rows_in, gain):
    values = rows_in.astype(jnp.float32)
    mean_square = jnp.mean(values * values, axis=-1, keepdims=True)
    return (values * lax.rsqrt(mean_square + eps) * gain.astype(jnp.float32)).astype(jnp.bfloat16)


def rotate(values, positions):
    half_dim = values.shape[-1] // 2
    inverse = 10000.0 ** (-2.0 * jnp.arange(half_dim, dtype=jnp.float32) / values.shape[-1])
    angles = positions.astype(jnp.float32)[:, None] * inverse[None, :]
    cosine = jnp.cos(angles)[:, None, :]
    sine_part = jnp.sin(angles)[:, None, :]
    front = values[..., :half_dim]
    back = values[..., half_dim:]
    return jnp.concatenate(
        [front * cosine - back * sine_part, back * cosine + front * sine_part], axis=-1
    )


def route_weights(logits, routes):
    expert_iota = jnp.arange(logits.shape[1], dtype=jnp.int32)[None, :]
    first_logit = jnp.sum(jnp.where(routes[:, 0:1] == expert_iota, logits, 0.0), axis=1)
    second_logit = jnp.sum(jnp.where(routes[:, 1:2] == expert_iota, logits, 0.0), axis=1)
    first_weight = 1.0 / (1.0 + jnp.exp(second_logit - first_logit))
    second_weight = 1.0 / (1.0 + jnp.exp(first_logit - second_logit))
    return jnp.stack([first_weight, second_weight], axis=1)


def expert_apply(rows_in, gate_up, down_part):
    both = jnp.einsum("td,kdf->ktf", rows_in, gate_up, preferred_element_type=jnp.float32)
    inner = (jax.nn.silu(both[0]) * both[1]).astype(jnp.bfloat16)
    return jnp.dot(inner, down_part, preferred_element_type=jnp.float32)


def attend(query, key_new, value_new, cache_k, cache_v, cache_len):
    cached_scores = (
        jnp.einsum("rhqd,rhkd->rhqk", query, cache_k, preferred_element_type=jnp.float32) * 0.125
    )
    fresh_scores = (
        jnp.einsum("rhqd,rhkd->rhqk", query, key_new, preferred_element_type=jnp.float32) * 0.125
    )
    key_pos = jnp.arange(cache_k.shape[2], dtype=jnp.int32)
    cached_mask = key_pos[None, None, None, :] < cache_len[:, None, None, None]
    new_pos = jnp.arange(query.shape[2], dtype=jnp.int32)
    fresh_mask = (new_pos[:, None] >= new_pos[None, :])[None, None]
    cached_scores = jnp.where(cached_mask, cached_scores, -1e30)
    fresh_scores = jnp.where(fresh_mask, fresh_scores, -1e30)
    peak = jnp.maximum(
        jnp.max(cached_scores, axis=-1, keepdims=True),
        jnp.max(fresh_scores, axis=-1, keepdims=True),
    )
    cached_expo = jnp.exp(cached_scores - peak)
    fresh_expo = jnp.exp(fresh_scores - peak)
    denominator = jnp.sum(cached_expo, axis=-1, keepdims=True) + jnp.sum(
        fresh_expo, axis=-1, keepdims=True
    )
    mixed = jnp.einsum(
        "rhqk,rhkd->rhqd",
        cached_expo.astype(jnp.bfloat16),
        cache_v,
        preferred_element_type=jnp.float32,
    )
    mixed = mixed + jnp.einsum(
        "rhqk,rhkd->rhqd",
        fresh_expo.astype(jnp.bfloat16),
        value_new,
        preferred_element_type=jnp.float32,
    )
    return (mixed / denominator).astype(jnp.bfloat16)


def shifts(axis, step):
    n = SIZE[axis]
    return [(i, (i + step) % n) for i in range(n)]


def gather_stage(rows, axis):
    n = SIZE[axis]
    me = lax.axis_index(axis)
    blk = rows.shape[0]
    out = jnp.zeros((n * blk,) + rows.shape[1:], rows.dtype)
    out = lax.dynamic_update_slice_in_dim(out, rows, me * blk, axis=0)
    for step in range(1, n):
        got = lax.ppermute(rows, axis, shifts(axis, step))
        out = lax.dynamic_update_slice_in_dim(out, got, ((me - step) % n) * blk, axis=0)
    return out


def scatter_stage(rows, axis):
    n = SIZE[axis]
    me = lax.axis_index(axis)
    chunks = rows.reshape((n, rows.shape[0] // n) + rows.shape[1:])
    total = lax.dynamic_index_in_dim(chunks, me, axis=0, keepdims=False).astype(jnp.float32)
    for step in range(1, n):
        send = lax.dynamic_index_in_dim(chunks, (me + step) % n, axis=0, keepdims=False)
        got = lax.ppermute(send.astype(jnp.bfloat16), axis, shifts(axis, step))
        total = total + got.astype(jnp.float32)
    return total


def ring_peers(axis):
    here = {name: lax.axis_index(name) for name in ("dp",) + TENSOR}
    n = SIZE[axis]
    me = here[axis]

    def at(member):
        return tuple(member if name == axis else here[name] for name in ("dp",) + TENSOR)

    return me, n, at((me + 1) % n), at((me + n - 1) % n)


def halves(ref):
    half = ref.shape[-1] // 2
    return ref.at[..., pl.ds(0, half)], ref.at[..., pl.ds(half, half)]


def remote(src, dst, send_sem, recv_sem, peer):
    return pltpu.make_async_remote_copy(
        src_ref=src,
        dst_ref=dst,
        send_sem=send_sem,
        recv_sem=recv_sem,
        device_id=peer,
        device_id_type=pl.DeviceIdType.MESH,
    )


def ring_gather(slot, first, axis, send_sem, recv_sem, sent):
    me, n, right, left = ring_peers(axis)
    opposite = (me + 2) % n
    for k, peer in ((0, right), (1, left)):
        copy = remote(first, slot(me), send_sem.at[k], recv_sem.at[k], peer)
        copy.start()
        sent.append(copy)
    remote(first, slot((me + n - 1) % n), send_sem.at[0], recv_sem.at[0], left).wait_recv()
    copy = remote(
        halves(slot((me + n - 1) % n))[0], halves(slot((me + n - 1) % n))[0],
        send_sem.at[2], recv_sem.at[2], right,
    )
    copy.start()
    sent.append(copy)
    remote(first, slot((me + 1) % n), send_sem.at[1], recv_sem.at[1], right).wait_recv()
    copy = remote(
        halves(slot((me + 1) % n))[1], halves(slot((me + 1) % n))[1],
        send_sem.at[3], recv_sem.at[3], left,
    )
    copy.start()
    sent.append(copy)
    lo, hi = halves(slot(opposite))
    remote(lo, lo, send_sem.at[2], recv_sem.at[2], left).wait_recv()
    remote(hi, hi, send_sem.at[3], recv_sem.at[3], right).wait_recv()


def gather_kernel(own_ref, out_ref, send_sem, recv_sem, local_sem):
    x = lax.axis_index("x")
    z = lax.axis_index("zh")
    c = lax.axis_index("core")
    _, _, z_right, z_left = ring_peers("zh")
    _, _, x_right, x_left = ring_peers("x")
    _, _, sibling, _ = ring_peers("core")
    barrier = pltpu.get_barrier_semaphore()
    for peer in (z_right, z_left, x_right, x_left, sibling):
        pl.semaphore_signal(barrier, 1, device_id=peer, device_id_type=pl.DeviceIdType.MESH)
    pl.semaphore_wait(barrier, 5)
    local = pltpu.make_async_copy(own_ref, out_ref.at[c, x, z], local_sem.at[0])
    local.start()
    sent = []
    ring_gather(lambda i: out_ref.at[c, x, i], own_ref, "zh", send_sem.at[0:4], recv_sem.at[0:4], sent)
    local.wait()
    ring_gather(lambda i: out_ref.at[c, i], out_ref.at[c, x], "x", send_sem.at[4:8], recv_sem.at[4:8], sent)
    copy = remote(out_ref.at[c], out_ref.at[c], send_sem.at[8], recv_sem.at[8], sibling)
    copy.start()
    sent.append(copy)
    remote(out_ref.at[c], out_ref.at[1 - c], send_sem.at[8], recv_sem.at[8], sibling).wait_recv()
    for copy in sent:
        copy.wait_send()


def gather_rows(rows):
    nx, nz, nc = SIZE["x"], SIZE["zh"], SIZE["core"]
    links = 9
    out = pl.pallas_call(
        gather_kernel,
        out_shape=jax.ShapeDtypeStruct((nc, nx, nz) + rows.shape, rows.dtype),
        in_specs=[pl.BlockSpec(memory_space=pltpu.VMEM)],
        out_specs=pl.BlockSpec(memory_space=pltpu.VMEM),
        scratch_shapes=[
            pltpu.SemaphoreType.DMA((links,)),
            pltpu.SemaphoreType.DMA((links,)),
            pltpu.SemaphoreType.DMA((1,)),
        ],
        compiler_params=pltpu.CompilerParams(collective_id=0, has_side_effects=True),
    )(rows)
    return out.reshape((nc * nx * nz * rows.shape[0],) + rows.shape[1:])


def ring_scatter(chunk, axis, buffers, send_sem, recv_sem, sent):
    me, n, right, left = ring_peers(axis)
    got_lo, got_hi, to_right, to_left, from_left, from_right = buffers
    lo, hi = halves(chunk((me + 2) % n))
    for k, src, dst, peer in ((0, lo, got_lo, right), (1, hi, got_hi, left)):
        copy = remote(src, dst, send_sem.at[k], recv_sem.at[k], peer)
        copy.start()
        sent.append(copy)
    half = to_right.shape[-1] // 2
    remote(lo, got_lo, send_sem.at[0], recv_sem.at[0], left).wait_recv()
    ahead = chunk((me + 1) % n)
    to_right[..., :half] = (
        ahead[..., :half].astype(jnp.float32) + got_lo[...].astype(jnp.float32)
    ).astype(to_right.dtype)
    to_right[..., half:] = ahead[..., half:]
    copy = remote(to_right, from_left, send_sem.at[2], recv_sem.at[2], right)
    copy.start()
    sent.append(copy)
    remote(hi, got_hi, send_sem.at[1], recv_sem.at[1], right).wait_recv()
    behind = chunk((me + n - 1) % n)
    to_left[..., :half] = behind[..., :half]
    to_left[..., half:] = (
        behind[..., half:].astype(jnp.float32) + got_hi[...].astype(jnp.float32)
    ).astype(to_left.dtype)
    copy = remote(to_left, from_right, send_sem.at[3], recv_sem.at[3], left)
    copy.start()
    sent.append(copy)
    remote(to_right, from_left, send_sem.at[2], recv_sem.at[2], left).wait_recv()
    remote(to_left, from_right, send_sem.at[3], recv_sem.at[3], right).wait_recv()
    return (
        chunk(me)[...].astype(jnp.float32)
        + from_left[...].astype(jnp.float32)
        + from_right[...].astype(jnp.float32)
    )


def scatter_kernel(part_ref, out_ref, got_c, sum_c, x_bufs, sum_x, z_bufs, send_sem, recv_sem):
    c = lax.axis_index("core")
    _, _, z_right, z_left = ring_peers("zh")
    _, _, x_right, x_left = ring_peers("x")
    _, _, sibling, _ = ring_peers("core")
    barrier = pltpu.get_barrier_semaphore()
    for peer in (sibling, x_right, x_left, z_right, z_left):
        pl.semaphore_signal(barrier, 1, device_id=peer, device_id_type=pl.DeviceIdType.MESH)
    pl.semaphore_wait(barrier, 5)
    sent = []
    copy = remote(part_ref.at[1 - c], got_c, send_sem.at[0], recv_sem.at[0], sibling)
    copy.start()
    sent.append(copy)
    copy.wait_recv()
    sum_c[...] = (
        part_ref[c].astype(jnp.float32) + got_c[...].astype(jnp.float32)
    ).astype(sum_c.dtype)
    x_bufs = [x_bufs.at[0, 0], x_bufs.at[0, 1]] + [x_bufs.at[1, k] for k in range(4)]
    x_bufs = [x_bufs[0].at[..., pl.ds(0, x_bufs[0].shape[-1] // 2)], x_bufs[1].at[..., pl.ds(0, x_bufs[1].shape[-1] // 2)]] + x_bufs[2:]
    total = ring_scatter(lambda i: sum_c.at[i], "x", x_bufs, send_sem.at[1:5], recv_sem.at[1:5], sent)
    sum_x[...] = total.astype(sum_x.dtype)
    z_bufs = [z_bufs.at[0, 0], z_bufs.at[0, 1]] + [z_bufs.at[1, k] for k in range(4)]
    z_bufs = [z_bufs[0].at[..., pl.ds(0, z_bufs[0].shape[-1] // 2)], z_bufs[1].at[..., pl.ds(0, z_bufs[1].shape[-1] // 2)]] + z_bufs[2:]
    out_ref[...] = ring_scatter(lambda i: sum_x.at[i], "zh", z_bufs, send_sem.at[5:9], recv_sem.at[5:9], sent)
    for copy in sent:
        copy.wait_send()


def scatter_rows(rows):
    nx, nz, nc = SIZE["x"], SIZE["zh"], SIZE["core"]
    blk = rows.shape[0] // (nx * nz * nc)
    tail = rows.shape[1:]
    part = rows.reshape((nc, nx, nz, blk) + tail)
    links = 9
    return pl.pallas_call(
        scatter_kernel,
        out_shape=jax.ShapeDtypeStruct((blk,) + tail, jnp.float32),
        in_specs=[pl.BlockSpec(memory_space=pltpu.VMEM)],
        out_specs=pl.BlockSpec(memory_space=pltpu.VMEM),
        scratch_shapes=[
            pltpu.VMEM((nx, nz, blk) + tail, rows.dtype),
            pltpu.VMEM((nx, nz, blk) + tail, rows.dtype),
            pltpu.VMEM((2, 4, nz, blk) + tail, rows.dtype),
            pltpu.VMEM((nz, blk) + tail, rows.dtype),
            pltpu.VMEM((2, 4, blk) + tail, rows.dtype),
            pltpu.SemaphoreType.DMA((links,)),
            pltpu.SemaphoreType.DMA((links,)),
        ],
        compiler_params=pltpu.CompilerParams(collective_id=1, has_side_effects=True),
    )(part)


def to_request_order(values):
    nx, nz, nc = SIZE["x"], SIZE["zh"], SIZE["core"]
    blk = TOKENS // (nx * nz * nc)
    tail = values.shape[1:]
    values = values.reshape((nc, nx, nz, blk) + tail)
    values = jnp.moveaxis(values, 0, 2)
    return values.reshape((TOKENS,) + tail)


def from_request_order(values):
    nx, nz, nc = SIZE["x"], SIZE["zh"], SIZE["core"]
    blk = TOKENS // (nx * nz * nc)
    tail = values.shape[1:]
    values = values.reshape((nx, nz, nc, blk) + tail)
    values = jnp.moveaxis(values, 2, 0)
    return values.reshape((TOKENS,) + tail)


def local(
    hidden_in,
    attn_gain,
    w_query,
    w_key,
    w_value,
    w_out,
    cache_k,
    cache_v,
    cache_len,
    ffn_gain,
    router,
    routes,
    w_gate_up,
    w_down,
):
    width = hidden_in.shape[1]
    head_dev = cache_k.shape[1]
    n_experts = w_gate_up.shape[0]
    whole_in = gather_rows(hidden_in)
    normed = rms_scale(whole_in, attn_gain)
    positions = (cache_len[:, None] + jnp.arange(NEW, dtype=jnp.int32)[None, :]).reshape(-1)
    positions = from_request_order(positions)

    def project(weight):
        return jnp.dot(normed, weight, preferred_element_type=jnp.float32).reshape(
            TOKENS, head_dev, HDIM
        )

    def by_request(values):
        values = to_request_order(values)
        return values.reshape(REQS, NEW, head_dev, HDIM).transpose(0, 2, 1, 3)

    query = rotate(project(w_query), positions).astype(jnp.bfloat16)
    key_new = rotate(project(w_key), positions).astype(jnp.bfloat16)
    value_new = project(w_value).astype(jnp.bfloat16)
    heads_out = attend(
        by_request(query), by_request(key_new), by_request(value_new), cache_k, cache_v, cache_len
    )
    heads_flat = from_request_order(heads_out.transpose(0, 2, 1, 3).reshape(TOKENS, head_dev * HDIM))
    attn = scatter_rows(
        jnp.dot(heads_flat, w_out, preferred_element_type=jnp.float32).astype(jnp.bfloat16)
    )
    middle = (hidden_in.astype(jnp.float32) + attn).astype(jnp.bfloat16)
    normed2 = gather_rows(rms_scale(middle, ffn_gain))
    logits = jnp.dot(normed2, router, preferred_element_type=jnp.float32)
    routes = from_request_order(routes)
    pair_weights = route_weights(logits, routes)
    running = jnp.zeros((TOKENS, width), jnp.float32)
    for expert in range(n_experts):
        dense_weight = jnp.sum(jnp.where(routes == expert, pair_weights, 0.0), axis=1)
        running = (
            running
            + expert_apply(normed2, w_gate_up[expert], w_down[expert]) * dense_weight[:, None]
        )
    expert_out = scatter_rows(running.astype(jnp.bfloat16))
    return (middle.astype(jnp.float32) + expert_out).astype(jnp.bfloat16)


def solution(mesh):
    dp = mesh.shape["dp"]
    fine = Mesh(mesh.devices.reshape((dp,) + tuple(n for _, n in SUB)), ("dp",) + TENSOR)
    rows = ("dp",) + TENSOR
    in_specs = (
        P(rows, None),
        P(),
        P(None, TENSOR),
        P(None, TENSOR),
        P(None, TENSOR),
        P(TENSOR, None),
        P("dp", TENSOR, None, None),
        P("dp", TENSOR, None, None),
        P("dp"),
        P(),
        P(),
        P("dp", None),
        P(None, None, None, TENSOR),
        P(None, TENSOR, None),
    )
    out_specs = P(rows, None)
    return jax.shard_map(local, mesh=fine, in_specs=in_specs, out_specs=out_specs, check_vma=False)
```

```python
import functools

import jax
import jax.numpy as jnp
from jax import lax
from jax.experimental import pallas as pl
from jax.experimental.pallas import tpu as pltpu
from jax.sharding import Mesh
from jax.sharding import PartitionSpec as P

HDIM = 64
REQS = 8
NEW = 96
TOKENS = 768

SUB = (("x", 4), ("zh", 4), ("core", 2))
TENSOR = tuple(name for name, _ in SUB)
SIZE = dict(SUB)

eps = 1e-05


def rms_scale(rows_in, gain):
    values = rows_in.astype(jnp.float32)
    mean_square = jnp.mean(values * values, axis=-1, keepdims=True)
    return (values * lax.rsqrt(mean_square + eps) * gain.astype(jnp.float32)).astype(jnp.bfloat16)


def rotate(values, positions):
    half_dim = values.shape[-1] // 2
    inverse = 10000.0 ** (-2.0 * jnp.arange(half_dim, dtype=jnp.float32) / values.shape[-1])
    angles = positions.astype(jnp.float32)[:, None] * inverse[None, :]
    cosine = jnp.cos(angles)[:, None, :]
    sine_part = jnp.sin(angles)[:, None, :]
    front = values[..., :half_dim]
    back = values[..., half_dim:]
    return jnp.concatenate(
        [front * cosine - back * sine_part, back * cosine + front * sine_part], axis=-1
    )


def route_weights(logits, routes):
    expert_iota = jnp.arange(logits.shape[1], dtype=jnp.int32)[None, :]
    first_logit = jnp.sum(jnp.where(routes[:, 0:1] == expert_iota, logits, 0.0), axis=1)
    second_logit = jnp.sum(jnp.where(routes[:, 1:2] == expert_iota, logits, 0.0), axis=1)
    first_weight = 1.0 / (1.0 + jnp.exp(second_logit - first_logit))
    second_weight = 1.0 / (1.0 + jnp.exp(first_logit - second_logit))
    return jnp.stack([first_weight, second_weight], axis=1)


def expert_apply(rows_in, gate_up, down_part):
    both = jnp.einsum("td,kdf->ktf", rows_in, gate_up, preferred_element_type=jnp.float32)
    inner = (jax.nn.silu(both[0]) * both[1]).astype(jnp.bfloat16)
    return jnp.dot(inner, down_part, preferred_element_type=jnp.float32)


def attend(query, key_new, value_new, cache_k, cache_v, cache_len):
    cached_scores = (
        jnp.einsum("rhqd,rhkd->rhqk", query, cache_k, preferred_element_type=jnp.float32) * 0.125
    )
    fresh_scores = (
        jnp.einsum("rhqd,rhkd->rhqk", query, key_new, preferred_element_type=jnp.float32) * 0.125
    )
    key_pos = jnp.arange(cache_k.shape[2], dtype=jnp.int32)
    cached_mask = key_pos[None, None, None, :] < cache_len[:, None, None, None]
    new_pos = jnp.arange(query.shape[2], dtype=jnp.int32)
    fresh_mask = (new_pos[:, None] >= new_pos[None, :])[None, None]
    cached_scores = jnp.where(cached_mask, cached_scores, -1e30)
    fresh_scores = jnp.where(fresh_mask, fresh_scores, -1e30)
    peak = jnp.maximum(
        jnp.max(cached_scores, axis=-1, keepdims=True),
        jnp.max(fresh_scores, axis=-1, keepdims=True),
    )
    cached_expo = jnp.exp(cached_scores - peak)
    fresh_expo = jnp.exp(fresh_scores - peak)
    denominator = jnp.sum(cached_expo, axis=-1, keepdims=True) + jnp.sum(
        fresh_expo, axis=-1, keepdims=True
    )
    mixed = jnp.einsum(
        "rhqk,rhkd->rhqd",
        cached_expo.astype(jnp.bfloat16),
        cache_v,
        preferred_element_type=jnp.float32,
    )
    mixed = mixed + jnp.einsum(
        "rhqk,rhkd->rhqd",
        fresh_expo.astype(jnp.bfloat16),
        value_new,
        preferred_element_type=jnp.float32,
    )
    return (mixed / denominator).astype(jnp.bfloat16)


def shifts(axis, step):
    n = SIZE[axis]
    return [(i, (i + step) % n) for i in range(n)]


def gather_stage(rows, axis):
    n = SIZE[axis]
    me = lax.axis_index(axis)
    blk = rows.shape[0]
    out = jnp.zeros((n * blk,) + rows.shape[1:], rows.dtype)
    out = lax.dynamic_update_slice_in_dim(out, rows, me * blk, axis=0)
    for step in range(1, n):
        got = lax.ppermute(rows, axis, shifts(axis, step))
        out = lax.dynamic_update_slice_in_dim(out, got, ((me - step) % n) * blk, axis=0)
    return out


def scatter_stage(rows, axis):
    n = SIZE[axis]
    me = lax.axis_index(axis)
    chunks = rows.reshape((n, rows.shape[0] // n) + rows.shape[1:])
    total = lax.dynamic_index_in_dim(chunks, me, axis=0, keepdims=False).astype(jnp.float32)
    for step in range(1, n):
        send = lax.dynamic_index_in_dim(chunks, (me + step) % n, axis=0, keepdims=False)
        got = lax.ppermute(send.astype(jnp.bfloat16), axis, shifts(axis, step))
        total = total + got.astype(jnp.float32)
    return total


def ring_peers(axis):
    here = {name: lax.axis_index(name) for name in ("dp",) + TENSOR}
    n = SIZE[axis]
    me = here[axis]

    def at(member):
        return tuple(member if name == axis else here[name] for name in ("dp",) + TENSOR)

    return me, n, at((me + 1) % n), at((me + n - 1) % n)


def halves(ref):
    half = ref.shape[-1] // 2
    return ref.at[..., pl.ds(0, half)], ref.at[..., pl.ds(half, half)]


def remote(src, dst, send_sem, recv_sem, peer):
    return pltpu.make_async_remote_copy(
        src_ref=src,
        dst_ref=dst,
        send_sem=send_sem,
        recv_sem=recv_sem,
        device_id=peer,
        device_id_type=pl.DeviceIdType.MESH,
    )


def ring_gather(slot, first, axis, send_sem, recv_sem, sent):
    me, n, right, left = ring_peers(axis)
    opposite = (me + 2) % n
    for k, peer in ((0, right), (1, left)):
        copy = remote(first, slot(me), send_sem.at[k], recv_sem.at[k], peer)
        copy.start()
        sent.append(copy)
    remote(first, slot((me + n - 1) % n), send_sem.at[0], recv_sem.at[0], left).wait_recv()
    copy = remote(
        halves(slot((me + n - 1) % n))[0], halves(slot((me + n - 1) % n))[0],
        send_sem.at[2], recv_sem.at[2], right,
    )
    copy.start()
    sent.append(copy)
    remote(first, slot((me + 1) % n), send_sem.at[1], recv_sem.at[1], right).wait_recv()
    copy = remote(
        halves(slot((me + 1) % n))[1], halves(slot((me + 1) % n))[1],
        send_sem.at[3], recv_sem.at[3], left,
    )
    copy.start()
    sent.append(copy)
    lo, hi = halves(slot(opposite))
    remote(lo, lo, send_sem.at[2], recv_sem.at[2], left).wait_recv()
    remote(hi, hi, send_sem.at[3], recv_sem.at[3], right).wait_recv()


def gather_kernel(own_ref, out_ref, send_sem, recv_sem, local_sem):
    x = lax.axis_index("x")
    z = lax.axis_index("zh")
    c = lax.axis_index("core")
    _, _, z_right, z_left = ring_peers("zh")
    _, _, x_right, x_left = ring_peers("x")
    _, _, sibling, _ = ring_peers("core")
    barrier = pltpu.get_barrier_semaphore()
    for peer in (z_right, z_left, x_right, x_left, sibling):
        pl.semaphore_signal(barrier, 1, device_id=peer, device_id_type=pl.DeviceIdType.MESH)
    pl.semaphore_wait(barrier, 5)
    local = pltpu.make_async_copy(own_ref, out_ref.at[c, x, z], local_sem.at[0])
    local.start()
    sent = []
    ring_gather(lambda i: out_ref.at[c, x, i], own_ref, "zh", send_sem.at[0:4], recv_sem.at[0:4], sent)
    local.wait()
    ring_gather(lambda i: out_ref.at[c, i], out_ref.at[c, x], "x", send_sem.at[4:8], recv_sem.at[4:8], sent)
    copy = remote(out_ref.at[c], out_ref.at[c], send_sem.at[8], recv_sem.at[8], sibling)
    copy.start()
    sent.append(copy)
    remote(out_ref.at[c], out_ref.at[1 - c], send_sem.at[8], recv_sem.at[8], sibling).wait_recv()
    for copy in sent:
        copy.wait_send()


def gather_rows(rows):
    nx, nz, nc = SIZE["x"], SIZE["zh"], SIZE["core"]
    links = 9
    out = pl.pallas_call(
        gather_kernel,
        out_shape=jax.ShapeDtypeStruct((nc, nx, nz) + rows.shape, rows.dtype),
        in_specs=[pl.BlockSpec(memory_space=pltpu.VMEM)],
        out_specs=pl.BlockSpec(memory_space=pltpu.VMEM),
        scratch_shapes=[
            pltpu.SemaphoreType.DMA((links,)),
            pltpu.SemaphoreType.DMA((links,)),
            pltpu.SemaphoreType.DMA((1,)),
        ],
        compiler_params=pltpu.CompilerParams(collective_id=0, has_side_effects=True),
    )(rows)
    return out.reshape((nc * nx * nz * rows.shape[0],) + rows.shape[1:])


def ring_scatter(chunk, axis, buffers, send_sem, recv_sem, sent):
    me, n, right, left = ring_peers(axis)
    got_lo, got_hi, to_right, to_left, from_left, from_right = buffers
    lo, hi = halves(chunk((me + 2) % n))
    for k, src, dst, peer in ((0, lo, got_lo, right), (1, hi, got_hi, left)):
        copy = remote(src, dst, send_sem.at[k], recv_sem.at[k], peer)
        copy.start()
        sent.append(copy)
    half = to_right.shape[-1] // 2
    remote(lo, got_lo, send_sem.at[0], recv_sem.at[0], left).wait_recv()
    ahead = chunk((me + 1) % n)
    to_right[..., :half] = (
        ahead[..., :half].astype(jnp.float32) + got_lo[...].astype(jnp.float32)
    ).astype(to_right.dtype)
    to_right[..., half:] = ahead[..., half:]
    copy = remote(to_right, from_left, send_sem.at[2], recv_sem.at[2], right)
    copy.start()
    sent.append(copy)
    remote(hi, got_hi, send_sem.at[1], recv_sem.at[1], right).wait_recv()
    behind = chunk((me + n - 1) % n)
    to_left[..., :half] = behind[..., :half]
    to_left[..., half:] = (
        behind[..., half:].astype(jnp.float32) + got_hi[...].astype(jnp.float32)
    ).astype(to_left.dtype)
    copy = remote(to_left, from_right, send_sem.at[3], recv_sem.at[3], left)
    copy.start()
    sent.append(copy)
    remote(to_right, from_left, send_sem.at[2], recv_sem.at[2], left).wait_recv()
    remote(to_left, from_right, send_sem.at[3], recv_sem.at[3], right).wait_recv()
    return (
        chunk(me)[...].astype(jnp.float32)
        + from_left[...].astype(jnp.float32)
        + from_right[...].astype(jnp.float32)
    )


def scatter_kernel(with_core, part_ref, out_ref, got_c, sum_c, x_bufs, sum_x, z_bufs, send_sem, recv_sem):
    c = lax.axis_index("core")
    _, _, z_right, z_left = ring_peers("zh")
    _, _, x_right, x_left = ring_peers("x")
    _, _, sibling, _ = ring_peers("core")
    barrier = pltpu.get_barrier_semaphore()
    peers = ((sibling,) if with_core else ()) + (x_right, x_left, z_right, z_left)
    for peer in peers:
        pl.semaphore_signal(barrier, 1, device_id=peer, device_id_type=pl.DeviceIdType.MESH)
    pl.semaphore_wait(barrier, len(peers))
    sent = []
    if with_core:
        copy = remote(part_ref.at[1 - c], got_c, send_sem.at[0], recv_sem.at[0], sibling)
        copy.start()
        sent.append(copy)
        copy.wait_recv()
        sum_c[...] = (
            part_ref[c].astype(jnp.float32) + got_c[...].astype(jnp.float32)
        ).astype(sum_c.dtype)
    else:
        sum_c = part_ref
    x_bufs = [x_bufs.at[0, 0], x_bufs.at[0, 1]] + [x_bufs.at[1, k] for k in range(4)]
    x_bufs = [x_bufs[0].at[..., pl.ds(0, x_bufs[0].shape[-1] // 2)], x_bufs[1].at[..., pl.ds(0, x_bufs[1].shape[-1] // 2)]] + x_bufs[2:]
    total = ring_scatter(lambda i: sum_c.at[i], "x", x_bufs, send_sem.at[1:5], recv_sem.at[1:5], sent)
    sum_x[...] = total.astype(sum_x.dtype)
    z_bufs = [z_bufs.at[0, 0], z_bufs.at[0, 1]] + [z_bufs.at[1, k] for k in range(4)]
    z_bufs = [z_bufs[0].at[..., pl.ds(0, z_bufs[0].shape[-1] // 2)], z_bufs[1].at[..., pl.ds(0, z_bufs[1].shape[-1] // 2)]] + z_bufs[2:]
    out_ref[...] = ring_scatter(lambda i: sum_x.at[i], "zh", z_bufs, send_sem.at[5:9], recv_sem.at[5:9], sent)
    for copy in sent:
        copy.wait_send()


def scatter_rows(rows, with_core=True):
    nx, nz, nc = SIZE["x"], SIZE["zh"], SIZE["core"]
    halves_in = nc if with_core else 1
    blk = rows.shape[0] // (nx * nz * halves_in)
    tail = rows.shape[1:]
    part = rows.reshape(((nc,) if with_core else ()) + (nx, nz, blk) + tail)
    links = 9
    return pl.pallas_call(
        functools.partial(scatter_kernel, with_core),
        out_shape=jax.ShapeDtypeStruct((blk,) + tail, jnp.float32),
        in_specs=[pl.BlockSpec(memory_space=pltpu.VMEM)],
        out_specs=pl.BlockSpec(memory_space=pltpu.VMEM),
        scratch_shapes=[
            pltpu.VMEM((nx, nz, blk) + tail, rows.dtype),
            pltpu.VMEM((nx, nz, blk) + tail, rows.dtype),
            pltpu.VMEM((2, 4, nz, blk) + tail, rows.dtype),
            pltpu.VMEM((nz, blk) + tail, rows.dtype),
            pltpu.VMEM((2, 4, blk) + tail, rows.dtype),
            pltpu.SemaphoreType.DMA((links,)),
            pltpu.SemaphoreType.DMA((links,)),
        ],
        compiler_params=pltpu.CompilerParams(
            collective_id=1 if with_core else 2, has_side_effects=True
        ),
    )(part)


def to_request_order(values):
    nx, nz, nc = SIZE["x"], SIZE["zh"], SIZE["core"]
    blk = TOKENS // (nx * nz * nc)
    tail = values.shape[1:]
    values = values.reshape((nc, nx, nz, blk) + tail)
    values = jnp.moveaxis(values, 0, 2)
    return values.reshape((TOKENS,) + tail)


def from_request_order(values):
    nx, nz, nc = SIZE["x"], SIZE["zh"], SIZE["core"]
    blk = TOKENS // (nx * nz * nc)
    tail = values.shape[1:]
    values = values.reshape((nx, nz, nc, blk) + tail)
    values = jnp.moveaxis(values, 2, 0)
    return values.reshape((TOKENS,) + tail)


def local(
    hidden_in,
    attn_gain,
    w_query,
    w_key,
    w_value,
    w_out,
    cache_k,
    cache_v,
    cache_len,
    ffn_gain,
    router,
    routes,
    w_gate_up,
    w_down,
):
    width = hidden_in.shape[1]
    head_dev = cache_k.shape[1]
    n_experts = w_gate_up.shape[0]
    whole_in = gather_rows(hidden_in)
    normed = rms_scale(whole_in, attn_gain)
    positions = (cache_len[:, None] + jnp.arange(NEW, dtype=jnp.int32)[None, :]).reshape(-1)
    positions = from_request_order(positions)

    def project(weight):
        return jnp.dot(normed, weight, preferred_element_type=jnp.float32).reshape(
            TOKENS, head_dev, HDIM
        )

    def by_request(values):
        values = to_request_order(values)
        return values.reshape(REQS, NEW, head_dev, HDIM).transpose(0, 2, 1, 3)

    query = rotate(project(w_query), positions).astype(jnp.bfloat16)
    key_new = rotate(project(w_key), positions).astype(jnp.bfloat16)
    value_new = project(w_value).astype(jnp.bfloat16)
    heads_out = attend(
        by_request(query), by_request(key_new), by_request(value_new), cache_k, cache_v, cache_len
    )
    heads_flat = from_request_order(heads_out.transpose(0, 2, 1, 3).reshape(TOKENS, head_dev * HDIM))
    core = lax.axis_index("core")
    by_core = heads_flat.reshape(SIZE["core"], TOKENS // SIZE["core"], head_dev * HDIM)
    mine = lax.dynamic_index_in_dim(by_core, core, axis=0, keepdims=False)
    theirs = lax.dynamic_index_in_dim(by_core, 1 - core, axis=0, keepdims=False)
    swap = [(0, 1), (1, 0)]
    from_sibling = lax.ppermute(theirs, "core", swap)
    w_out_sibling = lax.ppermute(w_out, "core", swap)
    attn = scatter_rows(
        (
            jnp.dot(mine, w_out, preferred_element_type=jnp.float32)
            + jnp.dot(from_sibling, w_out_sibling, preferred_element_type=jnp.float32)
        ).astype(jnp.bfloat16),
        with_core=False,
    )
    middle = (hidden_in.astype(jnp.float32) + attn).astype(jnp.bfloat16)
    normed2 = gather_rows(rms_scale(middle, ffn_gain))
    logits = jnp.dot(normed2, router, preferred_element_type=jnp.float32)
    routes = from_request_order(routes)
    pair_weights = route_weights(logits, routes)
    running = jnp.zeros((TOKENS, width), jnp.float32)
    for expert in range(n_experts):
        dense_weight = jnp.sum(jnp.where(routes == expert, pair_weights, 0.0), axis=1)
        running = (
            running
            + expert_apply(normed2, w_gate_up[expert], w_down[expert]) * dense_weight[:, None]
        )
    expert_out = scatter_rows(running.astype(jnp.bfloat16))
    return (middle.astype(jnp.float32) + expert_out).astype(jnp.bfloat16)


def solution(mesh):
    dp = mesh.shape["dp"]
    fine = Mesh(mesh.devices.reshape((dp,) + tuple(n for _, n in SUB)), ("dp",) + TENSOR)
    rows = ("dp",) + TENSOR
    in_specs = (
        P(rows, None),
        P(),
        P(None, TENSOR),
        P(None, TENSOR),
        P(None, TENSOR),
        P(TENSOR, None),
        P("dp", TENSOR, None, None),
        P("dp", TENSOR, None, None),
        P("dp"),
        P(),
        P(),
        P("dp", None),
        P(None, None, None, TENSOR),
        P(None, TENSOR, None),
    )
    out_specs = P(rows, None)
    return jax.shard_map(local, mesh=fine, in_specs=in_specs, out_specs=out_specs, check_vma=False)
```

```python
import functools

import jax
import jax.numpy as jnp
from jax import lax
from jax.experimental import pallas as pl
from jax.experimental.pallas import tpu as pltpu
from jax.sharding import Mesh
from jax.sharding import PartitionSpec as P

HDIM = 64
REQS = 8
NEW = 96
TOKENS = 768

SUB = (("x", 4), ("zh", 4), ("core", 2))
TENSOR = tuple(name for name, _ in SUB)
SIZE = dict(SUB)

eps = 1e-05


def rms_scale(rows_in, gain):
    values = rows_in.astype(jnp.float32)
    mean_square = jnp.mean(values * values, axis=-1, keepdims=True)
    return (values * lax.rsqrt(mean_square + eps) * gain.astype(jnp.float32)).astype(jnp.bfloat16)


def rotate(values, positions):
    half_dim = values.shape[-1] // 2
    inverse = 10000.0 ** (-2.0 * jnp.arange(half_dim, dtype=jnp.float32) / values.shape[-1])
    angles = positions.astype(jnp.float32)[:, None] * inverse[None, :]
    cosine = jnp.cos(angles)[:, None, :]
    sine_part = jnp.sin(angles)[:, None, :]
    front = values[..., :half_dim]
    back = values[..., half_dim:]
    return jnp.concatenate(
        [front * cosine - back * sine_part, back * cosine + front * sine_part], axis=-1
    )


def route_weights(logits, routes):
    expert_iota = jnp.arange(logits.shape[1], dtype=jnp.int32)[None, :]
    first_logit = jnp.sum(jnp.where(routes[:, 0:1] == expert_iota, logits, 0.0), axis=1)
    second_logit = jnp.sum(jnp.where(routes[:, 1:2] == expert_iota, logits, 0.0), axis=1)
    first_weight = 1.0 / (1.0 + jnp.exp(second_logit - first_logit))
    second_weight = 1.0 / (1.0 + jnp.exp(first_logit - second_logit))
    return jnp.stack([first_weight, second_weight], axis=1)


def expert_apply(rows_in, gate_up, down_part):
    both = jnp.einsum("td,kdf->ktf", rows_in, gate_up, preferred_element_type=jnp.float32)
    inner = (jax.nn.silu(both[0]) * both[1]).astype(jnp.bfloat16)
    return jnp.dot(inner, down_part, preferred_element_type=jnp.float32)


def attend(query, key_new, value_new, cache_k, cache_v, cache_len):
    cached_scores = (
        jnp.einsum("rhqd,rhkd->rhqk", query, cache_k, preferred_element_type=jnp.float32) * 0.125
    )
    fresh_scores = (
        jnp.einsum("rhqd,rhkd->rhqk", query, key_new, preferred_element_type=jnp.float32) * 0.125
    )
    key_pos = jnp.arange(cache_k.shape[2], dtype=jnp.int32)
    cached_mask = key_pos[None, None, None, :] < cache_len[:, None, None, None]
    new_pos = jnp.arange(query.shape[2], dtype=jnp.int32)
    fresh_mask = (new_pos[:, None] >= new_pos[None, :])[None, None]
    cached_scores = jnp.where(cached_mask, cached_scores, -1e30)
    fresh_scores = jnp.where(fresh_mask, fresh_scores, -1e30)
    peak = jnp.maximum(
        jnp.max(cached_scores, axis=-1, keepdims=True),
        jnp.max(fresh_scores, axis=-1, keepdims=True),
    )
    cached_expo = jnp.exp(cached_scores - peak)
    fresh_expo = jnp.exp(fresh_scores - peak)
    denominator = jnp.sum(cached_expo, axis=-1, keepdims=True) + jnp.sum(
        fresh_expo, axis=-1, keepdims=True
    )
    mixed = jnp.einsum(
        "rhqk,rhkd->rhqd",
        cached_expo.astype(jnp.bfloat16),
        cache_v,
        preferred_element_type=jnp.float32,
    )
    mixed = mixed + jnp.einsum(
        "rhqk,rhkd->rhqd",
        fresh_expo.astype(jnp.bfloat16),
        value_new,
        preferred_element_type=jnp.float32,
    )
    return (mixed / denominator).astype(jnp.bfloat16)


def shifts(axis, step):
    n = SIZE[axis]
    return [(i, (i + step) % n) for i in range(n)]


def gather_stage(rows, axis):
    n = SIZE[axis]
    me = lax.axis_index(axis)
    blk = rows.shape[0]
    out = jnp.zeros((n * blk,) + rows.shape[1:], rows.dtype)
    out = lax.dynamic_update_slice_in_dim(out, rows, me * blk, axis=0)
    for step in range(1, n):
        got = lax.ppermute(rows, axis, shifts(axis, step))
        out = lax.dynamic_update_slice_in_dim(out, got, ((me - step) % n) * blk, axis=0)
    return out


def scatter_stage(rows, axis):
    n = SIZE[axis]
    me = lax.axis_index(axis)
    chunks = rows.reshape((n, rows.shape[0] // n) + rows.shape[1:])
    total = lax.dynamic_index_in_dim(chunks, me, axis=0, keepdims=False).astype(jnp.float32)
    for step in range(1, n):
        send = lax.dynamic_index_in_dim(chunks, (me + step) % n, axis=0, keepdims=False)
        got = lax.ppermute(send.astype(jnp.bfloat16), axis, shifts(axis, step))
        total = total + got.astype(jnp.float32)
    return total


def ring_peers(axis):
    here = {name: lax.axis_index(name) for name in ("dp",) + TENSOR}
    n = SIZE[axis]
    me = here[axis]

    def at(member):
        return tuple(member if name == axis else here[name] for name in ("dp",) + TENSOR)

    return me, n, at((me + 1) % n), at((me + n - 1) % n)


def halves(ref):
    half = ref.shape[-1] // 2
    return ref.at[..., pl.ds(0, half)], ref.at[..., pl.ds(half, half)]


def remote(src, dst, send_sem, recv_sem, peer):
    return pltpu.make_async_remote_copy(
        src_ref=src,
        dst_ref=dst,
        send_sem=send_sem,
        recv_sem=recv_sem,
        device_id=peer,
        device_id_type=pl.DeviceIdType.MESH,
    )


def ring_gather(slot, first, axis, send_sem, recv_sem, sent):
    me, n, right, left = ring_peers(axis)
    opposite = (me + 2) % n
    for k, peer in ((0, right), (1, left)):
        copy = remote(first, slot(me), send_sem.at[k], recv_sem.at[k], peer)
        copy.start()
        sent.append(copy)
    remote(first, slot((me + n - 1) % n), send_sem.at[0], recv_sem.at[0], left).wait_recv()
    copy = remote(
        halves(slot((me + n - 1) % n))[0], halves(slot((me + n - 1) % n))[0],
        send_sem.at[2], recv_sem.at[2], right,
    )
    copy.start()
    sent.append(copy)
    remote(first, slot((me + 1) % n), send_sem.at[1], recv_sem.at[1], right).wait_recv()
    copy = remote(
        halves(slot((me + 1) % n))[1], halves(slot((me + 1) % n))[1],
        send_sem.at[3], recv_sem.at[3], left,
    )
    copy.start()
    sent.append(copy)
    lo, hi = halves(slot(opposite))
    remote(lo, lo, send_sem.at[2], recv_sem.at[2], left).wait_recv()
    remote(hi, hi, send_sem.at[3], recv_sem.at[3], right).wait_recv()


def gather_kernel(own_ref, out_ref, send_sem, recv_sem, local_sem):
    x = lax.axis_index("x")
    z = lax.axis_index("zh")
    c = lax.axis_index("core")
    _, _, z_right, z_left = ring_peers("zh")
    _, _, x_right, x_left = ring_peers("x")
    _, _, sibling, _ = ring_peers("core")
    barrier = pltpu.get_barrier_semaphore()
    for peer in (z_right, z_left, x_right, x_left, sibling):
        pl.semaphore_signal(barrier, 1, device_id=peer, device_id_type=pl.DeviceIdType.MESH)
    pl.semaphore_wait(barrier, 5)
    local = pltpu.make_async_copy(own_ref, out_ref.at[c, x, z], local_sem.at[0])
    local.start()
    sent = []
    ring_gather(lambda i: out_ref.at[c, x, i], own_ref, "zh", send_sem.at[0:4], recv_sem.at[0:4], sent)
    local.wait()
    ring_gather(lambda i: out_ref.at[c, i], out_ref.at[c, x], "x", send_sem.at[4:8], recv_sem.at[4:8], sent)
    copy = remote(out_ref.at[c], out_ref.at[c], send_sem.at[8], recv_sem.at[8], sibling)
    copy.start()
    sent.append(copy)
    remote(out_ref.at[c], out_ref.at[1 - c], send_sem.at[8], recv_sem.at[8], sibling).wait_recv()
    for copy in sent:
        copy.wait_send()


def gather_rows(rows):
    nx, nz, nc = SIZE["x"], SIZE["zh"], SIZE["core"]
    links = 9
    out = pl.pallas_call(
        gather_kernel,
        out_shape=jax.ShapeDtypeStruct((nc, nx, nz) + rows.shape, rows.dtype),
        in_specs=[pl.BlockSpec(memory_space=pltpu.VMEM)],
        out_specs=pl.BlockSpec(memory_space=pltpu.VMEM),
        scratch_shapes=[
            pltpu.SemaphoreType.DMA((links,)),
            pltpu.SemaphoreType.DMA((links,)),
            pltpu.SemaphoreType.DMA((1,)),
        ],
        compiler_params=pltpu.CompilerParams(collective_id=0, has_side_effects=True),
    )(rows)
    return out.reshape((nc * nx * nz * rows.shape[0],) + rows.shape[1:])


def ring_scatter(chunk, axis, buffers, send_sem, recv_sem, sent):
    me, n, right, left = ring_peers(axis)
    got_lo, got_hi, to_right, to_left, from_left, from_right = buffers
    lo, hi = halves(chunk((me + 2) % n))
    for k, src, dst, peer in ((0, lo, got_lo, right), (1, hi, got_hi, left)):
        copy = remote(src, dst, send_sem.at[k], recv_sem.at[k], peer)
        copy.start()
        sent.append(copy)
    half = to_right.shape[-1] // 2
    remote(lo, got_lo, send_sem.at[0], recv_sem.at[0], left).wait_recv()
    ahead = chunk((me + 1) % n)
    to_right[..., :half] = (
        ahead[..., :half].astype(jnp.float32) + got_lo[...].astype(jnp.float32)
    ).astype(to_right.dtype)
    to_right[..., half:] = ahead[..., half:]
    copy = remote(to_right, from_left, send_sem.at[2], recv_sem.at[2], right)
    copy.start()
    sent.append(copy)
    remote(hi, got_hi, send_sem.at[1], recv_sem.at[1], right).wait_recv()
    behind = chunk((me + n - 1) % n)
    to_left[..., :half] = behind[..., :half]
    to_left[..., half:] = (
        behind[..., half:].astype(jnp.float32) + got_hi[...].astype(jnp.float32)
    ).astype(to_left.dtype)
    copy = remote(to_left, from_right, send_sem.at[3], recv_sem.at[3], left)
    copy.start()
    sent.append(copy)
    remote(to_right, from_left, send_sem.at[2], recv_sem.at[2], left).wait_recv()
    remote(to_left, from_right, send_sem.at[3], recv_sem.at[3], right).wait_recv()
    return (
        chunk(me)[...].astype(jnp.float32)
        + from_left[...].astype(jnp.float32)
        + from_right[...].astype(jnp.float32)
    )


def scatter_kernel(with_core, part_ref, out_ref, got_c, sum_c, x_bufs, sum_x, z_bufs, send_sem, recv_sem):
    c = lax.axis_index("core")
    _, _, z_right, z_left = ring_peers("zh")
    _, _, x_right, x_left = ring_peers("x")
    _, _, sibling, _ = ring_peers("core")
    barrier = pltpu.get_barrier_semaphore()
    peers = ((sibling,) if with_core else ()) + (x_right, x_left, z_right, z_left)
    for peer in peers:
        pl.semaphore_signal(barrier, 1, device_id=peer, device_id_type=pl.DeviceIdType.MESH)
    pl.semaphore_wait(barrier, len(peers))
    sent = []
    if with_core:
        copy = remote(part_ref.at[1 - c], got_c, send_sem.at[0], recv_sem.at[0], sibling)
        copy.start()
        sent.append(copy)
        copy.wait_recv()
        sum_c[...] = (
            part_ref[c].astype(jnp.float32) + got_c[...].astype(jnp.float32)
        ).astype(sum_c.dtype)
    else:
        sum_c = part_ref
    x_bufs = [x_bufs.at[0, 0], x_bufs.at[0, 1]] + [x_bufs.at[1, k] for k in range(4)]
    x_bufs = [x_bufs[0].at[..., pl.ds(0, x_bufs[0].shape[-1] // 2)], x_bufs[1].at[..., pl.ds(0, x_bufs[1].shape[-1] // 2)]] + x_bufs[2:]
    total = ring_scatter(lambda i: sum_c.at[i], "x", x_bufs, send_sem.at[1:5], recv_sem.at[1:5], sent)
    sum_x[...] = total.astype(sum_x.dtype)
    z_bufs = [z_bufs.at[0, 0], z_bufs.at[0, 1]] + [z_bufs.at[1, k] for k in range(4)]
    z_bufs = [z_bufs[0].at[..., pl.ds(0, z_bufs[0].shape[-1] // 2)], z_bufs[1].at[..., pl.ds(0, z_bufs[1].shape[-1] // 2)]] + z_bufs[2:]
    out_ref[...] = ring_scatter(lambda i: sum_x.at[i], "zh", z_bufs, send_sem.at[5:9], recv_sem.at[5:9], sent)
    for copy in sent:
        copy.wait_send()


def scatter_rows(rows, with_core=True):
    nx, nz, nc = SIZE["x"], SIZE["zh"], SIZE["core"]
    halves_in = nc if with_core else 1
    blk = rows.shape[0] // (nx * nz * halves_in)
    tail = rows.shape[1:]
    part = rows.reshape(((nc,) if with_core else ()) + (nx, nz, blk) + tail)
    links = 9
    return pl.pallas_call(
        functools.partial(scatter_kernel, with_core),
        out_shape=jax.ShapeDtypeStruct((blk,) + tail, jnp.float32),
        in_specs=[pl.BlockSpec(memory_space=pltpu.VMEM)],
        out_specs=pl.BlockSpec(memory_space=pltpu.VMEM),
        scratch_shapes=[
            pltpu.VMEM((nx, nz, blk) + tail, rows.dtype),
            pltpu.VMEM((nx, nz, blk) + tail, rows.dtype),
            pltpu.VMEM((2, 4, nz, blk) + tail, rows.dtype),
            pltpu.VMEM((nz, blk) + tail, rows.dtype),
            pltpu.VMEM((2, 4, blk) + tail, rows.dtype),
            pltpu.SemaphoreType.DMA((links,)),
            pltpu.SemaphoreType.DMA((links,)),
        ],
        compiler_params=pltpu.CompilerParams(
            collective_id=1 if with_core else 2, has_side_effects=True
        ),
    )(part)


def to_request_order(values):
    nx, nz, nc = SIZE["x"], SIZE["zh"], SIZE["core"]
    blk = TOKENS // (nx * nz * nc)
    tail = values.shape[1:]
    values = values.reshape((nc, nx, nz, blk) + tail)
    values = jnp.moveaxis(values, 0, 2)
    return values.reshape((TOKENS,) + tail)


def from_request_order(values):
    nx, nz, nc = SIZE["x"], SIZE["zh"], SIZE["core"]
    blk = TOKENS // (nx * nz * nc)
    tail = values.shape[1:]
    values = values.reshape((nx, nz, nc, blk) + tail)
    values = jnp.moveaxis(values, 2, 0)
    return values.reshape((TOKENS,) + tail)


def local(
    hidden_in,
    attn_gain,
    w_query,
    w_key,
    w_value,
    w_out,
    cache_k,
    cache_v,
    cache_len,
    ffn_gain,
    router,
    routes,
    w_gate_up,
    w_down,
):
    width = hidden_in.shape[1]
    head_dev = cache_k.shape[1]
    n_experts = w_gate_up.shape[0]
    whole_in = gather_rows(hidden_in)
    normed = rms_scale(whole_in, attn_gain)
    w_down_later, _ = lax.optimization_barrier((w_down, whole_in))
    w_down_sibling = lax.ppermute(w_down_later, "core", [(0, 1), (1, 0)])
    positions = (cache_len[:, None] + jnp.arange(NEW, dtype=jnp.int32)[None, :]).reshape(-1)
    positions = from_request_order(positions)

    def project(weight):
        return jnp.dot(normed, weight, preferred_element_type=jnp.float32).reshape(
            TOKENS, head_dev, HDIM
        )

    def by_request(values):
        values = to_request_order(values)
        return values.reshape(REQS, NEW, head_dev, HDIM).transpose(0, 2, 1, 3)

    query = rotate(project(w_query), positions).astype(jnp.bfloat16)
    key_new = rotate(project(w_key), positions).astype(jnp.bfloat16)
    value_new = project(w_value).astype(jnp.bfloat16)
    heads_out = attend(
        by_request(query), by_request(key_new), by_request(value_new), cache_k, cache_v, cache_len
    )
    heads_flat = from_request_order(heads_out.transpose(0, 2, 1, 3).reshape(TOKENS, head_dev * HDIM))
    heads_flat, w_down_sibling = lax.optimization_barrier((heads_flat, w_down_sibling))
    core = lax.axis_index("core")
    by_core = heads_flat.reshape(SIZE["core"], TOKENS // SIZE["core"], head_dev * HDIM)
    mine = lax.dynamic_index_in_dim(by_core, core, axis=0, keepdims=False)
    theirs = lax.dynamic_index_in_dim(by_core, 1 - core, axis=0, keepdims=False)
    swap = [(0, 1), (1, 0)]
    from_sibling = lax.ppermute(theirs, "core", swap)
    w_out_sibling = lax.ppermute(w_out, "core", swap)
    attn = scatter_rows(
        (
            jnp.dot(mine, w_out, preferred_element_type=jnp.float32)
            + jnp.dot(from_sibling, w_out_sibling, preferred_element_type=jnp.float32)
        ).astype(jnp.bfloat16),
        with_core=False,
    )
    middle = (hidden_in.astype(jnp.float32) + attn).astype(jnp.bfloat16)
    normed2 = gather_rows(rms_scale(middle, ffn_gain))
    logits = jnp.dot(normed2, router, preferred_element_type=jnp.float32)
    routes = from_request_order(routes)
    pair_weights = route_weights(logits, routes)
    half = TOKENS // SIZE["core"]
    both = jnp.einsum("td,ekdf->ektf", normed2, w_gate_up, preferred_element_type=jnp.float32)
    inner = (jax.nn.silu(both[:, 0]) * both[:, 1]).astype(jnp.bfloat16)
    inner = inner.reshape(n_experts, SIZE["core"], half, -1)
    inner_mine = lax.dynamic_index_in_dim(inner, core, axis=1, keepdims=False)
    inner_theirs = lax.dynamic_index_in_dim(inner, 1 - core, axis=1, keepdims=False)
    inner_sibling = lax.ppermute(inner_theirs, "core", swap)
    running = jnp.zeros((half, width), jnp.float32)
    for expert in range(n_experts):
        dense_weight = jnp.sum(jnp.where(routes == expert, pair_weights, 0.0), axis=1)
        weight_mine = lax.dynamic_index_in_dim(
            dense_weight.reshape(SIZE["core"], half), core, axis=0, keepdims=False
        )
        running = running + (
            jnp.dot(inner_mine[expert], w_down[expert], preferred_element_type=jnp.float32)
            + jnp.dot(
                inner_sibling[expert], w_down_sibling[expert], preferred_element_type=jnp.float32
            )
        ) * weight_mine[:, None]
    expert_out = scatter_rows(running.astype(jnp.bfloat16), with_core=False)
    return (middle.astype(jnp.float32) + expert_out).astype(jnp.bfloat16)


def solution(mesh):
    dp = mesh.shape["dp"]
    fine = Mesh(mesh.devices.reshape((dp,) + tuple(n for _, n in SUB)), ("dp",) + TENSOR)
    rows = ("dp",) + TENSOR
    in_specs = (
        P(rows, None),
        P(),
        P(None, TENSOR),
        P(None, TENSOR),
        P(None, TENSOR),
        P(TENSOR, None),
        P("dp", TENSOR, None, None),
        P("dp", TENSOR, None, None),
        P("dp"),
        P(),
        P(),
        P("dp", None),
        P(None, None, None, TENSOR),
        P(None, TENSOR, None),
    )
    out_specs = P(rows, None)
    return jax.shard_map(local, mesh=fine, in_specs=in_specs, out_specs=out_specs, check_vma=False)
```

```python
import functools

import jax
import jax.numpy as jnp
from jax import lax
from jax.experimental import pallas as pl
from jax.experimental.pallas import tpu as pltpu
from jax.sharding import Mesh
from jax.sharding import PartitionSpec as P

HDIM = 64
REQS = 8
NEW = 96
TOKENS = 768

SUB = (("x", 4), ("zh", 4), ("core", 2))
TENSOR = tuple(name for name, _ in SUB)
SIZE = dict(SUB)

eps = 1e-05


def rms_scale(rows_in, gain):
    values = rows_in.astype(jnp.float32)
    mean_square = jnp.mean(values * values, axis=-1, keepdims=True)
    return (values * lax.rsqrt(mean_square + eps) * gain.astype(jnp.float32)).astype(jnp.bfloat16)


def rotate(values, positions):
    half_dim = values.shape[-1] // 2
    inverse = 10000.0 ** (-2.0 * jnp.arange(half_dim, dtype=jnp.float32) / values.shape[-1])
    angles = positions.astype(jnp.float32)[:, None] * inverse[None, :]
    cosine = jnp.cos(angles)[:, None, :]
    sine_part = jnp.sin(angles)[:, None, :]
    front = values[..., :half_dim]
    back = values[..., half_dim:]
    return jnp.concatenate(
        [front * cosine - back * sine_part, back * cosine + front * sine_part], axis=-1
    )


def route_weights(logits, routes):
    expert_iota = jnp.arange(logits.shape[1], dtype=jnp.int32)[None, :]
    first_logit = jnp.sum(jnp.where(routes[:, 0:1] == expert_iota, logits, 0.0), axis=1)
    second_logit = jnp.sum(jnp.where(routes[:, 1:2] == expert_iota, logits, 0.0), axis=1)
    first_weight = 1.0 / (1.0 + jnp.exp(second_logit - first_logit))
    second_weight = 1.0 / (1.0 + jnp.exp(first_logit - second_logit))
    return jnp.stack([first_weight, second_weight], axis=1)


def expert_apply(rows_in, gate_up, down_part):
    both = jnp.einsum("td,kdf->ktf", rows_in, gate_up, preferred_element_type=jnp.float32)
    inner = (jax.nn.silu(both[0]) * both[1]).astype(jnp.bfloat16)
    return jnp.dot(inner, down_part, preferred_element_type=jnp.float32)


def attend(query, key_new, value_new, cache_k, cache_v, cache_len):
    cached_scores = (
        jnp.einsum("rhqd,rhkd->rhqk", query, cache_k, preferred_element_type=jnp.float32) * 0.125
    )
    fresh_scores = (
        jnp.einsum("rhqd,rhkd->rhqk", query, key_new, preferred_element_type=jnp.float32) * 0.125
    )
    key_pos = jnp.arange(cache_k.shape[2], dtype=jnp.int32)
    cached_mask = key_pos[None, None, None, :] < cache_len[:, None, None, None]
    new_pos = jnp.arange(query.shape[2], dtype=jnp.int32)
    fresh_mask = (new_pos[:, None] >= new_pos[None, :])[None, None]
    cached_scores = jnp.where(cached_mask, cached_scores, -1e30)
    fresh_scores = jnp.where(fresh_mask, fresh_scores, -1e30)
    peak = jnp.maximum(
        jnp.max(cached_scores, axis=-1, keepdims=True),
        jnp.max(fresh_scores, axis=-1, keepdims=True),
    )
    cached_expo = jnp.exp(cached_scores - peak)
    fresh_expo = jnp.exp(fresh_scores - peak)
    denominator = jnp.sum(cached_expo, axis=-1, keepdims=True) + jnp.sum(
        fresh_expo, axis=-1, keepdims=True
    )
    mixed = jnp.einsum(
        "rhqk,rhkd->rhqd",
        cached_expo.astype(jnp.bfloat16),
        cache_v,
        preferred_element_type=jnp.float32,
    )
    mixed = mixed + jnp.einsum(
        "rhqk,rhkd->rhqd",
        fresh_expo.astype(jnp.bfloat16),
        value_new,
        preferred_element_type=jnp.float32,
    )
    return (mixed / denominator).astype(jnp.bfloat16)


def shifts(axis, step):
    n = SIZE[axis]
    return [(i, (i + step) % n) for i in range(n)]


def gather_stage(rows, axis):
    n = SIZE[axis]
    me = lax.axis_index(axis)
    blk = rows.shape[0]
    out = jnp.zeros((n * blk,) + rows.shape[1:], rows.dtype)
    out = lax.dynamic_update_slice_in_dim(out, rows, me * blk, axis=0)
    for step in range(1, n):
        got = lax.ppermute(rows, axis, shifts(axis, step))
        out = lax.dynamic_update_slice_in_dim(out, got, ((me - step) % n) * blk, axis=0)
    return out


def scatter_stage(rows, axis):
    n = SIZE[axis]
    me = lax.axis_index(axis)
    chunks = rows.reshape((n, rows.shape[0] // n) + rows.shape[1:])
    total = lax.dynamic_index_in_dim(chunks, me, axis=0, keepdims=False).astype(jnp.float32)
    for step in range(1, n):
        send = lax.dynamic_index_in_dim(chunks, (me + step) % n, axis=0, keepdims=False)
        got = lax.ppermute(send.astype(jnp.bfloat16), axis, shifts(axis, step))
        total = total + got.astype(jnp.float32)
    return total


def ring_peers(axis):
    here = {name: lax.axis_index(name) for name in ("dp",) + TENSOR}
    n = SIZE[axis]
    me = here[axis]

    def at(member):
        return tuple(member if name == axis else here[name] for name in ("dp",) + TENSOR)

    return me, n, at((me + 1) % n), at((me + n - 1) % n)


def halves(ref):
    half = ref.shape[-1] // 2
    return ref.at[..., pl.ds(0, half)], ref.at[..., pl.ds(half, half)]


def remote(src, dst, send_sem, recv_sem, peer):
    return pltpu.make_async_remote_copy(
        src_ref=src,
        dst_ref=dst,
        send_sem=send_sem,
        recv_sem=recv_sem,
        device_id=peer,
        device_id_type=pl.DeviceIdType.MESH,
    )


def ring_gather(slot, first, axis, send_sem, recv_sem, sent):
    me, n, right, left = ring_peers(axis)
    opposite = (me + 2) % n
    for k, peer in ((0, right), (1, left)):
        copy = remote(first, slot(me), send_sem.at[k], recv_sem.at[k], peer)
        copy.start()
        sent.append(copy)
    remote(first, slot((me + n - 1) % n), send_sem.at[0], recv_sem.at[0], left).wait_recv()
    copy = remote(
        halves(slot((me + n - 1) % n))[0], halves(slot((me + n - 1) % n))[0],
        send_sem.at[2], recv_sem.at[2], right,
    )
    copy.start()
    sent.append(copy)
    remote(first, slot((me + 1) % n), send_sem.at[1], recv_sem.at[1], right).wait_recv()
    copy = remote(
        halves(slot((me + 1) % n))[1], halves(slot((me + 1) % n))[1],
        send_sem.at[3], recv_sem.at[3], left,
    )
    copy.start()
    sent.append(copy)
    lo, hi = halves(slot(opposite))
    remote(lo, lo, send_sem.at[2], recv_sem.at[2], left).wait_recv()
    remote(hi, hi, send_sem.at[3], recv_sem.at[3], right).wait_recv()


def gather_kernel(own_ref, out_ref, send_sem, recv_sem, local_sem):
    x = lax.axis_index("x")
    z = lax.axis_index("zh")
    c = lax.axis_index("core")
    _, _, z_right, z_left = ring_peers("zh")
    _, _, x_right, x_left = ring_peers("x")
    _, _, sibling, _ = ring_peers("core")
    barrier = pltpu.get_barrier_semaphore()
    for peer in (z_right, z_left, x_right, x_left, sibling):
        pl.semaphore_signal(barrier, 1, device_id=peer, device_id_type=pl.DeviceIdType.MESH)
    pl.semaphore_wait(barrier, 5)
    local = pltpu.make_async_copy(own_ref, out_ref.at[c, x, z], local_sem.at[0])
    local.start()
    sent = []
    ring_gather(lambda i: out_ref.at[c, x, i], own_ref, "zh", send_sem.at[0:4], recv_sem.at[0:4], sent)
    local.wait()
    ring_gather(lambda i: out_ref.at[c, i], out_ref.at[c, x], "x", send_sem.at[4:8], recv_sem.at[4:8], sent)
    copy = remote(out_ref.at[c], out_ref.at[c], send_sem.at[8], recv_sem.at[8], sibling)
    copy.start()
    sent.append(copy)
    remote(out_ref.at[c], out_ref.at[1 - c], send_sem.at[8], recv_sem.at[8], sibling).wait_recv()
    for copy in sent:
        copy.wait_send()


def gather_rows(rows):
    nx, nz, nc = SIZE["x"], SIZE["zh"], SIZE["core"]
    links = 9
    out = pl.pallas_call(
        gather_kernel,
        out_shape=jax.ShapeDtypeStruct((nc, nx, nz) + rows.shape, rows.dtype),
        in_specs=[pl.BlockSpec(memory_space=pltpu.VMEM)],
        out_specs=pl.BlockSpec(memory_space=pltpu.VMEM),
        scratch_shapes=[
            pltpu.SemaphoreType.DMA((links,)),
            pltpu.SemaphoreType.DMA((links,)),
            pltpu.SemaphoreType.DMA((1,)),
        ],
        compiler_params=pltpu.CompilerParams(collective_id=0, has_side_effects=True),
    )(rows)
    return out.reshape((nc * nx * nz * rows.shape[0],) + rows.shape[1:])


def ring_scatter(chunk, axis, buffers, send_sem, recv_sem, sent):
    me, n, right, left = ring_peers(axis)
    got_lo, got_hi, to_right, to_left, from_left, from_right = buffers
    lo, hi = halves(chunk((me + 2) % n))
    for k, src, dst, peer in ((0, lo, got_lo, right), (1, hi, got_hi, left)):
        copy = remote(src, dst, send_sem.at[k], recv_sem.at[k], peer)
        copy.start()
        sent.append(copy)
    half = to_right.shape[-1] // 2
    remote(lo, got_lo, send_sem.at[0], recv_sem.at[0], left).wait_recv()
    ahead = chunk((me + 1) % n)
    to_right[..., :half] = (
        ahead[..., :half].astype(jnp.float32) + got_lo[...].astype(jnp.float32)
    ).astype(to_right.dtype)
    to_right[..., half:] = ahead[..., half:]
    copy = remote(to_right, from_left, send_sem.at[2], recv_sem.at[2], right)
    copy.start()
    sent.append(copy)
    remote(hi, got_hi, send_sem.at[1], recv_sem.at[1], right).wait_recv()
    behind = chunk((me + n - 1) % n)
    to_left[..., :half] = behind[..., :half]
    to_left[..., half:] = (
        behind[..., half:].astype(jnp.float32) + got_hi[...].astype(jnp.float32)
    ).astype(to_left.dtype)
    copy = remote(to_left, from_right, send_sem.at[3], recv_sem.at[3], left)
    copy.start()
    sent.append(copy)
    remote(to_right, from_left, send_sem.at[2], recv_sem.at[2], left).wait_recv()
    remote(to_left, from_right, send_sem.at[3], recv_sem.at[3], right).wait_recv()
    return (
        chunk(me)[...].astype(jnp.float32)
        + from_left[...].astype(jnp.float32)
        + from_right[...].astype(jnp.float32)
    )


def scatter_kernel(with_core, part_ref, out_ref, got_c, sum_c, x_bufs, sum_x, z_bufs, send_sem, recv_sem):
    c = lax.axis_index("core")
    _, _, z_right, z_left = ring_peers("zh")
    _, _, x_right, x_left = ring_peers("x")
    _, _, sibling, _ = ring_peers("core")
    barrier = pltpu.get_barrier_semaphore()
    peers = ((sibling,) if with_core else ()) + (x_right, x_left, z_right, z_left)
    for peer in peers:
        pl.semaphore_signal(barrier, 1, device_id=peer, device_id_type=pl.DeviceIdType.MESH)
    pl.semaphore_wait(barrier, len(peers))
    sent = []
    if with_core:
        copy = remote(part_ref.at[1 - c], got_c, send_sem.at[0], recv_sem.at[0], sibling)
        copy.start()
        sent.append(copy)
        copy.wait_recv()
        sum_c[...] = (
            part_ref[c].astype(jnp.float32) + got_c[...].astype(jnp.float32)
        ).astype(sum_c.dtype)
    else:
        sum_c = part_ref
    x_bufs = [x_bufs.at[0, 0], x_bufs.at[0, 1]] + [x_bufs.at[1, k] for k in range(4)]
    x_bufs = [x_bufs[0].at[..., pl.ds(0, x_bufs[0].shape[-1] // 2)], x_bufs[1].at[..., pl.ds(0, x_bufs[1].shape[-1] // 2)]] + x_bufs[2:]
    total = ring_scatter(lambda i: sum_c.at[i], "x", x_bufs, send_sem.at[1:5], recv_sem.at[1:5], sent)
    sum_x[...] = total.astype(sum_x.dtype)
    z_bufs = [z_bufs.at[0, 0], z_bufs.at[0, 1]] + [z_bufs.at[1, k] for k in range(4)]
    z_bufs = [z_bufs[0].at[..., pl.ds(0, z_bufs[0].shape[-1] // 2)], z_bufs[1].at[..., pl.ds(0, z_bufs[1].shape[-1] // 2)]] + z_bufs[2:]
    out_ref[...] = ring_scatter(lambda i: sum_x.at[i], "zh", z_bufs, send_sem.at[5:9], recv_sem.at[5:9], sent)
    for copy in sent:
        copy.wait_send()


def scatter_rows(rows, with_core=True):
    nx, nz, nc = SIZE["x"], SIZE["zh"], SIZE["core"]
    halves_in = nc if with_core else 1
    blk = rows.shape[0] // (nx * nz * halves_in)
    tail = rows.shape[1:]
    part = rows.reshape(((nc,) if with_core else ()) + (nx, nz, blk) + tail)
    links = 9
    return pl.pallas_call(
        functools.partial(scatter_kernel, with_core),
        out_shape=jax.ShapeDtypeStruct((blk,) + tail, jnp.float32),
        in_specs=[pl.BlockSpec(memory_space=pltpu.VMEM)],
        out_specs=pl.BlockSpec(memory_space=pltpu.VMEM),
        scratch_shapes=[
            pltpu.VMEM((nx, nz, blk) + tail, rows.dtype),
            pltpu.VMEM((nx, nz, blk) + tail, rows.dtype),
            pltpu.VMEM((2, 4, nz, blk) + tail, rows.dtype),
            pltpu.VMEM((nz, blk) + tail, rows.dtype),
            pltpu.VMEM((2, 4, blk) + tail, rows.dtype),
            pltpu.SemaphoreType.DMA((links,)),
            pltpu.SemaphoreType.DMA((links,)),
        ],
        compiler_params=pltpu.CompilerParams(
            collective_id=1 if with_core else 2, has_side_effects=True
        ),
    )(part)


def to_request_order(values):
    nx, nz, nc = SIZE["x"], SIZE["zh"], SIZE["core"]
    blk = TOKENS // (nx * nz * nc)
    tail = values.shape[1:]
    values = values.reshape((nc, nx, nz, blk) + tail)
    values = jnp.moveaxis(values, 0, 2)
    return values.reshape((TOKENS,) + tail)


def from_request_order(values):
    nx, nz, nc = SIZE["x"], SIZE["zh"], SIZE["core"]
    blk = TOKENS // (nx * nz * nc)
    tail = values.shape[1:]
    values = values.reshape((nx, nz, nc, blk) + tail)
    values = jnp.moveaxis(values, 2, 0)
    return values.reshape((TOKENS,) + tail)


def local(
    hidden_in,
    attn_gain,
    w_query,
    w_key,
    w_value,
    w_out,
    cache_k,
    cache_v,
    cache_len,
    ffn_gain,
    router,
    routes,
    w_gate_up,
    w_down,
):
    width = hidden_in.shape[1]
    head_dev = cache_k.shape[1]
    n_experts = w_gate_up.shape[0]
    whole_in = gather_rows(hidden_in)
    normed = rms_scale(whole_in, attn_gain)
    w_down_later, _ = lax.optimization_barrier((w_down, whole_in))
    w_down_sibling = lax.ppermute(w_down_later, "core", [(0, 1), (1, 0)])
    positions = (cache_len[:, None] + jnp.arange(NEW, dtype=jnp.int32)[None, :]).reshape(-1)
    positions = from_request_order(positions)

    def project(weight):
        return jnp.dot(normed, weight, preferred_element_type=jnp.float32).reshape(
            TOKENS, head_dev, HDIM
        )

    def by_request(values):
        values = to_request_order(values)
        return values.reshape(REQS, NEW, head_dev, HDIM).transpose(0, 2, 1, 3)

    query = rotate(project(w_query), positions).astype(jnp.bfloat16)
    key_new = rotate(project(w_key), positions).astype(jnp.bfloat16)
    value_new = project(w_value).astype(jnp.bfloat16)
    heads_out = attend(
        by_request(query), by_request(key_new), by_request(value_new), cache_k, cache_v, cache_len
    )
    heads_flat = from_request_order(heads_out.transpose(0, 2, 1, 3).reshape(TOKENS, head_dev * HDIM))
    heads_flat, w_down_sibling = lax.optimization_barrier((heads_flat, w_down_sibling))
    core = lax.axis_index("core")
    by_core = heads_flat.reshape(SIZE["core"], TOKENS // SIZE["core"], head_dev * HDIM)
    mine = lax.dynamic_index_in_dim(by_core, core, axis=0, keepdims=False)
    theirs = lax.dynamic_index_in_dim(by_core, 1 - core, axis=0, keepdims=False)
    swap = [(0, 1), (1, 0)]
    from_sibling = lax.ppermute(theirs, "core", swap)
    w_out_sibling = lax.ppermute(w_out, "core", swap)
    attn = scatter_rows(
        (
            jnp.dot(mine, w_out, preferred_element_type=jnp.float32)
            + jnp.dot(from_sibling, w_out_sibling, preferred_element_type=jnp.float32)
        ).astype(jnp.bfloat16),
        with_core=False,
    )
    middle = (hidden_in.astype(jnp.float32) + attn).astype(jnp.bfloat16)
    normed2 = gather_rows(rms_scale(middle, ffn_gain))
    logits = jnp.dot(normed2, router, preferred_element_type=jnp.float32)
    routes = from_request_order(routes)
    pair_weights = route_weights(logits, routes)
    half = TOKENS // SIZE["core"]
    both = jnp.einsum("td,ekdf->ektf", normed2, w_gate_up, preferred_element_type=jnp.float32)
    inner = (jax.nn.silu(both[:, 0]) * both[:, 1]).astype(jnp.bfloat16)
    inner = inner.reshape(n_experts, SIZE["core"], half, -1)
    inner_mine = lax.dynamic_index_in_dim(inner, core, axis=1, keepdims=False)
    inner_theirs = lax.dynamic_index_in_dim(inner, 1 - core, axis=1, keepdims=False)
    inner_sibling = lax.ppermute(inner_theirs, "core", swap)
    dense_weight = jnp.stack(
        [jnp.sum(jnp.where(routes == expert, pair_weights, 0.0), axis=1) for expert in range(n_experts)]
    )
    weight_mine = lax.dynamic_index_in_dim(
        dense_weight.reshape(n_experts, SIZE["core"], half), core, axis=1, keepdims=False
    )[..., None]
    scaled_mine = (inner_mine.astype(jnp.float32) * weight_mine).astype(jnp.bfloat16)
    scaled_sibling = (inner_sibling.astype(jnp.float32) * weight_mine).astype(jnp.bfloat16)
    running = jnp.einsum(
        "etf,efd->td", scaled_mine, w_down, preferred_element_type=jnp.float32
    ) + jnp.einsum("etf,efd->td", scaled_sibling, w_down_sibling, preferred_element_type=jnp.float32)
    expert_out = scatter_rows(running.astype(jnp.bfloat16), with_core=False)
    return (middle.astype(jnp.float32) + expert_out).astype(jnp.bfloat16)


def solution(mesh):
    dp = mesh.shape["dp"]
    fine = Mesh(mesh.devices.reshape((dp,) + tuple(n for _, n in SUB)), ("dp",) + TENSOR)
    rows = ("dp",) + TENSOR
    in_specs = (
        P(rows, None),
        P(),
        P(None, TENSOR),
        P(None, TENSOR),
        P(None, TENSOR),
        P(TENSOR, None),
        P("dp", TENSOR, None, None),
        P("dp", TENSOR, None, None),
        P("dp"),
        P(),
        P(),
        P("dp", None),
        P(None, None, None, TENSOR),
        P(None, TENSOR, None),
    )
    out_specs = P(rows, None)
    return jax.shard_map(local, mesh=fine, in_specs=in_specs, out_specs=out_specs, check_vma=False)
```

```python
import functools

import jax
import jax.numpy as jnp
from jax import lax
from jax.experimental import pallas as pl
from jax.experimental.pallas import tpu as pltpu
from jax.sharding import Mesh
from jax.sharding import PartitionSpec as P

HDIM = 64
REQS = 8
NEW = 96
TOKENS = 768

SUB = (("x", 4), ("zh", 4), ("core", 2))
TENSOR = tuple(name for name, _ in SUB)
SIZE = dict(SUB)

eps = 1e-05


def rms_scale(rows_in, gain):
    values = rows_in.astype(jnp.float32)
    mean_square = jnp.mean(values * values, axis=-1, keepdims=True)
    return (values * lax.rsqrt(mean_square + eps) * gain.astype(jnp.float32)).astype(jnp.bfloat16)


def rotate(values, positions):
    half_dim = values.shape[-1] // 2
    inverse = 10000.0 ** (-2.0 * jnp.arange(half_dim, dtype=jnp.float32) / values.shape[-1])
    angles = positions.astype(jnp.float32)[:, None] * inverse[None, :]
    cosine = jnp.cos(angles)[:, None, :]
    sine_part = jnp.sin(angles)[:, None, :]
    front = values[..., :half_dim]
    back = values[..., half_dim:]
    return jnp.concatenate(
        [front * cosine - back * sine_part, back * cosine + front * sine_part], axis=-1
    )


def route_weights(logits, routes):
    expert_iota = jnp.arange(logits.shape[1], dtype=jnp.int32)[None, :]
    first_logit = jnp.sum(jnp.where(routes[:, 0:1] == expert_iota, logits, 0.0), axis=1)
    second_logit = jnp.sum(jnp.where(routes[:, 1:2] == expert_iota, logits, 0.0), axis=1)
    first_weight = 1.0 / (1.0 + jnp.exp(second_logit - first_logit))
    second_weight = 1.0 / (1.0 + jnp.exp(first_logit - second_logit))
    return jnp.stack([first_weight, second_weight], axis=1)


def expert_apply(rows_in, gate_up, down_part):
    both = jnp.einsum("td,kdf->ktf", rows_in, gate_up, preferred_element_type=jnp.float32)
    inner = (jax.nn.silu(both[0]) * both[1]).astype(jnp.bfloat16)
    return jnp.dot(inner, down_part, preferred_element_type=jnp.float32)


def attend(query, key_new, value_new, cache_k, cache_v, cache_len):
    cached_scores = (
        jnp.einsum("rhqd,rhkd->rhqk", query, cache_k, preferred_element_type=jnp.float32) * 0.125
    )
    fresh_scores = (
        jnp.einsum("rhqd,rhkd->rhqk", query, key_new, preferred_element_type=jnp.float32) * 0.125
    )
    key_pos = jnp.arange(cache_k.shape[2], dtype=jnp.int32)
    cached_mask = key_pos[None, None, None, :] < cache_len[:, None, None, None]
    new_pos = jnp.arange(query.shape[2], dtype=jnp.int32)
    fresh_mask = (new_pos[:, None] >= new_pos[None, :])[None, None]
    cached_scores = jnp.where(cached_mask, cached_scores, -1e30)
    fresh_scores = jnp.where(fresh_mask, fresh_scores, -1e30)
    peak = jnp.maximum(
        jnp.max(cached_scores, axis=-1, keepdims=True),
        jnp.max(fresh_scores, axis=-1, keepdims=True),
    )
    cached_expo = jnp.exp(cached_scores - peak)
    fresh_expo = jnp.exp(fresh_scores - peak)
    denominator = jnp.sum(cached_expo, axis=-1, keepdims=True) + jnp.sum(
        fresh_expo, axis=-1, keepdims=True
    )
    mixed = jnp.einsum(
        "rhqk,rhkd->rhqd",
        cached_expo.astype(jnp.bfloat16),
        cache_v,
        preferred_element_type=jnp.float32,
    )
    mixed = mixed + jnp.einsum(
        "rhqk,rhkd->rhqd",
        fresh_expo.astype(jnp.bfloat16),
        value_new,
        preferred_element_type=jnp.float32,
    )
    return (mixed / denominator).astype(jnp.bfloat16)


def shifts(axis, step):
    n = SIZE[axis]
    return [(i, (i + step) % n) for i in range(n)]


def gather_stage(rows, axis):
    n = SIZE[axis]
    me = lax.axis_index(axis)
    blk = rows.shape[0]
    out = jnp.zeros((n * blk,) + rows.shape[1:], rows.dtype)
    out = lax.dynamic_update_slice_in_dim(out, rows, me * blk, axis=0)
    for step in range(1, n):
        got = lax.ppermute(rows, axis, shifts(axis, step))
        out = lax.dynamic_update_slice_in_dim(out, got, ((me - step) % n) * blk, axis=0)
    return out


def scatter_stage(rows, axis):
    n = SIZE[axis]
    me = lax.axis_index(axis)
    chunks = rows.reshape((n, rows.shape[0] // n) + rows.shape[1:])
    total = lax.dynamic_index_in_dim(chunks, me, axis=0, keepdims=False).astype(jnp.float32)
    for step in range(1, n):
        send = lax.dynamic_index_in_dim(chunks, (me + step) % n, axis=0, keepdims=False)
        got = lax.ppermute(send.astype(jnp.bfloat16), axis, shifts(axis, step))
        total = total + got.astype(jnp.float32)
    return total


def ring_peers(axis):
    here = {name: lax.axis_index(name) for name in ("dp",) + TENSOR}
    n = SIZE[axis]
    me = here[axis]

    def at(member):
        return tuple(member if name == axis else here[name] for name in ("dp",) + TENSOR)

    return me, n, at((me + 1) % n), at((me + n - 1) % n)


def halves(ref):
    half = ref.shape[-1] // 2
    return ref.at[..., pl.ds(0, half)], ref.at[..., pl.ds(half, half)]


def remote(src, dst, send_sem, recv_sem, peer):
    return pltpu.make_async_remote_copy(
        src_ref=src,
        dst_ref=dst,
        send_sem=send_sem,
        recv_sem=recv_sem,
        device_id=peer,
        device_id_type=pl.DeviceIdType.MESH,
    )


def ring_gather(slot, first, axis, send_sem, recv_sem, sent):
    me, n, right, left = ring_peers(axis)
    opposite = (me + 2) % n
    for k, peer in ((0, right), (1, left)):
        copy = remote(first, slot(me), send_sem.at[k], recv_sem.at[k], peer)
        copy.start()
        sent.append(copy)
    remote(first, slot((me + n - 1) % n), send_sem.at[0], recv_sem.at[0], left).wait_recv()
    copy = remote(
        halves(slot((me + n - 1) % n))[0], halves(slot((me + n - 1) % n))[0],
        send_sem.at[2], recv_sem.at[2], right,
    )
    copy.start()
    sent.append(copy)
    remote(first, slot((me + 1) % n), send_sem.at[1], recv_sem.at[1], right).wait_recv()
    copy = remote(
        halves(slot((me + 1) % n))[1], halves(slot((me + 1) % n))[1],
        send_sem.at[3], recv_sem.at[3], left,
    )
    copy.start()
    sent.append(copy)
    lo, hi = halves(slot(opposite))
    remote(lo, lo, send_sem.at[2], recv_sem.at[2], left).wait_recv()
    remote(hi, hi, send_sem.at[3], recv_sem.at[3], right).wait_recv()


def gather_kernel(own_ref, out_ref, send_sem, recv_sem, local_sem):
    x = lax.axis_index("x")
    z = lax.axis_index("zh")
    c = lax.axis_index("core")
    _, _, z_right, z_left = ring_peers("zh")
    _, _, x_right, x_left = ring_peers("x")
    _, _, sibling, _ = ring_peers("core")
    barrier = pltpu.get_barrier_semaphore()
    for peer in (z_right, z_left, x_right, x_left, sibling):
        pl.semaphore_signal(barrier, 1, device_id=peer, device_id_type=pl.DeviceIdType.MESH)
    pl.semaphore_wait(barrier, 5)
    local = pltpu.make_async_copy(own_ref, out_ref.at[c, x, z], local_sem.at[0])
    local.start()
    sent = []
    ring_gather(lambda i: out_ref.at[c, x, i], own_ref, "zh", send_sem.at[0:4], recv_sem.at[0:4], sent)
    local.wait()
    ring_gather(lambda i: out_ref.at[c, i], out_ref.at[c, x], "x", send_sem.at[4:8], recv_sem.at[4:8], sent)
    copy = remote(out_ref.at[c], out_ref.at[c], send_sem.at[8], recv_sem.at[8], sibling)
    copy.start()
    sent.append(copy)
    remote(out_ref.at[c], out_ref.at[1 - c], send_sem.at[8], recv_sem.at[8], sibling).wait_recv()
    for copy in sent:
        copy.wait_send()


def gather_rows(rows):
    nx, nz, nc = SIZE["x"], SIZE["zh"], SIZE["core"]
    links = 9
    out = pl.pallas_call(
        gather_kernel,
        out_shape=jax.ShapeDtypeStruct((nc, nx, nz) + rows.shape, rows.dtype),
        in_specs=[pl.BlockSpec(memory_space=pltpu.VMEM)],
        out_specs=pl.BlockSpec(memory_space=pltpu.VMEM),
        scratch_shapes=[
            pltpu.SemaphoreType.DMA((links,)),
            pltpu.SemaphoreType.DMA((links,)),
            pltpu.SemaphoreType.DMA((1,)),
        ],
        compiler_params=pltpu.CompilerParams(collective_id=0, has_side_effects=True),
    )(rows)
    return out.reshape((nc * nx * nz * rows.shape[0],) + rows.shape[1:])


def ring_scatter(chunk, axis, buffers, send_sem, recv_sem, sent):
    me, n, right, left = ring_peers(axis)
    got_lo, got_hi, to_right, to_left, from_left, from_right = buffers
    lo, hi = halves(chunk((me + 2) % n))
    for k, src, dst, peer in ((0, lo, got_lo, right), (1, hi, got_hi, left)):
        copy = remote(src, dst, send_sem.at[k], recv_sem.at[k], peer)
        copy.start()
        sent.append(copy)
    half = to_right.shape[-1] // 2
    remote(lo, got_lo, send_sem.at[0], recv_sem.at[0], left).wait_recv()
    ahead = chunk((me + 1) % n)
    to_right[..., :half] = (
        ahead[..., :half].astype(jnp.float32) + got_lo[...].astype(jnp.float32)
    ).astype(to_right.dtype)
    to_right[..., half:] = ahead[..., half:]
    copy = remote(to_right, from_left, send_sem.at[2], recv_sem.at[2], right)
    copy.start()
    sent.append(copy)
    remote(hi, got_hi, send_sem.at[1], recv_sem.at[1], right).wait_recv()
    behind = chunk((me + n - 1) % n)
    to_left[..., :half] = behind[..., :half]
    to_left[..., half:] = (
        behind[..., half:].astype(jnp.float32) + got_hi[...].astype(jnp.float32)
    ).astype(to_left.dtype)
    copy = remote(to_left, from_right, send_sem.at[3], recv_sem.at[3], left)
    copy.start()
    sent.append(copy)
    remote(to_right, from_left, send_sem.at[2], recv_sem.at[2], left).wait_recv()
    remote(to_left, from_right, send_sem.at[3], recv_sem.at[3], right).wait_recv()
    return (
        chunk(me)[...].astype(jnp.float32)
        + from_left[...].astype(jnp.float32)
        + from_right[...].astype(jnp.float32)
    )


def scatter_kernel(with_core, part_ref, out_ref, got_c, sum_c, x_bufs, sum_x, z_bufs, send_sem, recv_sem):
    c = lax.axis_index("core")
    _, _, z_right, z_left = ring_peers("zh")
    _, _, x_right, x_left = ring_peers("x")
    _, _, sibling, _ = ring_peers("core")
    barrier = pltpu.get_barrier_semaphore()
    peers = ((sibling,) if with_core else ()) + (x_right, x_left, z_right, z_left)
    for peer in peers:
        pl.semaphore_signal(barrier, 1, device_id=peer, device_id_type=pl.DeviceIdType.MESH)
    pl.semaphore_wait(barrier, len(peers))
    sent = []
    if with_core:
        copy = remote(part_ref.at[1 - c], got_c, send_sem.at[0], recv_sem.at[0], sibling)
        copy.start()
        sent.append(copy)
        copy.wait_recv()
        sum_c[...] = (
            part_ref[c].astype(jnp.float32) + got_c[...].astype(jnp.float32)
        ).astype(sum_c.dtype)
    else:
        sum_c = part_ref
    x_bufs = [x_bufs.at[0, 0], x_bufs.at[0, 1]] + [x_bufs.at[1, k] for k in range(4)]
    x_bufs = [x_bufs[0].at[..., pl.ds(0, x_bufs[0].shape[-1] // 2)], x_bufs[1].at[..., pl.ds(0, x_bufs[1].shape[-1] // 2)]] + x_bufs[2:]
    total = ring_scatter(lambda i: sum_c.at[i], "x", x_bufs, send_sem.at[1:5], recv_sem.at[1:5], sent)
    sum_x[...] = total.astype(sum_x.dtype)
    z_bufs = [z_bufs.at[0, 0], z_bufs.at[0, 1]] + [z_bufs.at[1, k] for k in range(4)]
    z_bufs = [z_bufs[0].at[..., pl.ds(0, z_bufs[0].shape[-1] // 2)], z_bufs[1].at[..., pl.ds(0, z_bufs[1].shape[-1] // 2)]] + z_bufs[2:]
    out_ref[...] = ring_scatter(lambda i: sum_x.at[i], "zh", z_bufs, send_sem.at[5:9], recv_sem.at[5:9], sent)
    for copy in sent:
        copy.wait_send()


def scatter_rows(rows, with_core=True):
    nx, nz, nc = SIZE["x"], SIZE["zh"], SIZE["core"]
    halves_in = nc if with_core else 1
    blk = rows.shape[0] // (nx * nz * halves_in)
    tail = rows.shape[1:]
    part = rows.reshape(((nc,) if with_core else ()) + (nx, nz, blk) + tail)
    links = 9
    return pl.pallas_call(
        functools.partial(scatter_kernel, with_core),
        out_shape=jax.ShapeDtypeStruct((blk,) + tail, jnp.float32),
        in_specs=[pl.BlockSpec(memory_space=pltpu.VMEM)],
        out_specs=pl.BlockSpec(memory_space=pltpu.VMEM),
        scratch_shapes=[
            pltpu.VMEM((nx, nz, blk) + tail, rows.dtype),
            pltpu.VMEM((nx, nz, blk) + tail, rows.dtype),
            pltpu.VMEM((2, 4, nz, blk) + tail, rows.dtype),
            pltpu.VMEM((nz, blk) + tail, rows.dtype),
            pltpu.VMEM((2, 4, blk) + tail, rows.dtype),
            pltpu.SemaphoreType.DMA((links,)),
            pltpu.SemaphoreType.DMA((links,)),
        ],
        compiler_params=pltpu.CompilerParams(
            collective_id=1 if with_core else 2, has_side_effects=True
        ),
    )(part)


def to_request_order(values):
    nx, nz, nc = SIZE["x"], SIZE["zh"], SIZE["core"]
    blk = TOKENS // (nx * nz * nc)
    tail = values.shape[1:]
    values = values.reshape((nc, nx, nz, blk) + tail)
    values = jnp.moveaxis(values, 0, 2)
    return values.reshape((TOKENS,) + tail)


def from_request_order(values):
    nx, nz, nc = SIZE["x"], SIZE["zh"], SIZE["core"]
    blk = TOKENS // (nx * nz * nc)
    tail = values.shape[1:]
    values = values.reshape((nx, nz, nc, blk) + tail)
    values = jnp.moveaxis(values, 2, 0)
    return values.reshape((TOKENS,) + tail)


def local(
    hidden_in,
    attn_gain,
    w_query,
    w_key,
    w_value,
    w_out,
    cache_k,
    cache_v,
    cache_len,
    ffn_gain,
    router,
    routes,
    w_gate_up,
    w_down,
):
    width = hidden_in.shape[1]
    head_dev = cache_k.shape[1]
    n_experts = w_gate_up.shape[0]
    normed = gather_rows(rms_scale(hidden_in, attn_gain))
    w_down_later, _ = lax.optimization_barrier((w_down, normed))
    w_down_sibling = lax.ppermute(w_down_later, "core", [(0, 1), (1, 0)])
    positions = (cache_len[:, None] + jnp.arange(NEW, dtype=jnp.int32)[None, :]).reshape(-1)
    positions = from_request_order(positions)

    def project(weight):
        return jnp.dot(normed, weight, preferred_element_type=jnp.float32).reshape(
            TOKENS, head_dev, HDIM
        )

    def by_request(values):
        values = to_request_order(values)
        return values.reshape(REQS, NEW, head_dev, HDIM).transpose(0, 2, 1, 3)

    query = rotate(project(w_query), positions).astype(jnp.bfloat16)
    key_new = rotate(project(w_key), positions).astype(jnp.bfloat16)
    value_new = project(w_value).astype(jnp.bfloat16)
    heads_out = attend(
        by_request(query), by_request(key_new), by_request(value_new), cache_k, cache_v, cache_len
    )
    heads_flat = from_request_order(heads_out.transpose(0, 2, 1, 3).reshape(TOKENS, head_dev * HDIM))
    heads_flat, w_down_sibling = lax.optimization_barrier((heads_flat, w_down_sibling))
    core = lax.axis_index("core")
    by_core = heads_flat.reshape(SIZE["core"], TOKENS // SIZE["core"], head_dev * HDIM)
    mine = lax.dynamic_index_in_dim(by_core, core, axis=0, keepdims=False)
    theirs = lax.dynamic_index_in_dim(by_core, 1 - core, axis=0, keepdims=False)
    swap = [(0, 1), (1, 0)]
    from_sibling = lax.ppermute(theirs, "core", swap)
    w_out_sibling = lax.ppermute(w_out, "core", swap)
    attn = scatter_rows(
        (
            jnp.dot(mine, w_out, preferred_element_type=jnp.float32)
            + jnp.dot(from_sibling, w_out_sibling, preferred_element_type=jnp.float32)
        ).astype(jnp.bfloat16),
        with_core=False,
    )
    middle = (hidden_in.astype(jnp.float32) + attn).astype(jnp.bfloat16)
    normed2 = gather_rows(rms_scale(middle, ffn_gain))
    logits = jnp.dot(normed2, router, preferred_element_type=jnp.float32)
    routes = from_request_order(routes)
    pair_weights = route_weights(logits, routes)
    half = TOKENS // SIZE["core"]
    both = jnp.einsum("td,ekdf->ektf", normed2, w_gate_up, preferred_element_type=jnp.float32)
    inner = (jax.nn.silu(both[:, 0]) * both[:, 1]).astype(jnp.bfloat16)
    inner = inner.reshape(n_experts, SIZE["core"], half, -1)
    inner_mine = lax.dynamic_index_in_dim(inner, core, axis=1, keepdims=False)
    inner_theirs = lax.dynamic_index_in_dim(inner, 1 - core, axis=1, keepdims=False)
    inner_sibling = lax.ppermute(inner_theirs, "core", swap)
    dense_weight = jnp.stack(
        [jnp.sum(jnp.where(routes == expert, pair_weights, 0.0), axis=1) for expert in range(n_experts)]
    )
    weight_mine = lax.dynamic_index_in_dim(
        dense_weight.reshape(n_experts, SIZE["core"], half), core, axis=1, keepdims=False
    )[..., None]
    scaled_mine = (inner_mine.astype(jnp.float32) * weight_mine).astype(jnp.bfloat16)
    scaled_sibling = (inner_sibling.astype(jnp.float32) * weight_mine).astype(jnp.bfloat16)
    running = jnp.einsum(
        "etf,efd->td", scaled_mine, w_down, preferred_element_type=jnp.float32
    ) + jnp.einsum("etf,efd->td", scaled_sibling, w_down_sibling, preferred_element_type=jnp.float32)
    expert_out = scatter_rows(running.astype(jnp.bfloat16), with_core=False)
    return (middle.astype(jnp.float32) + expert_out).astype(jnp.bfloat16)


def solution(mesh):
    dp = mesh.shape["dp"]
    fine = Mesh(mesh.devices.reshape((dp,) + tuple(n for _, n in SUB)), ("dp",) + TENSOR)
    rows = ("dp",) + TENSOR
    in_specs = (
        P(rows, None),
        P(),
        P(None, TENSOR),
        P(None, TENSOR),
        P(None, TENSOR),
        P(TENSOR, None),
        P("dp", TENSOR, None, None),
        P("dp", TENSOR, None, None),
        P("dp"),
        P(),
        P(),
        P("dp", None),
        P(None, None, None, TENSOR),
        P(None, TENSOR, None),
    )
    out_specs = P(rows, None)
    return jax.shard_map(local, mesh=fine, in_specs=in_specs, out_specs=out_specs, check_vma=False)
```

```python
import functools

import jax
import jax.numpy as jnp
from jax import lax
from jax.experimental import pallas as pl
from jax.experimental.pallas import tpu as pltpu
from jax.sharding import Mesh
from jax.sharding import PartitionSpec as P

HDIM = 64
REQS = 8
NEW = 96
TOKENS = 768

SUB = (("x", 4), ("zh", 4), ("core", 2))
TENSOR = tuple(name for name, _ in SUB)
SIZE = dict(SUB)

eps = 1e-05


def rms_scale(rows_in, gain):
    values = rows_in.astype(jnp.float32)
    mean_square = jnp.mean(values * values, axis=-1, keepdims=True)
    return (values * lax.rsqrt(mean_square + eps) * gain.astype(jnp.float32)).astype(jnp.bfloat16)


def rotate(values, positions):
    half_dim = values.shape[-1] // 2
    inverse = 10000.0 ** (-2.0 * jnp.arange(half_dim, dtype=jnp.float32) / values.shape[-1])
    angles = positions.astype(jnp.float32)[:, None] * inverse[None, :]
    cosine = jnp.cos(angles)[:, None, :]
    sine_part = jnp.sin(angles)[:, None, :]
    front = values[..., :half_dim]
    back = values[..., half_dim:]
    return jnp.concatenate(
        [front * cosine - back * sine_part, back * cosine + front * sine_part], axis=-1
    )


def route_weights(logits, routes):
    expert_iota = jnp.arange(logits.shape[1], dtype=jnp.int32)[None, :]
    first_logit = jnp.sum(jnp.where(routes[:, 0:1] == expert_iota, logits, 0.0), axis=1)
    second_logit = jnp.sum(jnp.where(routes[:, 1:2] == expert_iota, logits, 0.0), axis=1)
    first_weight = 1.0 / (1.0 + jnp.exp(second_logit - first_logit))
    second_weight = 1.0 / (1.0 + jnp.exp(first_logit - second_logit))
    return jnp.stack([first_weight, second_weight], axis=1)


def expert_apply(rows_in, gate_up, down_part):
    both = jnp.einsum("td,kdf->ktf", rows_in, gate_up, preferred_element_type=jnp.float32)
    inner = (jax.nn.silu(both[0]) * both[1]).astype(jnp.bfloat16)
    return jnp.dot(inner, down_part, preferred_element_type=jnp.float32)


def attend(query, key_new, value_new, cache_k, cache_v, cache_len):
    cached_scores = (
        jnp.einsum("rhqd,rhkd->rhqk", query, cache_k, preferred_element_type=jnp.float32) * 0.125
    )
    fresh_scores = (
        jnp.einsum("rhqd,rhkd->rhqk", query, key_new, preferred_element_type=jnp.float32) * 0.125
    )
    key_pos = jnp.arange(cache_k.shape[2], dtype=jnp.int32)
    cached_mask = key_pos[None, None, None, :] < cache_len[:, None, None, None]
    new_pos = jnp.arange(query.shape[2], dtype=jnp.int32)
    fresh_mask = (new_pos[:, None] >= new_pos[None, :])[None, None]
    cached_scores = jnp.where(cached_mask, cached_scores, -1e30)
    fresh_scores = jnp.where(fresh_mask, fresh_scores, -1e30)
    peak = jnp.maximum(
        jnp.max(cached_scores, axis=-1, keepdims=True),
        jnp.max(fresh_scores, axis=-1, keepdims=True),
    )
    cached_expo = jnp.exp(cached_scores - peak)
    fresh_expo = jnp.exp(fresh_scores - peak)
    denominator = jnp.sum(cached_expo, axis=-1, keepdims=True) + jnp.sum(
        fresh_expo, axis=-1, keepdims=True
    )
    mixed = jnp.einsum(
        "rhqk,rhkd->rhqd",
        cached_expo.astype(jnp.bfloat16),
        cache_v,
        preferred_element_type=jnp.float32,
    )
    mixed = mixed + jnp.einsum(
        "rhqk,rhkd->rhqd",
        fresh_expo.astype(jnp.bfloat16),
        value_new,
        preferred_element_type=jnp.float32,
    )
    return (mixed / denominator).astype(jnp.bfloat16)


def shifts(axis, step):
    n = SIZE[axis]
    return [(i, (i + step) % n) for i in range(n)]


def gather_stage(rows, axis):
    n = SIZE[axis]
    me = lax.axis_index(axis)
    blk = rows.shape[0]
    out = jnp.zeros((n * blk,) + rows.shape[1:], rows.dtype)
    out = lax.dynamic_update_slice_in_dim(out, rows, me * blk, axis=0)
    for step in range(1, n):
        got = lax.ppermute(rows, axis, shifts(axis, step))
        out = lax.dynamic_update_slice_in_dim(out, got, ((me - step) % n) * blk, axis=0)
    return out


def scatter_stage(rows, axis):
    n = SIZE[axis]
    me = lax.axis_index(axis)
    chunks = rows.reshape((n, rows.shape[0] // n) + rows.shape[1:])
    total = lax.dynamic_index_in_dim(chunks, me, axis=0, keepdims=False).astype(jnp.float32)
    for step in range(1, n):
        send = lax.dynamic_index_in_dim(chunks, (me + step) % n, axis=0, keepdims=False)
        got = lax.ppermute(send.astype(jnp.bfloat16), axis, shifts(axis, step))
        total = total + got.astype(jnp.float32)
    return total


def ring_peers(axis):
    here = {name: lax.axis_index(name) for name in ("dp",) + TENSOR}
    n = SIZE[axis]
    me = here[axis]

    def at(member):
        return tuple(member if name == axis else here[name] for name in ("dp",) + TENSOR)

    return me, n, at((me + 1) % n), at((me + n - 1) % n)


def halves(ref):
    half = ref.shape[-1] // 2
    return ref.at[..., pl.ds(0, half)], ref.at[..., pl.ds(half, half)]


def remote(src, dst, send_sem, recv_sem, peer):
    return pltpu.make_async_remote_copy(
        src_ref=src,
        dst_ref=dst,
        send_sem=send_sem,
        recv_sem=recv_sem,
        device_id=peer,
        device_id_type=pl.DeviceIdType.MESH,
    )


def ring_gather(slot, first, axis, send_sem, recv_sem, sent):
    me, n, right, left = ring_peers(axis)
    opposite = (me + 2) % n
    for k, peer in ((0, right), (1, left)):
        copy = remote(first, slot(me), send_sem.at[k], recv_sem.at[k], peer)
        copy.start()
        sent.append(copy)
    remote(first, slot((me + n - 1) % n), send_sem.at[0], recv_sem.at[0], left).wait_recv()
    copy = remote(
        halves(slot((me + n - 1) % n))[0], halves(slot((me + n - 1) % n))[0],
        send_sem.at[2], recv_sem.at[2], right,
    )
    copy.start()
    sent.append(copy)
    remote(first, slot((me + 1) % n), send_sem.at[1], recv_sem.at[1], right).wait_recv()
    copy = remote(
        halves(slot((me + 1) % n))[1], halves(slot((me + 1) % n))[1],
        send_sem.at[3], recv_sem.at[3], left,
    )
    copy.start()
    sent.append(copy)
    lo, hi = halves(slot(opposite))
    remote(lo, lo, send_sem.at[2], recv_sem.at[2], left).wait_recv()
    remote(hi, hi, send_sem.at[3], recv_sem.at[3], right).wait_recv()


def gather_kernel(with_core, own_ref, out_ref, send_sem, recv_sem, local_sem):
    x = lax.axis_index("x")
    z = lax.axis_index("zh")
    c = lax.axis_index("core")
    _, _, z_right, z_left = ring_peers("zh")
    _, _, x_right, x_left = ring_peers("x")
    _, _, sibling, _ = ring_peers("core")
    barrier = pltpu.get_barrier_semaphore()
    peers = (z_right, z_left, x_right, x_left) + ((sibling,) if with_core else ())
    for peer in peers:
        pl.semaphore_signal(barrier, 1, device_id=peer, device_id_type=pl.DeviceIdType.MESH)
    pl.semaphore_wait(barrier, len(peers))

    def view(*index):
        return out_ref.at[((c,) if with_core else ()) + index]

    local = pltpu.make_async_copy(own_ref, view(x, z), local_sem.at[0])
    local.start()
    sent = []
    ring_gather(lambda i: view(x, i), own_ref, "zh", send_sem.at[0:4], recv_sem.at[0:4], sent)
    local.wait()
    ring_gather(lambda i: view(i), view(x), "x", send_sem.at[4:8], recv_sem.at[4:8], sent)
    if with_core:
        copy = remote(out_ref.at[c], out_ref.at[c], send_sem.at[8], recv_sem.at[8], sibling)
        copy.start()
        sent.append(copy)
        remote(out_ref.at[c], out_ref.at[1 - c], send_sem.at[8], recv_sem.at[8], sibling).wait_recv()
    for copy in sent:
        copy.wait_send()


def gather_rows(rows, with_core=True):
    nx, nz, nc = SIZE["x"], SIZE["zh"], SIZE["core"]
    links = 9
    lead = (nc, nx, nz) if with_core else (nx, nz)
    out = pl.pallas_call(
        functools.partial(gather_kernel, with_core),
        out_shape=jax.ShapeDtypeStruct(lead + rows.shape, rows.dtype),
        in_specs=[pl.BlockSpec(memory_space=pltpu.VMEM)],
        out_specs=pl.BlockSpec(memory_space=pltpu.VMEM),
        scratch_shapes=[
            pltpu.SemaphoreType.DMA((links,)),
            pltpu.SemaphoreType.DMA((links,)),
            pltpu.SemaphoreType.DMA((1,)),
        ],
        compiler_params=pltpu.CompilerParams(
            collective_id=0 if with_core else 3, has_side_effects=True
        ),
    )(rows)
    return out.reshape((-1,) + rows.shape[1:])


def ring_scatter(chunk, axis, buffers, send_sem, recv_sem, sent):
    me, n, right, left = ring_peers(axis)
    got_lo, got_hi, to_right, to_left, from_left, from_right = buffers
    lo, hi = halves(chunk((me + 2) % n))
    for k, src, dst, peer in ((0, lo, got_lo, right), (1, hi, got_hi, left)):
        copy = remote(src, dst, send_sem.at[k], recv_sem.at[k], peer)
        copy.start()
        sent.append(copy)
    half = to_right.shape[-1] // 2
    remote(lo, got_lo, send_sem.at[0], recv_sem.at[0], left).wait_recv()
    ahead = chunk((me + 1) % n)
    to_right[..., :half] = (
        ahead[..., :half].astype(jnp.float32) + got_lo[...].astype(jnp.float32)
    ).astype(to_right.dtype)
    to_right[..., half:] = ahead[..., half:]
    copy = remote(to_right, from_left, send_sem.at[2], recv_sem.at[2], right)
    copy.start()
    sent.append(copy)
    remote(hi, got_hi, send_sem.at[1], recv_sem.at[1], right).wait_recv()
    behind = chunk((me + n - 1) % n)
    to_left[..., :half] = behind[..., :half]
    to_left[..., half:] = (
        behind[..., half:].astype(jnp.float32) + got_hi[...].astype(jnp.float32)
    ).astype(to_left.dtype)
    copy = remote(to_left, from_right, send_sem.at[3], recv_sem.at[3], left)
    copy.start()
    sent.append(copy)
    remote(to_right, from_left, send_sem.at[2], recv_sem.at[2], left).wait_recv()
    remote(to_left, from_right, send_sem.at[3], recv_sem.at[3], right).wait_recv()
    return (
        chunk(me)[...].astype(jnp.float32)
        + from_left[...].astype(jnp.float32)
        + from_right[...].astype(jnp.float32)
    )


def scatter_kernel(with_core, part_ref, out_ref, got_c, sum_c, x_bufs, sum_x, z_bufs, send_sem, recv_sem):
    c = lax.axis_index("core")
    _, _, z_right, z_left = ring_peers("zh")
    _, _, x_right, x_left = ring_peers("x")
    _, _, sibling, _ = ring_peers("core")
    barrier = pltpu.get_barrier_semaphore()
    peers = ((sibling,) if with_core else ()) + (x_right, x_left, z_right, z_left)
    for peer in peers:
        pl.semaphore_signal(barrier, 1, device_id=peer, device_id_type=pl.DeviceIdType.MESH)
    pl.semaphore_wait(barrier, len(peers))
    sent = []
    if with_core:
        copy = remote(part_ref.at[1 - c], got_c, send_sem.at[0], recv_sem.at[0], sibling)
        copy.start()
        sent.append(copy)
        copy.wait_recv()
        sum_c[...] = (
            part_ref[c].astype(jnp.float32) + got_c[...].astype(jnp.float32)
        ).astype(sum_c.dtype)
    else:
        sum_c = part_ref
    x_bufs = [x_bufs.at[0, 0], x_bufs.at[0, 1]] + [x_bufs.at[1, k] for k in range(4)]
    x_bufs = [x_bufs[0].at[..., pl.ds(0, x_bufs[0].shape[-1] // 2)], x_bufs[1].at[..., pl.ds(0, x_bufs[1].shape[-1] // 2)]] + x_bufs[2:]
    total = ring_scatter(lambda i: sum_c.at[i], "x", x_bufs, send_sem.at[1:5], recv_sem.at[1:5], sent)
    sum_x[...] = total.astype(sum_x.dtype)
    z_bufs = [z_bufs.at[0, 0], z_bufs.at[0, 1]] + [z_bufs.at[1, k] for k in range(4)]
    z_bufs = [z_bufs[0].at[..., pl.ds(0, z_bufs[0].shape[-1] // 2)], z_bufs[1].at[..., pl.ds(0, z_bufs[1].shape[-1] // 2)]] + z_bufs[2:]
    out_ref[...] = ring_scatter(lambda i: sum_x.at[i], "zh", z_bufs, send_sem.at[5:9], recv_sem.at[5:9], sent)
    for copy in sent:
        copy.wait_send()


def scatter_rows(rows, with_core=True):
    nx, nz, nc = SIZE["x"], SIZE["zh"], SIZE["core"]
    halves_in = nc if with_core else 1
    blk = rows.shape[0] // (nx * nz * halves_in)
    tail = rows.shape[1:]
    part = rows.reshape(((nc,) if with_core else ()) + (nx, nz, blk) + tail)
    links = 9
    return pl.pallas_call(
        functools.partial(scatter_kernel, with_core),
        out_shape=jax.ShapeDtypeStruct((blk,) + tail, jnp.float32),
        in_specs=[pl.BlockSpec(memory_space=pltpu.VMEM)],
        out_specs=pl.BlockSpec(memory_space=pltpu.VMEM),
        scratch_shapes=[
            pltpu.VMEM((nx, nz, blk) + tail, rows.dtype),
            pltpu.VMEM((nx, nz, blk) + tail, rows.dtype),
            pltpu.VMEM((2, 4, nz, blk) + tail, rows.dtype),
            pltpu.VMEM((nz, blk) + tail, rows.dtype),
            pltpu.VMEM((2, 4, blk) + tail, rows.dtype),
            pltpu.SemaphoreType.DMA((links,)),
            pltpu.SemaphoreType.DMA((links,)),
        ],
        compiler_params=pltpu.CompilerParams(
            collective_id=1 if with_core else 2, has_side_effects=True
        ),
    )(part)


def to_request_order(values):
    nx, nz, nc = SIZE["x"], SIZE["zh"], SIZE["core"]
    blk = TOKENS // (nx * nz * nc)
    tail = values.shape[1:]
    values = values.reshape((nc, nx, nz, blk) + tail)
    values = jnp.moveaxis(values, 0, 2)
    return values.reshape((TOKENS,) + tail)


def from_request_order(values):
    nx, nz, nc = SIZE["x"], SIZE["zh"], SIZE["core"]
    blk = TOKENS // (nx * nz * nc)
    tail = values.shape[1:]
    values = values.reshape((nx, nz, nc, blk) + tail)
    values = jnp.moveaxis(values, 2, 0)
    return values.reshape((TOKENS,) + tail)


def local(
    hidden_in,
    attn_gain,
    w_query,
    w_key,
    w_value,
    w_out,
    cache_k,
    cache_v,
    cache_len,
    ffn_gain,
    router,
    routes,
    w_gate_up,
    w_down,
):
    width = hidden_in.shape[1]
    head_dev = cache_k.shape[1]
    n_experts = w_gate_up.shape[0]
    core = lax.axis_index("core")
    swap = [(0, 1), (1, 0)]
    w_qkv = jnp.concatenate([w_query, w_key, w_value], axis=1)
    w_qkv_sibling = lax.ppermute(w_qkv, "core", swap)
    normed_half = gather_rows(rms_scale(hidden_in, attn_gain), with_core=False)
    w_down_later, _ = lax.optimization_barrier((w_down, normed_half))
    w_down_sibling = lax.ppermute(w_down_later, "core", swap)
    qkv_mine = jnp.dot(normed_half, w_qkv, preferred_element_type=jnp.float32)
    qkv_for_sibling = jnp.dot(normed_half, w_qkv_sibling, preferred_element_type=jnp.float32)
    qkv_other = lax.ppermute(qkv_for_sibling, "core", swap)
    qkv = jnp.where(
        core == 0,
        jnp.concatenate([qkv_mine, qkv_other], axis=0),
        jnp.concatenate([qkv_other, qkv_mine], axis=0),
    ).reshape(TOKENS, 3, head_dev, HDIM)
    positions = (cache_len[:, None] + jnp.arange(NEW, dtype=jnp.int32)[None, :]).reshape(-1)
    positions = from_request_order(positions)

    def by_request(values):
        values = to_request_order(values)
        return values.reshape(REQS, NEW, head_dev, HDIM).transpose(0, 2, 1, 3)

    query = rotate(qkv[:, 0], positions).astype(jnp.bfloat16)
    key_new = rotate(qkv[:, 1], positions).astype(jnp.bfloat16)
    value_new = qkv[:, 2].astype(jnp.bfloat16)
    heads_out = attend(
        by_request(query), by_request(key_new), by_request(value_new), cache_k, cache_v, cache_len
    )
    heads_flat = from_request_order(heads_out.transpose(0, 2, 1, 3).reshape(TOKENS, head_dev * HDIM))
    heads_flat, w_down_sibling = lax.optimization_barrier((heads_flat, w_down_sibling))
    by_core = heads_flat.reshape(SIZE["core"], TOKENS // SIZE["core"], head_dev * HDIM)
    mine = lax.dynamic_index_in_dim(by_core, core, axis=0, keepdims=False)
    theirs = lax.dynamic_index_in_dim(by_core, 1 - core, axis=0, keepdims=False)
    from_sibling = lax.ppermute(theirs, "core", swap)
    w_out_sibling = lax.ppermute(w_out, "core", swap)
    attn = scatter_rows(
        (
            jnp.dot(mine, w_out, preferred_element_type=jnp.float32)
            + jnp.dot(from_sibling, w_out_sibling, preferred_element_type=jnp.float32)
        ).astype(jnp.bfloat16),
        with_core=False,
    )
    middle = (hidden_in.astype(jnp.float32) + attn).astype(jnp.bfloat16)
    normed2 = gather_rows(rms_scale(middle, ffn_gain))
    logits = jnp.dot(normed2, router, preferred_element_type=jnp.float32)
    routes = from_request_order(routes)
    pair_weights = route_weights(logits, routes)
    half = TOKENS // SIZE["core"]
    both = jnp.einsum("td,ekdf->ektf", normed2, w_gate_up, preferred_element_type=jnp.float32)
    inner = (jax.nn.silu(both[:, 0]) * both[:, 1]).astype(jnp.bfloat16)
    inner = inner.reshape(n_experts, SIZE["core"], half, -1)
    inner_mine = lax.dynamic_index_in_dim(inner, core, axis=1, keepdims=False)
    inner_theirs = lax.dynamic_index_in_dim(inner, 1 - core, axis=1, keepdims=False)
    inner_sibling = lax.ppermute(inner_theirs, "core", swap)
    dense_weight = jnp.stack(
        [jnp.sum(jnp.where(routes == expert, pair_weights, 0.0), axis=1) for expert in range(n_experts)]
    )
    weight_mine = lax.dynamic_index_in_dim(
        dense_weight.reshape(n_experts, SIZE["core"], half), core, axis=1, keepdims=False
    )[..., None]
    scaled_mine = (inner_mine.astype(jnp.float32) * weight_mine).astype(jnp.bfloat16)
    scaled_sibling = (inner_sibling.astype(jnp.float32) * weight_mine).astype(jnp.bfloat16)
    running = jnp.einsum(
        "etf,efd->td", scaled_mine, w_down, preferred_element_type=jnp.float32
    ) + jnp.einsum("etf,efd->td", scaled_sibling, w_down_sibling, preferred_element_type=jnp.float32)
    expert_out = scatter_rows(running.astype(jnp.bfloat16), with_core=False)
    return (middle.astype(jnp.float32) + expert_out).astype(jnp.bfloat16)


def solution(mesh):
    dp = mesh.shape["dp"]
    fine = Mesh(mesh.devices.reshape((dp,) + tuple(n for _, n in SUB)), ("dp",) + TENSOR)
    rows = ("dp",) + TENSOR
    in_specs = (
        P(rows, None),
        P(),
        P(None, TENSOR),
        P(None, TENSOR),
        P(None, TENSOR),
        P(TENSOR, None),
        P("dp", TENSOR, None, None),
        P("dp", TENSOR, None, None),
        P("dp"),
        P(),
        P(),
        P("dp", None),
        P(None, None, None, TENSOR),
        P(None, TENSOR, None),
    )
    out_specs = P(rows, None)
    return jax.shard_map(local, mesh=fine, in_specs=in_specs, out_specs=out_specs, check_vma=False)
```

```python
import functools

import jax
import jax.numpy as jnp
from jax import lax
from jax.experimental import pallas as pl
from jax.experimental.pallas import tpu as pltpu
from jax.sharding import Mesh
from jax.sharding import PartitionSpec as P

HDIM = 64
REQS = 8
NEW = 96
TOKENS = 768

SUB = (("x", 4), ("zh", 4), ("core", 2))
TENSOR = tuple(name for name, _ in SUB)
SIZE = dict(SUB)

eps = 1e-05


def rms_scale(rows_in, gain):
    values = rows_in.astype(jnp.float32)
    mean_square = jnp.mean(values * values, axis=-1, keepdims=True)
    return (values * lax.rsqrt(mean_square + eps) * gain.astype(jnp.float32)).astype(jnp.bfloat16)


def rotate(values, positions):
    half_dim = values.shape[-1] // 2
    inverse = 10000.0 ** (-2.0 * jnp.arange(half_dim, dtype=jnp.float32) / values.shape[-1])
    angles = positions.astype(jnp.float32)[:, None] * inverse[None, :]
    cosine = jnp.cos(angles)[:, None, :]
    sine_part = jnp.sin(angles)[:, None, :]
    front = values[..., :half_dim]
    back = values[..., half_dim:]
    return jnp.concatenate(
        [front * cosine - back * sine_part, back * cosine + front * sine_part], axis=-1
    )


def route_weights(logits, routes):
    expert_iota = jnp.arange(logits.shape[1], dtype=jnp.int32)[None, :]
    first_logit = jnp.sum(jnp.where(routes[:, 0:1] == expert_iota, logits, 0.0), axis=1)
    second_logit = jnp.sum(jnp.where(routes[:, 1:2] == expert_iota, logits, 0.0), axis=1)
    first_weight = 1.0 / (1.0 + jnp.exp(second_logit - first_logit))
    second_weight = 1.0 / (1.0 + jnp.exp(first_logit - second_logit))
    return jnp.stack([first_weight, second_weight], axis=1)


def expert_apply(rows_in, gate_up, down_part):
    both = jnp.einsum("td,kdf->ktf", rows_in, gate_up, preferred_element_type=jnp.float32)
    inner = (jax.nn.silu(both[0]) * both[1]).astype(jnp.bfloat16)
    return jnp.dot(inner, down_part, preferred_element_type=jnp.float32)


def attend(query, key_new, value_new, cache_k, cache_v, cache_len):
    cached_scores = (
        jnp.einsum("rhqd,rhkd->rhqk", query, cache_k, preferred_element_type=jnp.float32) * 0.125
    )
    fresh_scores = (
        jnp.einsum("rhqd,rhkd->rhqk", query, key_new, preferred_element_type=jnp.float32) * 0.125
    )
    key_pos = jnp.arange(cache_k.shape[2], dtype=jnp.int32)
    cached_mask = key_pos[None, None, None, :] < cache_len[:, None, None, None]
    new_pos = jnp.arange(query.shape[2], dtype=jnp.int32)
    fresh_mask = (new_pos[:, None] >= new_pos[None, :])[None, None]
    cached_scores = jnp.where(cached_mask, cached_scores, -1e30)
    fresh_scores = jnp.where(fresh_mask, fresh_scores, -1e30)
    peak = jnp.maximum(
        jnp.max(cached_scores, axis=-1, keepdims=True),
        jnp.max(fresh_scores, axis=-1, keepdims=True),
    )
    cached_expo = jnp.exp(cached_scores - peak)
    fresh_expo = jnp.exp(fresh_scores - peak)
    denominator = jnp.sum(cached_expo, axis=-1, keepdims=True) + jnp.sum(
        fresh_expo, axis=-1, keepdims=True
    )
    mixed = jnp.einsum(
        "rhqk,rhkd->rhqd",
        cached_expo.astype(jnp.bfloat16),
        cache_v,
        preferred_element_type=jnp.float32,
    )
    mixed = mixed + jnp.einsum(
        "rhqk,rhkd->rhqd",
        fresh_expo.astype(jnp.bfloat16),
        value_new,
        preferred_element_type=jnp.float32,
    )
    return (mixed / denominator).astype(jnp.bfloat16)


def shifts(axis, step):
    n = SIZE[axis]
    return [(i, (i + step) % n) for i in range(n)]


def gather_stage(rows, axis):
    n = SIZE[axis]
    me = lax.axis_index(axis)
    blk = rows.shape[0]
    out = jnp.zeros((n * blk,) + rows.shape[1:], rows.dtype)
    out = lax.dynamic_update_slice_in_dim(out, rows, me * blk, axis=0)
    for step in range(1, n):
        got = lax.ppermute(rows, axis, shifts(axis, step))
        out = lax.dynamic_update_slice_in_dim(out, got, ((me - step) % n) * blk, axis=0)
    return out


def scatter_stage(rows, axis):
    n = SIZE[axis]
    me = lax.axis_index(axis)
    chunks = rows.reshape((n, rows.shape[0] // n) + rows.shape[1:])
    total = lax.dynamic_index_in_dim(chunks, me, axis=0, keepdims=False).astype(jnp.float32)
    for step in range(1, n):
        send = lax.dynamic_index_in_dim(chunks, (me + step) % n, axis=0, keepdims=False)
        got = lax.ppermute(send.astype(jnp.bfloat16), axis, shifts(axis, step))
        total = total + got.astype(jnp.float32)
    return total


def ring_peers(axis):
    here = {name: lax.axis_index(name) for name in ("dp",) + TENSOR}
    n = SIZE[axis]
    me = here[axis]

    def at(member):
        return tuple(member if name == axis else here[name] for name in ("dp",) + TENSOR)

    return me, n, at((me + 1) % n), at((me + n - 1) % n)


def halves(ref):
    half = ref.shape[-1] // 2
    return ref.at[..., pl.ds(0, half)], ref.at[..., pl.ds(half, half)]


def remote(src, dst, send_sem, recv_sem, peer):
    return pltpu.make_async_remote_copy(
        src_ref=src,
        dst_ref=dst,
        send_sem=send_sem,
        recv_sem=recv_sem,
        device_id=peer,
        device_id_type=pl.DeviceIdType.MESH,
    )


def ring_gather(slot, first, axis, send_sem, recv_sem, sent):
    me, n, right, left = ring_peers(axis)
    opposite = (me + 2) % n
    for k, peer in ((0, right), (1, left)):
        copy = remote(first, slot(me), send_sem.at[k], recv_sem.at[k], peer)
        copy.start()
        sent.append(copy)
    remote(first, slot((me + n - 1) % n), send_sem.at[0], recv_sem.at[0], left).wait_recv()
    copy = remote(
        halves(slot((me + n - 1) % n))[0], halves(slot((me + n - 1) % n))[0],
        send_sem.at[2], recv_sem.at[2], right,
    )
    copy.start()
    sent.append(copy)
    remote(first, slot((me + 1) % n), send_sem.at[1], recv_sem.at[1], right).wait_recv()
    copy = remote(
        halves(slot((me + 1) % n))[1], halves(slot((me + 1) % n))[1],
        send_sem.at[3], recv_sem.at[3], left,
    )
    copy.start()
    sent.append(copy)
    lo, hi = halves(slot(opposite))
    remote(lo, lo, send_sem.at[2], recv_sem.at[2], left).wait_recv()
    remote(hi, hi, send_sem.at[3], recv_sem.at[3], right).wait_recv()


def gather_kernel(with_core, own_ref, out_ref, send_sem, recv_sem, local_sem):
    x = lax.axis_index("x")
    z = lax.axis_index("zh")
    c = lax.axis_index("core")
    _, _, z_right, z_left = ring_peers("zh")
    _, _, x_right, x_left = ring_peers("x")
    _, _, sibling, _ = ring_peers("core")
    barrier = pltpu.get_barrier_semaphore()
    peers = (z_right, z_left, x_right, x_left) + ((sibling,) if with_core else ())
    for peer in peers:
        pl.semaphore_signal(barrier, 1, device_id=peer, device_id_type=pl.DeviceIdType.MESH)
    pl.semaphore_wait(barrier, len(peers))

    def view(*index):
        return out_ref.at[((c,) if with_core else ()) + index]

    local = pltpu.make_async_copy(own_ref, view(x, z), local_sem.at[0])
    local.start()
    sent = []
    ring_gather(lambda i: view(x, i), own_ref, "zh", send_sem.at[0:4], recv_sem.at[0:4], sent)
    local.wait()
    ring_gather(lambda i: view(i), view(x), "x", send_sem.at[4:8], recv_sem.at[4:8], sent)
    if with_core:
        copy = remote(out_ref.at[c], out_ref.at[c], send_sem.at[8], recv_sem.at[8], sibling)
        copy.start()
        sent.append(copy)
        remote(out_ref.at[c], out_ref.at[1 - c], send_sem.at[8], recv_sem.at[8], sibling).wait_recv()
    for copy in sent:
        copy.wait_send()


def gather_rows(rows, with_core=True):
    nx, nz, nc = SIZE["x"], SIZE["zh"], SIZE["core"]
    links = 9
    lead = (nc, nx, nz) if with_core else (nx, nz)
    out = pl.pallas_call(
        functools.partial(gather_kernel, with_core),
        out_shape=jax.ShapeDtypeStruct(lead + rows.shape, rows.dtype),
        in_specs=[pl.BlockSpec(memory_space=pltpu.VMEM)],
        out_specs=pl.BlockSpec(memory_space=pltpu.VMEM),
        scratch_shapes=[
            pltpu.SemaphoreType.DMA((links,)),
            pltpu.SemaphoreType.DMA((links,)),
            pltpu.SemaphoreType.DMA((1,)),
        ],
        compiler_params=pltpu.CompilerParams(
            collective_id=0 if with_core else 3, has_side_effects=True
        ),
    )(rows)
    return out.reshape((-1,) + rows.shape[1:])


def ring_scatter(chunk, axis, buffers, send_sem, recv_sem, sent):
    me, n, right, left = ring_peers(axis)
    got_lo, got_hi, to_right, to_left, from_left, from_right = buffers
    lo, hi = halves(chunk((me + 2) % n))
    for k, src, dst, peer in ((0, lo, got_lo, right), (1, hi, got_hi, left)):
        copy = remote(src, dst, send_sem.at[k], recv_sem.at[k], peer)
        copy.start()
        sent.append(copy)
    half = to_right.shape[-1] // 2
    remote(lo, got_lo, send_sem.at[0], recv_sem.at[0], left).wait_recv()
    ahead = chunk((me + 1) % n)
    to_right[..., :half] = (
        ahead[..., :half].astype(jnp.float32) + got_lo[...].astype(jnp.float32)
    ).astype(to_right.dtype)
    to_right[..., half:] = ahead[..., half:]
    copy = remote(to_right, from_left, send_sem.at[2], recv_sem.at[2], right)
    copy.start()
    sent.append(copy)
    remote(hi, got_hi, send_sem.at[1], recv_sem.at[1], right).wait_recv()
    behind = chunk((me + n - 1) % n)
    to_left[..., :half] = behind[..., :half]
    to_left[..., half:] = (
        behind[..., half:].astype(jnp.float32) + got_hi[...].astype(jnp.float32)
    ).astype(to_left.dtype)
    copy = remote(to_left, from_right, send_sem.at[3], recv_sem.at[3], left)
    copy.start()
    sent.append(copy)
    remote(to_right, from_left, send_sem.at[2], recv_sem.at[2], left).wait_recv()
    remote(to_left, from_right, send_sem.at[3], recv_sem.at[3], right).wait_recv()
    return (
        chunk(me)[...].astype(jnp.float32)
        + from_left[...].astype(jnp.float32)
        + from_right[...].astype(jnp.float32)
    )


def scatter_kernel(with_core, part_ref, out_ref, got_c, sum_c, x_bufs, sum_x, z_bufs, send_sem, recv_sem):
    c = lax.axis_index("core")
    _, _, z_right, z_left = ring_peers("zh")
    _, _, x_right, x_left = ring_peers("x")
    _, _, sibling, _ = ring_peers("core")
    barrier = pltpu.get_barrier_semaphore()
    peers = ((sibling,) if with_core else ()) + (x_right, x_left, z_right, z_left)
    for peer in peers:
        pl.semaphore_signal(barrier, 1, device_id=peer, device_id_type=pl.DeviceIdType.MESH)
    pl.semaphore_wait(barrier, len(peers))
    sent = []
    if with_core:
        copy = remote(part_ref.at[1 - c], got_c, send_sem.at[0], recv_sem.at[0], sibling)
        copy.start()
        sent.append(copy)
        copy.wait_recv()
        sum_c[...] = (
            part_ref[c].astype(jnp.float32) + got_c[...].astype(jnp.float32)
        ).astype(sum_c.dtype)
    else:
        sum_c = part_ref
    x_bufs = [x_bufs.at[0, 0], x_bufs.at[0, 1]] + [x_bufs.at[1, k] for k in range(4)]
    x_bufs = [x_bufs[0].at[..., pl.ds(0, x_bufs[0].shape[-1] // 2)], x_bufs[1].at[..., pl.ds(0, x_bufs[1].shape[-1] // 2)]] + x_bufs[2:]
    total = ring_scatter(lambda i: sum_c.at[i], "x", x_bufs, send_sem.at[1:5], recv_sem.at[1:5], sent)
    sum_x[...] = total.astype(sum_x.dtype)
    z_bufs = [z_bufs.at[0, 0], z_bufs.at[0, 1]] + [z_bufs.at[1, k] for k in range(4)]
    z_bufs = [z_bufs[0].at[..., pl.ds(0, z_bufs[0].shape[-1] // 2)], z_bufs[1].at[..., pl.ds(0, z_bufs[1].shape[-1] // 2)]] + z_bufs[2:]
    out_ref[...] = ring_scatter(lambda i: sum_x.at[i], "zh", z_bufs, send_sem.at[5:9], recv_sem.at[5:9], sent)
    for copy in sent:
        copy.wait_send()


def scatter_rows(rows, with_core=True):
    nx, nz, nc = SIZE["x"], SIZE["zh"], SIZE["core"]
    halves_in = nc if with_core else 1
    blk = rows.shape[0] // (nx * nz * halves_in)
    tail = rows.shape[1:]
    part = rows.reshape(((nc,) if with_core else ()) + (nx, nz, blk) + tail)
    links = 9
    return pl.pallas_call(
        functools.partial(scatter_kernel, with_core),
        out_shape=jax.ShapeDtypeStruct((blk,) + tail, jnp.float32),
        in_specs=[pl.BlockSpec(memory_space=pltpu.VMEM)],
        out_specs=pl.BlockSpec(memory_space=pltpu.VMEM),
        scratch_shapes=[
            pltpu.VMEM((nx, nz, blk) + tail, rows.dtype),
            pltpu.VMEM((nx, nz, blk) + tail, rows.dtype),
            pltpu.VMEM((2, 4, nz, blk) + tail, rows.dtype),
            pltpu.VMEM((nz, blk) + tail, rows.dtype),
            pltpu.VMEM((2, 4, blk) + tail, rows.dtype),
            pltpu.SemaphoreType.DMA((links,)),
            pltpu.SemaphoreType.DMA((links,)),
        ],
        compiler_params=pltpu.CompilerParams(
            collective_id=1 if with_core else 2, has_side_effects=True
        ),
    )(part)


def to_request_order(values):
    nx, nz, nc = SIZE["x"], SIZE["zh"], SIZE["core"]
    blk = TOKENS // (nx * nz * nc)
    tail = values.shape[1:]
    values = values.reshape((nc, nx, nz, blk) + tail)
    values = jnp.moveaxis(values, 0, 2)
    return values.reshape((TOKENS,) + tail)


def from_request_order(values):
    nx, nz, nc = SIZE["x"], SIZE["zh"], SIZE["core"]
    blk = TOKENS // (nx * nz * nc)
    tail = values.shape[1:]
    values = values.reshape((nx, nz, nc, blk) + tail)
    values = jnp.moveaxis(values, 2, 0)
    return values.reshape((TOKENS,) + tail)


def local(
    hidden_in,
    attn_gain,
    w_query,
    w_key,
    w_value,
    w_out,
    cache_k,
    cache_v,
    cache_len,
    ffn_gain,
    router,
    routes,
    w_gate_up,
    w_down,
):
    width = hidden_in.shape[1]
    head_dev = cache_k.shape[1]
    n_experts = w_gate_up.shape[0]
    core = lax.axis_index("core")
    swap = [(0, 1), (1, 0)]
    w_qkv = jnp.stack([w_query, w_key, w_value])
    w_qkv_sibling = lax.ppermute(w_qkv, "core", swap)
    normed_half = gather_rows(rms_scale(hidden_in, attn_gain), with_core=False)
    w_down_later, _ = lax.optimization_barrier((w_down, normed_half))
    w_down_sibling = lax.ppermute(w_down_later, "core", swap)
    qkv_mine = jnp.einsum("td,kdf->ktf", normed_half, w_qkv, preferred_element_type=jnp.float32)
    qkv_for_sibling = jnp.einsum(
        "td,kdf->ktf", normed_half, w_qkv_sibling, preferred_element_type=jnp.float32
    )
    qkv_other = lax.ppermute(qkv_for_sibling, "core", swap)
    qkv = jnp.where(
        core == 0,
        jnp.concatenate([qkv_mine, qkv_other], axis=1),
        jnp.concatenate([qkv_other, qkv_mine], axis=1),
    ).reshape(3, TOKENS, head_dev, HDIM)
    positions = (cache_len[:, None] + jnp.arange(NEW, dtype=jnp.int32)[None, :]).reshape(-1)
    positions = from_request_order(positions)

    def by_request(values):
        values = to_request_order(values)
        return values.reshape(REQS, NEW, head_dev, HDIM).transpose(0, 2, 1, 3)

    query = rotate(qkv[0], positions).astype(jnp.bfloat16)
    key_new = rotate(qkv[1], positions).astype(jnp.bfloat16)
    value_new = qkv[2].astype(jnp.bfloat16)
    heads_out = attend(
        by_request(query), by_request(key_new), by_request(value_new), cache_k, cache_v, cache_len
    )
    heads_flat = from_request_order(heads_out.transpose(0, 2, 1, 3).reshape(TOKENS, head_dev * HDIM))
    heads_flat, w_down_sibling = lax.optimization_barrier((heads_flat, w_down_sibling))
    by_core = heads_flat.reshape(SIZE["core"], TOKENS // SIZE["core"], head_dev * HDIM)
    mine = lax.dynamic_index_in_dim(by_core, core, axis=0, keepdims=False)
    theirs = lax.dynamic_index_in_dim(by_core, 1 - core, axis=0, keepdims=False)
    from_sibling = lax.ppermute(theirs, "core", swap)
    w_out_sibling = lax.ppermute(w_out, "core", swap)
    attn = scatter_rows(
        (
            jnp.dot(mine, w_out, preferred_element_type=jnp.float32)
            + jnp.dot(from_sibling, w_out_sibling, preferred_element_type=jnp.float32)
        ).astype(jnp.bfloat16),
        with_core=False,
    )
    middle = (hidden_in.astype(jnp.float32) + attn).astype(jnp.bfloat16)
    normed2 = gather_rows(rms_scale(middle, ffn_gain))
    logits = jnp.dot(normed2, router, preferred_element_type=jnp.float32)
    routes = from_request_order(routes)
    pair_weights = route_weights(logits, routes)
    half = TOKENS // SIZE["core"]
    both = jnp.einsum("td,ekdf->ektf", normed2, w_gate_up, preferred_element_type=jnp.float32)
    inner = (jax.nn.silu(both[:, 0]) * both[:, 1]).astype(jnp.bfloat16)
    inner = inner.reshape(n_experts, SIZE["core"], half, -1)
    inner_mine = lax.dynamic_index_in_dim(inner, core, axis=1, keepdims=False)
    inner_theirs = lax.dynamic_index_in_dim(inner, 1 - core, axis=1, keepdims=False)
    inner_sibling = lax.ppermute(inner_theirs, "core", swap)
    dense_weight = jnp.stack(
        [jnp.sum(jnp.where(routes == expert, pair_weights, 0.0), axis=1) for expert in range(n_experts)]
    )
    weight_mine = lax.dynamic_index_in_dim(
        dense_weight.reshape(n_experts, SIZE["core"], half), core, axis=1, keepdims=False
    )[..., None]
    scaled_mine = (inner_mine.astype(jnp.float32) * weight_mine).astype(jnp.bfloat16)
    scaled_sibling = (inner_sibling.astype(jnp.float32) * weight_mine).astype(jnp.bfloat16)
    running = jnp.einsum(
        "etf,efd->td", scaled_mine, w_down, preferred_element_type=jnp.float32
    ) + jnp.einsum("etf,efd->td", scaled_sibling, w_down_sibling, preferred_element_type=jnp.float32)
    expert_out = scatter_rows(running.astype(jnp.bfloat16), with_core=False)
    return (middle.astype(jnp.float32) + expert_out).astype(jnp.bfloat16)


def solution(mesh):
    dp = mesh.shape["dp"]
    fine = Mesh(mesh.devices.reshape((dp,) + tuple(n for _, n in SUB)), ("dp",) + TENSOR)
    rows = ("dp",) + TENSOR
    in_specs = (
        P(rows, None),
        P(),
        P(None, TENSOR),
        P(None, TENSOR),
        P(None, TENSOR),
        P(TENSOR, None),
        P("dp", TENSOR, None, None),
        P("dp", TENSOR, None, None),
        P("dp"),
        P(),
        P(),
        P("dp", None),
        P(None, None, None, TENSOR),
        P(None, TENSOR, None),
    )
    out_specs = P(rows, None)
    return jax.shard_map(local, mesh=fine, in_specs=in_specs, out_specs=out_specs, check_vma=False)
```

```python
import functools

import jax
import jax.numpy as jnp
from jax import lax
from jax.experimental import pallas as pl
from jax.experimental.pallas import tpu as pltpu
from jax.sharding import Mesh
from jax.sharding import PartitionSpec as P

HDIM = 64
REQS = 8
NEW = 96
TOKENS = 768

SUB = (("x", 4), ("zh", 4), ("core", 2))
TENSOR = tuple(name for name, _ in SUB)
SIZE = dict(SUB)

eps = 1e-05


def rms_scale(rows_in, gain):
    values = rows_in.astype(jnp.float32)
    mean_square = jnp.mean(values * values, axis=-1, keepdims=True)
    return (values * lax.rsqrt(mean_square + eps) * gain.astype(jnp.float32)).astype(jnp.bfloat16)


def rotate(values, positions):
    half_dim = values.shape[-1] // 2
    inverse = 10000.0 ** (-2.0 * jnp.arange(half_dim, dtype=jnp.float32) / values.shape[-1])
    angles = positions.astype(jnp.float32)[:, None] * inverse[None, :]
    cosine = jnp.cos(angles)[:, None, :]
    sine_part = jnp.sin(angles)[:, None, :]
    front = values[..., :half_dim]
    back = values[..., half_dim:]
    return jnp.concatenate(
        [front * cosine - back * sine_part, back * cosine + front * sine_part], axis=-1
    )


def route_weights(logits, routes):
    expert_iota = jnp.arange(logits.shape[1], dtype=jnp.int32)[None, :]
    first_logit = jnp.sum(jnp.where(routes[:, 0:1] == expert_iota, logits, 0.0), axis=1)
    second_logit = jnp.sum(jnp.where(routes[:, 1:2] == expert_iota, logits, 0.0), axis=1)
    first_weight = 1.0 / (1.0 + jnp.exp(second_logit - first_logit))
    second_weight = 1.0 / (1.0 + jnp.exp(first_logit - second_logit))
    return jnp.stack([first_weight, second_weight], axis=1)


def expert_apply(rows_in, gate_up, down_part):
    both = jnp.einsum("td,kdf->ktf", rows_in, gate_up, preferred_element_type=jnp.float32)
    inner = (jax.nn.silu(both[0]) * both[1]).astype(jnp.bfloat16)
    return jnp.dot(inner, down_part, preferred_element_type=jnp.float32)


def attend(query, key_new, value_new, cache_k, cache_v, cache_len):
    cached_scores = (
        jnp.einsum("rhqd,rhkd->rhqk", query, cache_k, preferred_element_type=jnp.float32) * 0.125
    )
    fresh_scores = (
        jnp.einsum("rhqd,rhkd->rhqk", query, key_new, preferred_element_type=jnp.float32) * 0.125
    )
    key_pos = jnp.arange(cache_k.shape[2], dtype=jnp.int32)
    cached_mask = key_pos[None, None, None, :] < cache_len[:, None, None, None]
    new_pos = jnp.arange(query.shape[2], dtype=jnp.int32)
    fresh_mask = (new_pos[:, None] >= new_pos[None, :])[None, None]
    cached_scores = jnp.where(cached_mask, cached_scores, -1e30)
    fresh_scores = jnp.where(fresh_mask, fresh_scores, -1e30)
    peak = jnp.maximum(
        jnp.max(cached_scores, axis=-1, keepdims=True),
        jnp.max(fresh_scores, axis=-1, keepdims=True),
    )
    cached_expo = jnp.exp(cached_scores - peak)
    fresh_expo = jnp.exp(fresh_scores - peak)
    denominator = jnp.sum(cached_expo, axis=-1, keepdims=True) + jnp.sum(
        fresh_expo, axis=-1, keepdims=True
    )
    mixed = jnp.einsum(
        "rhqk,rhkd->rhqd",
        cached_expo.astype(jnp.bfloat16),
        cache_v,
        preferred_element_type=jnp.float32,
    )
    mixed = mixed + jnp.einsum(
        "rhqk,rhkd->rhqd",
        fresh_expo.astype(jnp.bfloat16),
        value_new,
        preferred_element_type=jnp.float32,
    )
    return (mixed / denominator).astype(jnp.bfloat16)


def shifts(axis, step):
    n = SIZE[axis]
    return [(i, (i + step) % n) for i in range(n)]


def gather_stage(rows, axis):
    n = SIZE[axis]
    me = lax.axis_index(axis)
    blk = rows.shape[0]
    out = jnp.zeros((n * blk,) + rows.shape[1:], rows.dtype)
    out = lax.dynamic_update_slice_in_dim(out, rows, me * blk, axis=0)
    for step in range(1, n):
        got = lax.ppermute(rows, axis, shifts(axis, step))
        out = lax.dynamic_update_slice_in_dim(out, got, ((me - step) % n) * blk, axis=0)
    return out


def scatter_stage(rows, axis):
    n = SIZE[axis]
    me = lax.axis_index(axis)
    chunks = rows.reshape((n, rows.shape[0] // n) + rows.shape[1:])
    total = lax.dynamic_index_in_dim(chunks, me, axis=0, keepdims=False).astype(jnp.float32)
    for step in range(1, n):
        send = lax.dynamic_index_in_dim(chunks, (me + step) % n, axis=0, keepdims=False)
        got = lax.ppermute(send.astype(jnp.bfloat16), axis, shifts(axis, step))
        total = total + got.astype(jnp.float32)
    return total


def ring_peers(axis):
    here = {name: lax.axis_index(name) for name in ("dp",) + TENSOR}
    n = SIZE[axis]
    me = here[axis]

    def at(member):
        return tuple(member if name == axis else here[name] for name in ("dp",) + TENSOR)

    return me, n, at((me + 1) % n), at((me + n - 1) % n)


def halves(ref):
    half = ref.shape[-1] // 2
    return ref.at[..., pl.ds(0, half)], ref.at[..., pl.ds(half, half)]


def remote(src, dst, send_sem, recv_sem, peer):
    return pltpu.make_async_remote_copy(
        src_ref=src,
        dst_ref=dst,
        send_sem=send_sem,
        recv_sem=recv_sem,
        device_id=peer,
        device_id_type=pl.DeviceIdType.MESH,
    )


def ring_gather(slot, first, axis, send_sem, recv_sem, sent):
    me, n, right, left = ring_peers(axis)
    opposite = (me + 2) % n
    for k, peer in ((0, right), (1, left)):
        copy = remote(first, slot(me), send_sem.at[k], recv_sem.at[k], peer)
        copy.start()
        sent.append(copy)
    remote(first, slot((me + n - 1) % n), send_sem.at[0], recv_sem.at[0], left).wait_recv()
    copy = remote(
        halves(slot((me + n - 1) % n))[0], halves(slot((me + n - 1) % n))[0],
        send_sem.at[2], recv_sem.at[2], right,
    )
    copy.start()
    sent.append(copy)
    remote(first, slot((me + 1) % n), send_sem.at[1], recv_sem.at[1], right).wait_recv()
    copy = remote(
        halves(slot((me + 1) % n))[1], halves(slot((me + 1) % n))[1],
        send_sem.at[3], recv_sem.at[3], left,
    )
    copy.start()
    sent.append(copy)
    lo, hi = halves(slot(opposite))
    remote(lo, lo, send_sem.at[2], recv_sem.at[2], left).wait_recv()
    remote(hi, hi, send_sem.at[3], recv_sem.at[3], right).wait_recv()


def gather_kernel(with_core, own_ref, out_ref, send_sem, recv_sem, local_sem):
    x = lax.axis_index("x")
    z = lax.axis_index("zh")
    c = lax.axis_index("core")
    _, _, z_right, z_left = ring_peers("zh")
    _, _, x_right, x_left = ring_peers("x")
    _, _, sibling, _ = ring_peers("core")
    barrier = pltpu.get_barrier_semaphore()
    peers = (z_right, z_left, x_right, x_left) + ((sibling,) if with_core else ())
    for peer in peers:
        pl.semaphore_signal(barrier, 1, device_id=peer, device_id_type=pl.DeviceIdType.MESH)
    pl.semaphore_wait(barrier, len(peers))

    def view(*index):
        return out_ref.at[((c,) if with_core else ()) + index]

    local = pltpu.make_async_copy(own_ref, view(x, z), local_sem.at[0])
    local.start()
    sent = []
    ring_gather(lambda i: view(x, i), own_ref, "zh", send_sem.at[0:4], recv_sem.at[0:4], sent)
    local.wait()
    ring_gather(lambda i: view(i), view(x), "x", send_sem.at[4:8], recv_sem.at[4:8], sent)
    if with_core:
        copy = remote(out_ref.at[c], out_ref.at[c], send_sem.at[8], recv_sem.at[8], sibling)
        copy.start()
        sent.append(copy)
        remote(out_ref.at[c], out_ref.at[1 - c], send_sem.at[8], recv_sem.at[8], sibling).wait_recv()
    for copy in sent:
        copy.wait_send()


def gather_rows(rows, with_core=True):
    nx, nz, nc = SIZE["x"], SIZE["zh"], SIZE["core"]
    links = 9
    lead = (nc, nx, nz) if with_core else (nx, nz)
    out = pl.pallas_call(
        functools.partial(gather_kernel, with_core),
        out_shape=jax.ShapeDtypeStruct(lead + rows.shape, rows.dtype),
        in_specs=[pl.BlockSpec(memory_space=pltpu.VMEM)],
        out_specs=pl.BlockSpec(memory_space=pltpu.VMEM),
        scratch_shapes=[
            pltpu.SemaphoreType.DMA((links,)),
            pltpu.SemaphoreType.DMA((links,)),
            pltpu.SemaphoreType.DMA((1,)),
        ],
        compiler_params=pltpu.CompilerParams(
            collective_id=0 if with_core else 3, has_side_effects=True
        ),
    )(rows)
    return out.reshape((-1,) + rows.shape[1:])


def ring_scatter(chunk, axis, buffers, send_sem, recv_sem, sent):
    me, n, right, left = ring_peers(axis)
    got_lo, got_hi, to_right, to_left, from_left, from_right = buffers
    lo, hi = halves(chunk((me + 2) % n))
    for k, src, dst, peer in ((0, lo, got_lo, right), (1, hi, got_hi, left)):
        copy = remote(src, dst, send_sem.at[k], recv_sem.at[k], peer)
        copy.start()
        sent.append(copy)
    half = to_right.shape[-1] // 2
    remote(lo, got_lo, send_sem.at[0], recv_sem.at[0], left).wait_recv()
    ahead = chunk((me + 1) % n)
    to_right[..., :half] = (
        ahead[..., :half].astype(jnp.float32) + got_lo[...].astype(jnp.float32)
    ).astype(to_right.dtype)
    to_right[..., half:] = ahead[..., half:]
    copy = remote(to_right, from_left, send_sem.at[2], recv_sem.at[2], right)
    copy.start()
    sent.append(copy)
    remote(hi, got_hi, send_sem.at[1], recv_sem.at[1], right).wait_recv()
    behind = chunk((me + n - 1) % n)
    to_left[..., :half] = behind[..., :half]
    to_left[..., half:] = (
        behind[..., half:].astype(jnp.float32) + got_hi[...].astype(jnp.float32)
    ).astype(to_left.dtype)
    copy = remote(to_left, from_right, send_sem.at[3], recv_sem.at[3], left)
    copy.start()
    sent.append(copy)
    remote(to_right, from_left, send_sem.at[2], recv_sem.at[2], left).wait_recv()
    remote(to_left, from_right, send_sem.at[3], recv_sem.at[3], right).wait_recv()
    return (
        chunk(me)[...].astype(jnp.float32)
        + from_left[...].astype(jnp.float32)
        + from_right[...].astype(jnp.float32)
    )


def scatter_kernel(with_core, part_ref, out_ref, got_c, sum_c, x_bufs, sum_x, z_bufs, send_sem, recv_sem):
    c = lax.axis_index("core")
    _, _, z_right, z_left = ring_peers("zh")
    _, _, x_right, x_left = ring_peers("x")
    _, _, sibling, _ = ring_peers("core")
    barrier = pltpu.get_barrier_semaphore()
    peers = ((sibling,) if with_core else ()) + (x_right, x_left, z_right, z_left)
    for peer in peers:
        pl.semaphore_signal(barrier, 1, device_id=peer, device_id_type=pl.DeviceIdType.MESH)
    pl.semaphore_wait(barrier, len(peers))
    sent = []
    if with_core:
        copy = remote(part_ref.at[1 - c], got_c, send_sem.at[0], recv_sem.at[0], sibling)
        copy.start()
        sent.append(copy)
        copy.wait_recv()
        sum_c[...] = (
            part_ref[c].astype(jnp.float32) + got_c[...].astype(jnp.float32)
        ).astype(sum_c.dtype)
    else:
        sum_c = part_ref
    x_bufs = [x_bufs.at[0, 0], x_bufs.at[0, 1]] + [x_bufs.at[1, k] for k in range(4)]
    x_bufs = [x_bufs[0].at[..., pl.ds(0, x_bufs[0].shape[-1] // 2)], x_bufs[1].at[..., pl.ds(0, x_bufs[1].shape[-1] // 2)]] + x_bufs[2:]
    total = ring_scatter(lambda i: sum_c.at[i], "x", x_bufs, send_sem.at[1:5], recv_sem.at[1:5], sent)
    sum_x[...] = total.astype(sum_x.dtype)
    z_bufs = [z_bufs.at[0, 0], z_bufs.at[0, 1]] + [z_bufs.at[1, k] for k in range(4)]
    z_bufs = [z_bufs[0].at[..., pl.ds(0, z_bufs[0].shape[-1] // 2)], z_bufs[1].at[..., pl.ds(0, z_bufs[1].shape[-1] // 2)]] + z_bufs[2:]
    out_ref[...] = ring_scatter(lambda i: sum_x.at[i], "zh", z_bufs, send_sem.at[5:9], recv_sem.at[5:9], sent)
    for copy in sent:
        copy.wait_send()


def scatter_rows(rows, with_core=True):
    nx, nz, nc = SIZE["x"], SIZE["zh"], SIZE["core"]
    halves_in = nc if with_core else 1
    blk = rows.shape[0] // (nx * nz * halves_in)
    tail = rows.shape[1:]
    part = rows.reshape(((nc,) if with_core else ()) + (nx, nz, blk) + tail)
    links = 9
    return pl.pallas_call(
        functools.partial(scatter_kernel, with_core),
        out_shape=jax.ShapeDtypeStruct((blk,) + tail, jnp.float32),
        in_specs=[pl.BlockSpec(memory_space=pltpu.VMEM)],
        out_specs=pl.BlockSpec(memory_space=pltpu.VMEM),
        scratch_shapes=[
            pltpu.VMEM((nx, nz, blk) + tail, rows.dtype),
            pltpu.VMEM((nx, nz, blk) + tail, rows.dtype),
            pltpu.VMEM((2, 4, nz, blk) + tail, rows.dtype),
            pltpu.VMEM((nz, blk) + tail, rows.dtype),
            pltpu.VMEM((2, 4, blk) + tail, rows.dtype),
            pltpu.SemaphoreType.DMA((links,)),
            pltpu.SemaphoreType.DMA((links,)),
        ],
        compiler_params=pltpu.CompilerParams(
            collective_id=1 if with_core else 2, has_side_effects=True
        ),
    )(part)


def to_request_order(values):
    nx, nz, nc = SIZE["x"], SIZE["zh"], SIZE["core"]
    blk = TOKENS // (nx * nz * nc)
    tail = values.shape[1:]
    values = values.reshape((nc, nx, nz, blk) + tail)
    values = jnp.moveaxis(values, 0, 2)
    return values.reshape((TOKENS,) + tail)


def from_request_order(values):
    nx, nz, nc = SIZE["x"], SIZE["zh"], SIZE["core"]
    blk = TOKENS // (nx * nz * nc)
    tail = values.shape[1:]
    values = values.reshape((nx, nz, nc, blk) + tail)
    values = jnp.moveaxis(values, 2, 0)
    return values.reshape((TOKENS,) + tail)


def local(
    hidden_in,
    attn_gain,
    w_query,
    w_key,
    w_value,
    w_out,
    cache_k,
    cache_v,
    cache_len,
    ffn_gain,
    router,
    routes,
    w_gate_up,
    w_down,
):
    width = hidden_in.shape[1]
    head_dev = cache_k.shape[1]
    n_experts = w_gate_up.shape[0]
    core = lax.axis_index("core")
    swap = [(0, 1), (1, 0)]
    w_qkv = jnp.stack([w_query, w_key, w_value])
    w_qkv_sibling = lax.ppermute(w_qkv, "core", swap)
    w_gate_up_sibling = lax.ppermute(w_gate_up, "core", swap)
    normed_half = gather_rows(rms_scale(hidden_in, attn_gain), with_core=False)
    w_down_later, _ = lax.optimization_barrier((w_down, normed_half))
    w_down_sibling = lax.ppermute(w_down_later, "core", swap)
    qkv_mine = jnp.einsum("td,kdf->ktf", normed_half, w_qkv, preferred_element_type=jnp.float32)
    qkv_for_sibling = jnp.einsum(
        "td,kdf->ktf", normed_half, w_qkv_sibling, preferred_element_type=jnp.float32
    )
    qkv_other = lax.ppermute(qkv_for_sibling, "core", swap)
    qkv = jnp.where(
        core == 0,
        jnp.concatenate([qkv_mine, qkv_other], axis=1),
        jnp.concatenate([qkv_other, qkv_mine], axis=1),
    ).reshape(3, TOKENS, head_dev, HDIM)
    positions = (cache_len[:, None] + jnp.arange(NEW, dtype=jnp.int32)[None, :]).reshape(-1)
    positions = from_request_order(positions)

    def by_request(values):
        values = to_request_order(values)
        return values.reshape(REQS, NEW, head_dev, HDIM).transpose(0, 2, 1, 3)

    query = rotate(qkv[0], positions).astype(jnp.bfloat16)
    key_new = rotate(qkv[1], positions).astype(jnp.bfloat16)
    value_new = qkv[2].astype(jnp.bfloat16)
    heads_out = attend(
        by_request(query), by_request(key_new), by_request(value_new), cache_k, cache_v, cache_len
    )
    heads_flat = from_request_order(heads_out.transpose(0, 2, 1, 3).reshape(TOKENS, head_dev * HDIM))
    heads_flat, w_down_sibling = lax.optimization_barrier((heads_flat, w_down_sibling))
    by_core = heads_flat.reshape(SIZE["core"], TOKENS // SIZE["core"], head_dev * HDIM)
    mine = lax.dynamic_index_in_dim(by_core, core, axis=0, keepdims=False)
    theirs = lax.dynamic_index_in_dim(by_core, 1 - core, axis=0, keepdims=False)
    from_sibling = lax.ppermute(theirs, "core", swap)
    w_out_sibling = lax.ppermute(w_out, "core", swap)
    attn = scatter_rows(
        (
            jnp.dot(mine, w_out, preferred_element_type=jnp.float32)
            + jnp.dot(from_sibling, w_out_sibling, preferred_element_type=jnp.float32)
        ).astype(jnp.bfloat16),
        with_core=False,
    )
    middle = (hidden_in.astype(jnp.float32) + attn).astype(jnp.bfloat16)
    half = TOKENS // SIZE["core"]
    normed2 = gather_rows(rms_scale(middle, ffn_gain), with_core=False)
    logits = jnp.dot(normed2, router, preferred_element_type=jnp.float32)
    routes = lax.dynamic_index_in_dim(
        from_request_order(routes).reshape(SIZE["core"], half, -1), core, axis=0, keepdims=False
    )
    pair_weights = route_weights(logits, routes)

    def hidden_units(gate_up):
        both = jnp.einsum("td,ekdf->ektf", normed2, gate_up, preferred_element_type=jnp.float32)
        return (jax.nn.silu(both[:, 0]) * both[:, 1]).astype(jnp.bfloat16)

    inner_mine = hidden_units(w_gate_up)
    inner_sibling = hidden_units(w_gate_up_sibling)
    dense_weight = jnp.stack(
        [jnp.sum(jnp.where(routes == expert, pair_weights, 0.0), axis=1) for expert in range(n_experts)]
    )
    weight_mine = dense_weight[..., None]
    scaled_mine = (inner_mine.astype(jnp.float32) * weight_mine).astype(jnp.bfloat16)
    scaled_sibling = (inner_sibling.astype(jnp.float32) * weight_mine).astype(jnp.bfloat16)
    running = jnp.einsum(
        "etf,efd->td", scaled_mine, w_down, preferred_element_type=jnp.float32
    ) + jnp.einsum("etf,efd->td", scaled_sibling, w_down_sibling, preferred_element_type=jnp.float32)
    expert_out = scatter_rows(running.astype(jnp.bfloat16), with_core=False)
    return (middle.astype(jnp.float32) + expert_out).astype(jnp.bfloat16)


def solution(mesh):
    dp = mesh.shape["dp"]
    fine = Mesh(mesh.devices.reshape((dp,) + tuple(n for _, n in SUB)), ("dp",) + TENSOR)
    rows = ("dp",) + TENSOR
    in_specs = (
        P(rows, None),
        P(),
        P(None, TENSOR),
        P(None, TENSOR),
        P(None, TENSOR),
        P(TENSOR, None),
        P("dp", TENSOR, None, None),
        P("dp", TENSOR, None, None),
        P("dp"),
        P(),
        P(),
        P("dp", None),
        P(None, None, None, TENSOR),
        P(None, TENSOR, None),
    )
    out_specs = P(rows, None)
    return jax.shard_map(local, mesh=fine, in_specs=in_specs, out_specs=out_specs, check_vma=False)
```

```python
import functools

import jax
import jax.numpy as jnp
from jax import lax
from jax.experimental import pallas as pl
from jax.experimental.pallas import tpu as pltpu
from jax.sharding import Mesh
from jax.sharding import PartitionSpec as P

HDIM = 64
REQS = 8
NEW = 96
TOKENS = 768

SUB = (("x", 4), ("zh", 4), ("core", 2))
TENSOR = tuple(name for name, _ in SUB)
SIZE = dict(SUB)

eps = 1e-05


def rms_scale(rows_in, gain):
    values = rows_in.astype(jnp.float32)
    mean_square = jnp.mean(values * values, axis=-1, keepdims=True)
    return (values * lax.rsqrt(mean_square + eps) * gain.astype(jnp.float32)).astype(jnp.bfloat16)


def rotate(values, positions):
    half_dim = values.shape[-1] // 2
    inverse = 10000.0 ** (-2.0 * jnp.arange(half_dim, dtype=jnp.float32) / values.shape[-1])
    angles = positions.astype(jnp.float32)[:, None] * inverse[None, :]
    cosine = jnp.cos(angles)[:, None, :]
    sine_part = jnp.sin(angles)[:, None, :]
    front = values[..., :half_dim]
    back = values[..., half_dim:]
    return jnp.concatenate(
        [front * cosine - back * sine_part, back * cosine + front * sine_part], axis=-1
    )


def route_weights(logits, routes):
    expert_iota = jnp.arange(logits.shape[1], dtype=jnp.int32)[None, :]
    first_logit = jnp.sum(jnp.where(routes[:, 0:1] == expert_iota, logits, 0.0), axis=1)
    second_logit = jnp.sum(jnp.where(routes[:, 1:2] == expert_iota, logits, 0.0), axis=1)
    first_weight = 1.0 / (1.0 + jnp.exp(second_logit - first_logit))
    second_weight = 1.0 / (1.0 + jnp.exp(first_logit - second_logit))
    return jnp.stack([first_weight, second_weight], axis=1)


def expert_apply(rows_in, gate_up, down_part):
    both = jnp.einsum("td,kdf->ktf", rows_in, gate_up, preferred_element_type=jnp.float32)
    inner = (jax.nn.silu(both[0]) * both[1]).astype(jnp.bfloat16)
    return jnp.dot(inner, down_part, preferred_element_type=jnp.float32)


def attend(query, key_new, value_new, cache_k, cache_v, cache_len):
    cached_scores = (
        jnp.einsum("rhqd,rhkd->rhqk", query, cache_k, preferred_element_type=jnp.float32) * 0.125
    )
    fresh_scores = (
        jnp.einsum("rhqd,rhkd->rhqk", query, key_new, preferred_element_type=jnp.float32) * 0.125
    )
    key_pos = jnp.arange(cache_k.shape[2], dtype=jnp.int32)
    cached_mask = key_pos[None, None, None, :] < cache_len[:, None, None, None]
    new_pos = jnp.arange(query.shape[2], dtype=jnp.int32)
    fresh_mask = (new_pos[:, None] >= new_pos[None, :])[None, None]
    cached_scores = jnp.where(cached_mask, cached_scores, -1e30)
    fresh_scores = jnp.where(fresh_mask, fresh_scores, -1e30)
    peak = jnp.maximum(
        jnp.max(cached_scores, axis=-1, keepdims=True),
        jnp.max(fresh_scores, axis=-1, keepdims=True),
    )
    cached_expo = jnp.exp(cached_scores - peak)
    fresh_expo = jnp.exp(fresh_scores - peak)
    denominator = jnp.sum(cached_expo, axis=-1, keepdims=True) + jnp.sum(
        fresh_expo, axis=-1, keepdims=True
    )
    mixed = jnp.einsum(
        "rhqk,rhkd->rhqd",
        cached_expo.astype(jnp.bfloat16),
        cache_v,
        preferred_element_type=jnp.float32,
    )
    mixed = mixed + jnp.einsum(
        "rhqk,rhkd->rhqd",
        fresh_expo.astype(jnp.bfloat16),
        value_new,
        preferred_element_type=jnp.float32,
    )
    return (mixed / denominator).astype(jnp.bfloat16)


def shifts(axis, step):
    n = SIZE[axis]
    return [(i, (i + step) % n) for i in range(n)]


def gather_stage(rows, axis):
    n = SIZE[axis]
    me = lax.axis_index(axis)
    blk = rows.shape[0]
    out = jnp.zeros((n * blk,) + rows.shape[1:], rows.dtype)
    out = lax.dynamic_update_slice_in_dim(out, rows, me * blk, axis=0)
    for step in range(1, n):
        got = lax.ppermute(rows, axis, shifts(axis, step))
        out = lax.dynamic_update_slice_in_dim(out, got, ((me - step) % n) * blk, axis=0)
    return out


def scatter_stage(rows, axis):
    n = SIZE[axis]
    me = lax.axis_index(axis)
    chunks = rows.reshape((n, rows.shape[0] // n) + rows.shape[1:])
    total = lax.dynamic_index_in_dim(chunks, me, axis=0, keepdims=False).astype(jnp.float32)
    for step in range(1, n):
        send = lax.dynamic_index_in_dim(chunks, (me + step) % n, axis=0, keepdims=False)
        got = lax.ppermute(send.astype(jnp.bfloat16), axis, shifts(axis, step))
        total = total + got.astype(jnp.float32)
    return total


def ring_peers(axis):
    here = {name: lax.axis_index(name) for name in ("dp",) + TENSOR}
    n = SIZE[axis]
    me = here[axis]

    def at(member):
        return tuple(member if name == axis else here[name] for name in ("dp",) + TENSOR)

    return me, n, at((me + 1) % n), at((me + n - 1) % n)


def halves(ref):
    half = ref.shape[-1] // 2
    return ref.at[..., pl.ds(0, half)], ref.at[..., pl.ds(half, half)]


def remote(src, dst, send_sem, recv_sem, peer):
    return pltpu.make_async_remote_copy(
        src_ref=src,
        dst_ref=dst,
        send_sem=send_sem,
        recv_sem=recv_sem,
        device_id=peer,
        device_id_type=pl.DeviceIdType.MESH,
    )


def ring_gather(slot, first, axis, send_sem, recv_sem, sent):
    me, n, right, left = ring_peers(axis)
    opposite = (me + 2) % n
    for k, peer in ((0, right), (1, left)):
        copy = remote(first, slot(me), send_sem.at[k], recv_sem.at[k], peer)
        copy.start()
        sent.append(copy)
    remote(first, slot((me + n - 1) % n), send_sem.at[0], recv_sem.at[0], left).wait_recv()
    copy = remote(
        halves(slot((me + n - 1) % n))[0], halves(slot((me + n - 1) % n))[0],
        send_sem.at[2], recv_sem.at[2], right,
    )
    copy.start()
    sent.append(copy)
    remote(first, slot((me + 1) % n), send_sem.at[1], recv_sem.at[1], right).wait_recv()
    copy = remote(
        halves(slot((me + 1) % n))[1], halves(slot((me + 1) % n))[1],
        send_sem.at[3], recv_sem.at[3], left,
    )
    copy.start()
    sent.append(copy)
    lo, hi = halves(slot(opposite))
    remote(lo, lo, send_sem.at[2], recv_sem.at[2], left).wait_recv()
    remote(hi, hi, send_sem.at[3], recv_sem.at[3], right).wait_recv()


def gather_kernel(with_core, own_ref, out_ref, send_sem, recv_sem, local_sem):
    x = lax.axis_index("x")
    z = lax.axis_index("zh")
    c = lax.axis_index("core")
    _, _, z_right, z_left = ring_peers("zh")
    _, _, x_right, x_left = ring_peers("x")
    _, _, sibling, _ = ring_peers("core")
    barrier = pltpu.get_barrier_semaphore()
    peers = (z_right, z_left, x_right, x_left) + ((sibling,) if with_core else ())
    for peer in peers:
        pl.semaphore_signal(barrier, 1, device_id=peer, device_id_type=pl.DeviceIdType.MESH)
    pl.semaphore_wait(barrier, len(peers))

    def view(*index):
        return out_ref.at[((c,) if with_core else ()) + index]

    local = pltpu.make_async_copy(own_ref, view(x, z), local_sem.at[0])
    local.start()
    sent = []
    ring_gather(lambda i: view(x, i), own_ref, "zh", send_sem.at[0:4], recv_sem.at[0:4], sent)
    local.wait()
    ring_gather(lambda i: view(i), view(x), "x", send_sem.at[4:8], recv_sem.at[4:8], sent)
    if with_core:
        copy = remote(out_ref.at[c], out_ref.at[c], send_sem.at[8], recv_sem.at[8], sibling)
        copy.start()
        sent.append(copy)
        remote(out_ref.at[c], out_ref.at[1 - c], send_sem.at[8], recv_sem.at[8], sibling).wait_recv()
    for copy in sent:
        copy.wait_send()


def gather_rows(rows, with_core=True):
    nx, nz, nc = SIZE["x"], SIZE["zh"], SIZE["core"]
    links = 9
    lead = (nc, nx, nz) if with_core else (nx, nz)
    out = pl.pallas_call(
        functools.partial(gather_kernel, with_core),
        out_shape=jax.ShapeDtypeStruct(lead + rows.shape, rows.dtype),
        in_specs=[pl.BlockSpec(memory_space=pltpu.VMEM)],
        out_specs=pl.BlockSpec(memory_space=pltpu.VMEM),
        scratch_shapes=[
            pltpu.SemaphoreType.DMA((links,)),
            pltpu.SemaphoreType.DMA((links,)),
            pltpu.SemaphoreType.DMA((1,)),
        ],
        compiler_params=pltpu.CompilerParams(
            collective_id=0 if with_core else 3, has_side_effects=True
        ),
    )(rows)
    return out.reshape((-1,) + rows.shape[1:])


def ring_scatter(chunk, axis, buffers, send_sem, recv_sem, sent):
    me, n, right, left = ring_peers(axis)
    got_lo, got_hi, to_right, to_left, from_left, from_right = buffers
    lo, hi = halves(chunk((me + 2) % n))
    for k, src, dst, peer in ((0, lo, got_lo, right), (1, hi, got_hi, left)):
        copy = remote(src, dst, send_sem.at[k], recv_sem.at[k], peer)
        copy.start()
        sent.append(copy)
    half = to_right.shape[-1] // 2
    remote(lo, got_lo, send_sem.at[0], recv_sem.at[0], left).wait_recv()
    ahead = chunk((me + 1) % n)
    to_right[..., :half] = (
        ahead[..., :half].astype(jnp.float32) + got_lo[...].astype(jnp.float32)
    ).astype(to_right.dtype)
    to_right[..., half:] = ahead[..., half:]
    copy = remote(to_right, from_left, send_sem.at[2], recv_sem.at[2], right)
    copy.start()
    sent.append(copy)
    remote(hi, got_hi, send_sem.at[1], recv_sem.at[1], right).wait_recv()
    behind = chunk((me + n - 1) % n)
    to_left[..., :half] = behind[..., :half]
    to_left[..., half:] = (
        behind[..., half:].astype(jnp.float32) + got_hi[...].astype(jnp.float32)
    ).astype(to_left.dtype)
    copy = remote(to_left, from_right, send_sem.at[3], recv_sem.at[3], left)
    copy.start()
    sent.append(copy)
    remote(to_right, from_left, send_sem.at[2], recv_sem.at[2], left).wait_recv()
    remote(to_left, from_right, send_sem.at[3], recv_sem.at[3], right).wait_recv()
    return (
        chunk(me)[...].astype(jnp.float32)
        + from_left[...].astype(jnp.float32)
        + from_right[...].astype(jnp.float32)
    )


def scatter_kernel(with_core, part_ref, out_ref, got_c, sum_c, x_bufs, sum_x, z_bufs, send_sem, recv_sem):
    c = lax.axis_index("core")
    _, _, z_right, z_left = ring_peers("zh")
    _, _, x_right, x_left = ring_peers("x")
    _, _, sibling, _ = ring_peers("core")
    barrier = pltpu.get_barrier_semaphore()
    peers = ((sibling,) if with_core else ()) + (x_right, x_left, z_right, z_left)
    for peer in peers:
        pl.semaphore_signal(barrier, 1, device_id=peer, device_id_type=pl.DeviceIdType.MESH)
    pl.semaphore_wait(barrier, len(peers))
    sent = []
    if with_core:
        copy = remote(part_ref.at[1 - c], got_c, send_sem.at[0], recv_sem.at[0], sibling)
        copy.start()
        sent.append(copy)
        copy.wait_recv()
        sum_c[...] = (
            part_ref[c].astype(jnp.float32) + got_c[...].astype(jnp.float32)
        ).astype(sum_c.dtype)
    else:
        sum_c = part_ref
    x_bufs = [x_bufs.at[0, 0], x_bufs.at[0, 1]] + [x_bufs.at[1, k] for k in range(4)]
    x_bufs = [x_bufs[0].at[..., pl.ds(0, x_bufs[0].shape[-1] // 2)], x_bufs[1].at[..., pl.ds(0, x_bufs[1].shape[-1] // 2)]] + x_bufs[2:]
    total = ring_scatter(lambda i: sum_c.at[i], "x", x_bufs, send_sem.at[1:5], recv_sem.at[1:5], sent)
    sum_x[...] = total.astype(sum_x.dtype)
    z_bufs = [z_bufs.at[0, 0], z_bufs.at[0, 1]] + [z_bufs.at[1, k] for k in range(4)]
    z_bufs = [z_bufs[0].at[..., pl.ds(0, z_bufs[0].shape[-1] // 2)], z_bufs[1].at[..., pl.ds(0, z_bufs[1].shape[-1] // 2)]] + z_bufs[2:]
    out_ref[...] = ring_scatter(lambda i: sum_x.at[i], "zh", z_bufs, send_sem.at[5:9], recv_sem.at[5:9], sent)
    for copy in sent:
        copy.wait_send()


def scatter_rows(rows, with_core=True):
    nx, nz, nc = SIZE["x"], SIZE["zh"], SIZE["core"]
    halves_in = nc if with_core else 1
    blk = rows.shape[0] // (nx * nz * halves_in)
    tail = rows.shape[1:]
    part = rows.reshape(((nc,) if with_core else ()) + (nx, nz, blk) + tail)
    links = 9
    return pl.pallas_call(
        functools.partial(scatter_kernel, with_core),
        out_shape=jax.ShapeDtypeStruct((blk,) + tail, jnp.float32),
        in_specs=[pl.BlockSpec(memory_space=pltpu.VMEM)],
        out_specs=pl.BlockSpec(memory_space=pltpu.VMEM),
        scratch_shapes=[
            pltpu.VMEM((nx, nz, blk) + tail, rows.dtype),
            pltpu.VMEM((nx, nz, blk) + tail, rows.dtype),
            pltpu.VMEM((2, 4, nz, blk) + tail, rows.dtype),
            pltpu.VMEM((nz, blk) + tail, rows.dtype),
            pltpu.VMEM((2, 4, blk) + tail, rows.dtype),
            pltpu.SemaphoreType.DMA((links,)),
            pltpu.SemaphoreType.DMA((links,)),
        ],
        compiler_params=pltpu.CompilerParams(
            collective_id=1 if with_core else 2, has_side_effects=True
        ),
    )(part)


def to_request_order(values):
    nx, nz, nc = SIZE["x"], SIZE["zh"], SIZE["core"]
    blk = TOKENS // (nx * nz * nc)
    tail = values.shape[1:]
    values = values.reshape((nc, nx, nz, blk) + tail)
    values = jnp.moveaxis(values, 0, 2)
    return values.reshape((TOKENS,) + tail)


def from_request_order(values):
    nx, nz, nc = SIZE["x"], SIZE["zh"], SIZE["core"]
    blk = TOKENS // (nx * nz * nc)
    tail = values.shape[1:]
    values = values.reshape((nx, nz, nc, blk) + tail)
    values = jnp.moveaxis(values, 2, 0)
    return values.reshape((TOKENS,) + tail)


def local(
    hidden_in,
    attn_gain,
    w_query,
    w_key,
    w_value,
    w_out,
    cache_k,
    cache_v,
    cache_len,
    ffn_gain,
    router,
    routes,
    w_gate_up,
    w_down,
):
    width = hidden_in.shape[1]
    head_dev = cache_k.shape[1]
    n_experts = w_gate_up.shape[0]
    core = lax.axis_index("core")
    swap = [(0, 1), (1, 0)]
    weights = (w_query, w_key, w_value)
    weights_sibling = [lax.ppermute(weight, "core", swap) for weight in weights]
    w_gate_up_sibling = lax.ppermute(w_gate_up, "core", swap)
    normed_half = gather_rows(rms_scale(hidden_in, attn_gain), with_core=False)
    w_down_later, _ = lax.optimization_barrier((w_down, normed_half))
    w_down_sibling = lax.ppermute(w_down_later, "core", swap)
    qkv_mine = jnp.stack(
        [jnp.dot(normed_half, weight, preferred_element_type=jnp.float32) for weight in weights]
    )
    qkv_for_sibling = jnp.stack(
        [jnp.dot(normed_half, weight, preferred_element_type=jnp.float32) for weight in weights_sibling]
    )
    qkv_other = lax.ppermute(qkv_for_sibling, "core", swap)
    qkv = jnp.where(
        core == 0,
        jnp.concatenate([qkv_mine, qkv_other], axis=1),
        jnp.concatenate([qkv_other, qkv_mine], axis=1),
    ).reshape(3, TOKENS, head_dev, HDIM)
    positions = (cache_len[:, None] + jnp.arange(NEW, dtype=jnp.int32)[None, :]).reshape(-1)
    positions = from_request_order(positions)

    def by_request(values):
        values = to_request_order(values)
        return values.reshape(REQS, NEW, head_dev, HDIM).transpose(0, 2, 1, 3)

    query = rotate(qkv[0], positions).astype(jnp.bfloat16)
    key_new = rotate(qkv[1], positions).astype(jnp.bfloat16)
    value_new = qkv[2].astype(jnp.bfloat16)
    heads_out = attend(
        by_request(query), by_request(key_new), by_request(value_new), cache_k, cache_v, cache_len
    )
    heads_flat = from_request_order(heads_out.transpose(0, 2, 1, 3).reshape(TOKENS, head_dev * HDIM))
    heads_flat, w_down_sibling = lax.optimization_barrier((heads_flat, w_down_sibling))
    by_core = heads_flat.reshape(SIZE["core"], TOKENS // SIZE["core"], head_dev * HDIM)
    mine = lax.dynamic_index_in_dim(by_core, core, axis=0, keepdims=False)
    theirs = lax.dynamic_index_in_dim(by_core, 1 - core, axis=0, keepdims=False)
    from_sibling = lax.ppermute(theirs, "core", swap)
    w_out_sibling = lax.ppermute(w_out, "core", swap)
    attn = scatter_rows(
        (
            jnp.dot(mine, w_out, preferred_element_type=jnp.float32)
            + jnp.dot(from_sibling, w_out_sibling, preferred_element_type=jnp.float32)
        ).astype(jnp.bfloat16),
        with_core=False,
    )
    middle = (hidden_in.astype(jnp.float32) + attn).astype(jnp.bfloat16)
    half = TOKENS // SIZE["core"]
    normed2 = gather_rows(rms_scale(middle, ffn_gain), with_core=False)
    logits = jnp.dot(normed2, router, preferred_element_type=jnp.float32)
    routes = lax.dynamic_index_in_dim(
        from_request_order(routes).reshape(SIZE["core"], half, -1), core, axis=0, keepdims=False
    )
    pair_weights = route_weights(logits, routes)

    def hidden_units(gate_up):
        both = jnp.einsum("td,ekdf->ektf", normed2, gate_up, preferred_element_type=jnp.float32)
        return (jax.nn.silu(both[:, 0]) * both[:, 1]).astype(jnp.bfloat16)

    inner_mine = hidden_units(w_gate_up)
    inner_sibling = hidden_units(w_gate_up_sibling)
    dense_weight = jnp.stack(
        [jnp.sum(jnp.where(routes == expert, pair_weights, 0.0), axis=1) for expert in range(n_experts)]
    )
    weight_mine = dense_weight[..., None]
    scaled_mine = (inner_mine.astype(jnp.float32) * weight_mine).astype(jnp.bfloat16)
    scaled_sibling = (inner_sibling.astype(jnp.float32) * weight_mine).astype(jnp.bfloat16)
    running = jnp.einsum(
        "etf,efd->td", scaled_mine, w_down, preferred_element_type=jnp.float32
    ) + jnp.einsum("etf,efd->td", scaled_sibling, w_down_sibling, preferred_element_type=jnp.float32)
    expert_out = scatter_rows(running.astype(jnp.bfloat16), with_core=False)
    return (middle.astype(jnp.float32) + expert_out).astype(jnp.bfloat16)


def solution(mesh):
    dp = mesh.shape["dp"]
    fine = Mesh(mesh.devices.reshape((dp,) + tuple(n for _, n in SUB)), ("dp",) + TENSOR)
    rows = ("dp",) + TENSOR
    in_specs = (
        P(rows, None),
        P(),
        P(None, TENSOR),
        P(None, TENSOR),
        P(None, TENSOR),
        P(TENSOR, None),
        P("dp", TENSOR, None, None),
        P("dp", TENSOR, None, None),
        P("dp"),
        P(),
        P(),
        P("dp", None),
        P(None, None, None, TENSOR),
        P(None, TENSOR, None),
    )
    out_specs = P(rows, None)
    return jax.shard_map(local, mesh=fine, in_specs=in_specs, out_specs=out_specs, check_vma=False)
```

```python
import functools

import jax
import jax.numpy as jnp
from jax import lax
from jax.experimental import pallas as pl
from jax.experimental.pallas import tpu as pltpu
from jax.sharding import Mesh
from jax.sharding import PartitionSpec as P

HDIM = 64
REQS = 8
NEW = 96
TOKENS = 768

SUB = (("x", 4), ("zh", 4), ("core", 2))
TENSOR = tuple(name for name, _ in SUB)
SIZE = dict(SUB)

eps = 1e-05


def rms_scale(rows_in, gain):
    values = rows_in.astype(jnp.float32)
    mean_square = jnp.mean(values * values, axis=-1, keepdims=True)
    return (values * lax.rsqrt(mean_square + eps) * gain.astype(jnp.float32)).astype(jnp.bfloat16)


def rotate(values, positions):
    half_dim = values.shape[-1] // 2
    inverse = 10000.0 ** (-2.0 * jnp.arange(half_dim, dtype=jnp.float32) / values.shape[-1])
    angles = positions.astype(jnp.float32)[:, None] * inverse[None, :]
    cosine = jnp.cos(angles)[:, None, :]
    sine_part = jnp.sin(angles)[:, None, :]
    front = values[..., :half_dim]
    back = values[..., half_dim:]
    return jnp.concatenate(
        [front * cosine - back * sine_part, back * cosine + front * sine_part], axis=-1
    )


def route_weights(logits, routes):
    expert_iota = jnp.arange(logits.shape[1], dtype=jnp.int32)[None, :]
    first_logit = jnp.sum(jnp.where(routes[:, 0:1] == expert_iota, logits, 0.0), axis=1)
    second_logit = jnp.sum(jnp.where(routes[:, 1:2] == expert_iota, logits, 0.0), axis=1)
    first_weight = 1.0 / (1.0 + jnp.exp(second_logit - first_logit))
    second_weight = 1.0 / (1.0 + jnp.exp(first_logit - second_logit))
    return jnp.stack([first_weight, second_weight], axis=1)


def expert_apply(rows_in, gate_up, down_part):
    both = jnp.einsum("td,kdf->ktf", rows_in, gate_up, preferred_element_type=jnp.float32)
    inner = (jax.nn.silu(both[0]) * both[1]).astype(jnp.bfloat16)
    return jnp.dot(inner, down_part, preferred_element_type=jnp.float32)


def attend(query, key_new, value_new, cache_k, cache_v, cache_len):
    cached_scores = (
        jnp.einsum("rhqd,rhkd->rhqk", query, cache_k, preferred_element_type=jnp.float32) * 0.125
    )
    fresh_scores = (
        jnp.einsum("rhqd,rhkd->rhqk", query, key_new, preferred_element_type=jnp.float32) * 0.125
    )
    key_pos = jnp.arange(cache_k.shape[2], dtype=jnp.int32)
    cached_mask = key_pos[None, None, None, :] < cache_len[:, None, None, None]
    new_pos = jnp.arange(query.shape[2], dtype=jnp.int32)
    fresh_mask = (new_pos[:, None] >= new_pos[None, :])[None, None]
    cached_scores = jnp.where(cached_mask, cached_scores, -1e30)
    fresh_scores = jnp.where(fresh_mask, fresh_scores, -1e30)
    peak = jnp.maximum(
        jnp.max(cached_scores, axis=-1, keepdims=True),
        jnp.max(fresh_scores, axis=-1, keepdims=True),
    )
    cached_expo = jnp.exp(cached_scores - peak)
    fresh_expo = jnp.exp(fresh_scores - peak)
    denominator = jnp.sum(cached_expo, axis=-1, keepdims=True) + jnp.sum(
        fresh_expo, axis=-1, keepdims=True
    )
    mixed = jnp.einsum(
        "rhqk,rhkd->rhqd",
        cached_expo.astype(jnp.bfloat16),
        cache_v,
        preferred_element_type=jnp.float32,
    )
    mixed = mixed + jnp.einsum(
        "rhqk,rhkd->rhqd",
        fresh_expo.astype(jnp.bfloat16),
        value_new,
        preferred_element_type=jnp.float32,
    )
    return (mixed / denominator).astype(jnp.bfloat16)


def shifts(axis, step):
    n = SIZE[axis]
    return [(i, (i + step) % n) for i in range(n)]


def gather_stage(rows, axis):
    n = SIZE[axis]
    me = lax.axis_index(axis)
    blk = rows.shape[0]
    out = jnp.zeros((n * blk,) + rows.shape[1:], rows.dtype)
    out = lax.dynamic_update_slice_in_dim(out, rows, me * blk, axis=0)
    for step in range(1, n):
        got = lax.ppermute(rows, axis, shifts(axis, step))
        out = lax.dynamic_update_slice_in_dim(out, got, ((me - step) % n) * blk, axis=0)
    return out


def scatter_stage(rows, axis):
    n = SIZE[axis]
    me = lax.axis_index(axis)
    chunks = rows.reshape((n, rows.shape[0] // n) + rows.shape[1:])
    total = lax.dynamic_index_in_dim(chunks, me, axis=0, keepdims=False).astype(jnp.float32)
    for step in range(1, n):
        send = lax.dynamic_index_in_dim(chunks, (me + step) % n, axis=0, keepdims=False)
        got = lax.ppermute(send.astype(jnp.bfloat16), axis, shifts(axis, step))
        total = total + got.astype(jnp.float32)
    return total


def ring_peers(axis):
    here = {name: lax.axis_index(name) for name in ("dp",) + TENSOR}
    n = SIZE[axis]
    me = here[axis]

    def at(member):
        return tuple(member if name == axis else here[name] for name in ("dp",) + TENSOR)

    return me, n, at((me + 1) % n), at((me + n - 1) % n)


def halves(ref):
    half = ref.shape[-1] // 2
    return ref.at[..., pl.ds(0, half)], ref.at[..., pl.ds(half, half)]


def remote(src, dst, send_sem, recv_sem, peer):
    return pltpu.make_async_remote_copy(
        src_ref=src,
        dst_ref=dst,
        send_sem=send_sem,
        recv_sem=recv_sem,
        device_id=peer,
        device_id_type=pl.DeviceIdType.MESH,
    )


def ring_gather(slot, first, axis, send_sem, recv_sem, sent):
    me, n, right, left = ring_peers(axis)
    opposite = (me + 2) % n
    for k, peer in ((0, right), (1, left)):
        copy = remote(first, slot(me), send_sem.at[k], recv_sem.at[k], peer)
        copy.start()
        sent.append(copy)
    remote(first, slot((me + n - 1) % n), send_sem.at[0], recv_sem.at[0], left).wait_recv()
    copy = remote(
        halves(slot((me + n - 1) % n))[0], halves(slot((me + n - 1) % n))[0],
        send_sem.at[2], recv_sem.at[2], right,
    )
    copy.start()
    sent.append(copy)
    remote(first, slot((me + 1) % n), send_sem.at[1], recv_sem.at[1], right).wait_recv()
    copy = remote(
        halves(slot((me + 1) % n))[1], halves(slot((me + 1) % n))[1],
        send_sem.at[3], recv_sem.at[3], left,
    )
    copy.start()
    sent.append(copy)
    lo, hi = halves(slot(opposite))
    remote(lo, lo, send_sem.at[2], recv_sem.at[2], left).wait_recv()
    remote(hi, hi, send_sem.at[3], recv_sem.at[3], right).wait_recv()


def gather_kernel(with_core, own_ref, out_ref, send_sem, recv_sem, local_sem):
    x = lax.axis_index("x")
    z = lax.axis_index("zh")
    c = lax.axis_index("core")
    _, _, z_right, z_left = ring_peers("zh")
    _, _, x_right, x_left = ring_peers("x")
    _, _, sibling, _ = ring_peers("core")
    barrier = pltpu.get_barrier_semaphore()
    peers = (z_right, z_left, x_right, x_left) + ((sibling,) if with_core else ())
    for peer in peers:
        pl.semaphore_signal(barrier, 1, device_id=peer, device_id_type=pl.DeviceIdType.MESH)
    pl.semaphore_wait(barrier, len(peers))

    def view(*index):
        return out_ref.at[((c,) if with_core else ()) + index]

    local = pltpu.make_async_copy(own_ref, view(x, z), local_sem.at[0])
    local.start()
    sent = []
    ring_gather(lambda i: view(x, i), own_ref, "zh", send_sem.at[0:4], recv_sem.at[0:4], sent)
    local.wait()
    ring_gather(lambda i: view(i), view(x), "x", send_sem.at[4:8], recv_sem.at[4:8], sent)
    if with_core:
        copy = remote(out_ref.at[c], out_ref.at[c], send_sem.at[8], recv_sem.at[8], sibling)
        copy.start()
        sent.append(copy)
        remote(out_ref.at[c], out_ref.at[1 - c], send_sem.at[8], recv_sem.at[8], sibling).wait_recv()
    for copy in sent:
        copy.wait_send()


def gather_rows(rows, with_core=True):
    nx, nz, nc = SIZE["x"], SIZE["zh"], SIZE["core"]
    links = 9
    lead = (nc, nx, nz) if with_core else (nx, nz)
    out = pl.pallas_call(
        functools.partial(gather_kernel, with_core),
        out_shape=jax.ShapeDtypeStruct(lead + rows.shape, rows.dtype),
        in_specs=[pl.BlockSpec(memory_space=pltpu.VMEM)],
        out_specs=pl.BlockSpec(memory_space=pltpu.VMEM),
        scratch_shapes=[
            pltpu.SemaphoreType.DMA((links,)),
            pltpu.SemaphoreType.DMA((links,)),
            pltpu.SemaphoreType.DMA((1,)),
        ],
        compiler_params=pltpu.CompilerParams(
            collective_id=0 if with_core else 3, has_side_effects=True
        ),
    )(rows)
    return out.reshape((-1,) + rows.shape[1:])


def ring_scatter(chunk, axis, buffers, send_sem, recv_sem, sent):
    me, n, right, left = ring_peers(axis)
    got_lo, got_hi, to_right, to_left, from_left, from_right = buffers
    lo, hi = halves(chunk((me + 2) % n))
    for k, src, dst, peer in ((0, lo, got_lo, right), (1, hi, got_hi, left)):
        copy = remote(src, dst, send_sem.at[k], recv_sem.at[k], peer)
        copy.start()
        sent.append(copy)
    half = to_right.shape[-1] // 2
    remote(lo, got_lo, send_sem.at[0], recv_sem.at[0], left).wait_recv()
    ahead = chunk((me + 1) % n)
    to_right[..., :half] = (
        ahead[..., :half].astype(jnp.float32) + got_lo[...].astype(jnp.float32)
    ).astype(to_right.dtype)
    to_right[..., half:] = ahead[..., half:]
    copy = remote(to_right, from_left, send_sem.at[2], recv_sem.at[2], right)
    copy.start()
    sent.append(copy)
    remote(hi, got_hi, send_sem.at[1], recv_sem.at[1], right).wait_recv()
    behind = chunk((me + n - 1) % n)
    to_left[..., :half] = behind[..., :half]
    to_left[..., half:] = (
        behind[..., half:].astype(jnp.float32) + got_hi[...].astype(jnp.float32)
    ).astype(to_left.dtype)
    copy = remote(to_left, from_right, send_sem.at[3], recv_sem.at[3], left)
    copy.start()
    sent.append(copy)
    remote(to_right, from_left, send_sem.at[2], recv_sem.at[2], left).wait_recv()
    remote(to_left, from_right, send_sem.at[3], recv_sem.at[3], right).wait_recv()
    return (
        chunk(me)[...].astype(jnp.float32)
        + from_left[...].astype(jnp.float32)
        + from_right[...].astype(jnp.float32)
    )


def scatter_kernel(with_core, part_ref, out_ref, got_c, sum_c, x_bufs, sum_x, z_bufs, send_sem, recv_sem):
    c = lax.axis_index("core")
    _, _, z_right, z_left = ring_peers("zh")
    _, _, x_right, x_left = ring_peers("x")
    _, _, sibling, _ = ring_peers("core")
    barrier = pltpu.get_barrier_semaphore()
    peers = ((sibling,) if with_core else ()) + (x_right, x_left, z_right, z_left)
    for peer in peers:
        pl.semaphore_signal(barrier, 1, device_id=peer, device_id_type=pl.DeviceIdType.MESH)
    pl.semaphore_wait(barrier, len(peers))
    sent = []
    if with_core:
        copy = remote(part_ref.at[1 - c], got_c, send_sem.at[0], recv_sem.at[0], sibling)
        copy.start()
        sent.append(copy)
        copy.wait_recv()
        sum_c[...] = (
            part_ref[c].astype(jnp.float32) + got_c[...].astype(jnp.float32)
        ).astype(sum_c.dtype)
    else:
        sum_c = part_ref
    x_bufs = [x_bufs.at[0, 0], x_bufs.at[0, 1]] + [x_bufs.at[1, k] for k in range(4)]
    x_bufs = [x_bufs[0].at[..., pl.ds(0, x_bufs[0].shape[-1] // 2)], x_bufs[1].at[..., pl.ds(0, x_bufs[1].shape[-1] // 2)]] + x_bufs[2:]
    total = ring_scatter(lambda i: sum_c.at[i], "x", x_bufs, send_sem.at[1:5], recv_sem.at[1:5], sent)
    sum_x[...] = total.astype(sum_x.dtype)
    z_bufs = [z_bufs.at[0, 0], z_bufs.at[0, 1]] + [z_bufs.at[1, k] for k in range(4)]
    z_bufs = [z_bufs[0].at[..., pl.ds(0, z_bufs[0].shape[-1] // 2)], z_bufs[1].at[..., pl.ds(0, z_bufs[1].shape[-1] // 2)]] + z_bufs[2:]
    out_ref[...] = ring_scatter(lambda i: sum_x.at[i], "zh", z_bufs, send_sem.at[5:9], recv_sem.at[5:9], sent)
    for copy in sent:
        copy.wait_send()


def scatter_rows(rows, with_core=True):
    nx, nz, nc = SIZE["x"], SIZE["zh"], SIZE["core"]
    halves_in = nc if with_core else 1
    blk = rows.shape[0] // (nx * nz * halves_in)
    tail = rows.shape[1:]
    part = rows.reshape(((nc,) if with_core else ()) + (nx, nz, blk) + tail)
    links = 9
    return pl.pallas_call(
        functools.partial(scatter_kernel, with_core),
        out_shape=jax.ShapeDtypeStruct((blk,) + tail, jnp.float32),
        in_specs=[pl.BlockSpec(memory_space=pltpu.VMEM)],
        out_specs=pl.BlockSpec(memory_space=pltpu.VMEM),
        scratch_shapes=[
            pltpu.VMEM((nx, nz, blk) + tail, rows.dtype),
            pltpu.VMEM((nx, nz, blk) + tail, rows.dtype),
            pltpu.VMEM((2, 4, nz, blk) + tail, rows.dtype),
            pltpu.VMEM((nz, blk) + tail, rows.dtype),
            pltpu.VMEM((2, 4, blk) + tail, rows.dtype),
            pltpu.SemaphoreType.DMA((links,)),
            pltpu.SemaphoreType.DMA((links,)),
        ],
        compiler_params=pltpu.CompilerParams(
            collective_id=1 if with_core else 2, has_side_effects=True
        ),
    )(part)


def to_request_order(values):
    nx, nz, nc = SIZE["x"], SIZE["zh"], SIZE["core"]
    blk = TOKENS // (nx * nz * nc)
    tail = values.shape[1:]
    values = values.reshape((nc, nx, nz, blk) + tail)
    values = jnp.moveaxis(values, 0, 2)
    return values.reshape((TOKENS,) + tail)


def from_request_order(values):
    nx, nz, nc = SIZE["x"], SIZE["zh"], SIZE["core"]
    blk = TOKENS // (nx * nz * nc)
    tail = values.shape[1:]
    values = values.reshape((nx, nz, nc, blk) + tail)
    values = jnp.moveaxis(values, 2, 0)
    return values.reshape((TOKENS,) + tail)


def local(
    hidden_in,
    attn_gain,
    w_query,
    w_key,
    w_value,
    w_out,
    cache_k,
    cache_v,
    cache_len,
    ffn_gain,
    router,
    routes,
    w_gate_up,
    w_down,
):
    width = hidden_in.shape[1]
    head_dev = cache_k.shape[1]
    n_experts = w_gate_up.shape[0]
    core = lax.axis_index("core")
    swap = [(0, 1), (1, 0)]
    w_qkv = jnp.stack([w_query, w_key, w_value])
    w_qkv_sibling = lax.ppermute(w_qkv, "core", swap)
    w_gate_up_sibling = lax.ppermute(w_gate_up, "core", swap)
    normed_half = gather_rows(rms_scale(hidden_in, attn_gain), with_core=False)
    w_down_later, _ = lax.optimization_barrier((w_down, normed_half))
    w_down_sibling = lax.ppermute(w_down_later, "core", swap)
    qkv_mine = jnp.einsum("td,kdf->ktf", normed_half, w_qkv, preferred_element_type=jnp.float32)
    qkv_for_sibling = jnp.einsum(
        "td,kdf->ktf", normed_half, w_qkv_sibling, preferred_element_type=jnp.float32
    )
    qkv_other = lax.ppermute(qkv_for_sibling, "core", swap)
    qkv = jnp.where(
        core == 0,
        jnp.concatenate([qkv_mine, qkv_other], axis=1),
        jnp.concatenate([qkv_other, qkv_mine], axis=1),
    ).reshape(3, TOKENS, head_dev, HDIM)
    positions = (cache_len[:, None] + jnp.arange(NEW, dtype=jnp.int32)[None, :]).reshape(-1)
    positions = from_request_order(positions)

    def by_request(values):
        values = to_request_order(values)
        return values.reshape(REQS, NEW, head_dev, HDIM).transpose(0, 2, 1, 3)

    query = rotate(qkv[0], positions).astype(jnp.bfloat16)
    key_new = rotate(qkv[1], positions).astype(jnp.bfloat16)
    value_new = qkv[2].astype(jnp.bfloat16)
    heads_out = attend(
        by_request(query), by_request(key_new), by_request(value_new), cache_k, cache_v, cache_len
    )
    heads_flat = from_request_order(heads_out.transpose(0, 2, 1, 3).reshape(TOKENS, head_dev * HDIM))
    heads_flat, w_down_sibling, w_gate_up_sibling = lax.optimization_barrier(
        (heads_flat, w_down_sibling, w_gate_up_sibling)
    )
    by_core = heads_flat.reshape(SIZE["core"], TOKENS // SIZE["core"], head_dev * HDIM)
    mine = lax.dynamic_index_in_dim(by_core, core, axis=0, keepdims=False)
    theirs = lax.dynamic_index_in_dim(by_core, 1 - core, axis=0, keepdims=False)
    from_sibling = lax.ppermute(theirs, "core", swap)
    w_out_sibling = lax.ppermute(w_out, "core", swap)
    attn = scatter_rows(
        (
            jnp.dot(mine, w_out, preferred_element_type=jnp.float32)
            + jnp.dot(from_sibling, w_out_sibling, preferred_element_type=jnp.float32)
        ).astype(jnp.bfloat16),
        with_core=False,
    )
    middle = (hidden_in.astype(jnp.float32) + attn).astype(jnp.bfloat16)
    half = TOKENS // SIZE["core"]
    normed2 = gather_rows(rms_scale(middle, ffn_gain), with_core=False)
    logits = jnp.dot(normed2, router, preferred_element_type=jnp.float32)
    routes = lax.dynamic_index_in_dim(
        from_request_order(routes).reshape(SIZE["core"], half, -1), core, axis=0, keepdims=False
    )
    pair_weights = route_weights(logits, routes)

    def hidden_units(gate_up):
        both = jnp.einsum("td,ekdf->ektf", normed2, gate_up, preferred_element_type=jnp.float32)
        return (jax.nn.silu(both[:, 0]) * both[:, 1]).astype(jnp.bfloat16)

    inner_mine = hidden_units(w_gate_up)
    inner_sibling = hidden_units(w_gate_up_sibling)
    dense_weight = jnp.stack(
        [jnp.sum(jnp.where(routes == expert, pair_weights, 0.0), axis=1) for expert in range(n_experts)]
    )
    weight_mine = dense_weight[..., None]
    scaled_mine = (inner_mine.astype(jnp.float32) * weight_mine).astype(jnp.bfloat16)
    scaled_sibling = (inner_sibling.astype(jnp.float32) * weight_mine).astype(jnp.bfloat16)
    running = jnp.einsum(
        "etf,efd->td", scaled_mine, w_down, preferred_element_type=jnp.float32
    ) + jnp.einsum("etf,efd->td", scaled_sibling, w_down_sibling, preferred_element_type=jnp.float32)
    expert_out = scatter_rows(running.astype(jnp.bfloat16), with_core=False)
    return (middle.astype(jnp.float32) + expert_out).astype(jnp.bfloat16)


def solution(mesh):
    dp = mesh.shape["dp"]
    fine = Mesh(mesh.devices.reshape((dp,) + tuple(n for _, n in SUB)), ("dp",) + TENSOR)
    rows = ("dp",) + TENSOR
    in_specs = (
        P(rows, None),
        P(),
        P(None, TENSOR),
        P(None, TENSOR),
        P(None, TENSOR),
        P(TENSOR, None),
        P("dp", TENSOR, None, None),
        P("dp", TENSOR, None, None),
        P("dp"),
        P(),
        P(),
        P("dp", None),
        P(None, None, None, TENSOR),
        P(None, TENSOR, None),
    )
    out_specs = P(rows, None)
    return jax.shard_map(local, mesh=fine, in_specs=in_specs, out_specs=out_specs, check_vma=False)
```
